32 devices in a mesh: parts: 2 (over y), space: 4 (over z), tm: 2 (over x), chan: 2 (over core).
Axes of the slice: x: 2, y: 2, z: 4, core: 2. Of those that a mesh axis runs over, the one named last changes fastest.
Arguments:
- events: int32 [16, 128, 128], P(('parts', 'tm'), 'space'), parts along dimension 0, may hold values 0 or 1
- soft_info: bfloat16 [16, 128, 128], P(('parts', 'tm'), 'space'), parts along dimension 0, may hold values from -6 to 6
- embed: float32 [4, 64], replicated, may hold values from -6 to 6
- soft_gain: float32 [64], replicated, may hold values from -6 to 6
- conv_weights: bfloat16 [3, 64, 1728], replicated, may hold values from -0.21875 to 0.21875
- conv_bias: float32 [3, 64], replicated, may hold values from -1.75 to 1.75
- readout_weight: float32 [64], replicated, may hold values from -0.75 to 0.75
Outputs:
- logits: float32 [16, 128, 128], P(('parts', 'tm'), 'space'), parts along dimension 0
The draws below stay inside these ranges and needn't reach their ends.
There are 2 independent parts, one for each index of `parts`. The reference program is written for one: setup_inputs(seed, part) draws one part's arguments, and reference() takes and returns one part's arrays. A program takes and returns all parts, laid end to end along the dimension named above; an argument that names none is the same for every part. Nothing has to cross between parts.
All inputs are finite; a program needn't handle non-finite values. No bound on the sum of `events` on one device may be relied on, other than what follows from the above.
Results may differ from the reference program's by a relative error of at most 0.024.
Values may be sent and summed in bfloat16 or wider, within the bound.
No kernel may reach another device: no remote copies, remote signals or barrier semaphores. Data moves between devices by JAX's collectives and lax.ppermute only.
A program may use at most 64 MiB of HBM per device.

```python
import jax
import jax.numpy as jnp
from jax import lax

CH = 64
GRID = 128
WIN = 2
LAYERS = 3
ROUNDS = 8
N_TM = 2


def place_ends(entries, key, least, top_value):
    shape = entries.shape
    place = [jax.random.randint(jax.random.fold_in(key, axis), (), 0, shape[axis]) for axis in range(len(shape))]
    entries = entries.at[tuple(place)].set(least)
    longest = shape.index(max(shape))
    place[longest] = (place[longest] + 1) % shape[longest]
    return entries.at[tuple(place)].set(top_value)


def block_scale(key, extent, pieces, least, top_value):
    def one(dim, parts):
        heights = jax.random.uniform(jax.random.fold_in(jax.random.fold_in(key, 6), dim), (parts,), jnp.float32, least / len(pieces), top_value / len(pieces))
        return jnp.repeat(jnp.exp(heights), extent[dim] // parts).reshape((-1,) + (1,) * (len(extent) - dim - 1))

    level = one(*pieces[0])
    for cut in pieces[1:]:
        level = level * one(*cut)
    return level


def normal_values(own_key, dims, deviation, most, split=(), kind=jnp.bfloat16):
    result = jax.random.normal(own_key, dims, jnp.float32) * deviation
    if len(split) > 0:
        result = block_scale(own_key, dims, split, -0.22, 0.18) * result
    return jnp.clip(result, min=-most, max=most).astype(kind)


def setup_inputs(seed: int = 0, part: int = 0) -> dict:
    keys = jax.random.split(jax.random.key(seed), 8)
    own_keys = jax.random.split(jax.random.fold_in(keys[7], part), 8)
    events = place_ends((jax.random.randint(own_keys[0], (ROUNDS, GRID, GRID), 0, 4) < 1).astype(jnp.int32), jax.random.fold_in(own_keys[0], 1), 0, 1)
    soft_info = normal_values(own_keys[1], (ROUNDS, GRID, GRID), 1.0, 6.0, ((0, 2), (1, 4)))
    embed = normal_values(keys[2], (4, CH), 1.0, 6.0, (), jnp.float32)
    soft_gain = normal_values(keys[3], (CH,), 1.0, 6.0, (), jnp.float32)
    conv_weights = normal_values(keys[4], (LAYERS, CH, CH * 27), (CH * 27 // 2) ** -0.5, 0.21875)
    conv_bias = normal_values(keys[5], (LAYERS, CH), 0.3, 1.75, (), jnp.float32)
    readout_weight = normal_values(keys[6], (CH,), CH ** -0.5, 0.75, (), jnp.float32)
    return {"events": events, "soft_info": soft_info, "embed": embed, "soft_gain": soft_gain, "conv_weights": conv_weights, "conv_bias": conv_bias, "readout_weight": readout_weight}


def conv_layer(inputs, kernel, bias_row):
    output = lax.conv_general_dilated(inputs, kernel, (1, 1, 1), ((0, 0), (1, 1), (1, 1)), dimension_numbers=("NCDHW", "OIDHW", "NCDHW"), preferred_element_type=jnp.float32)
    return jnp.maximum(output + bias_row[None, :, None, None, None], 0.0).astype(jnp.bfloat16)


def run_window(hidden, front, back, kernels, conv_bias):
    for layer in range(LAYERS):
        hidden = conv_layer(jnp.concatenate([front, hidden, back], 2), kernels[layer], conv_bias[layer])
    return hidden


def reference(events, soft_info, embed, soft_gain, conv_weights, conv_bias, readout_weight):
    positions = jnp.arange(GRID, dtype=jnp.int32)
    parity = (positions[:, None] + positions[None, :]) % 2
    code = 2 * parity[None] + events
    onehot = (code[None] == jnp.arange(4, dtype=jnp.int32)[:, None, None, None]).astype(jnp.float32)
    start = jnp.einsum('kc,kryx->cryx', embed, onehot) + soft_gain[:, None, None, None] * soft_info.astype(jnp.float32)[None]
    start = start.astype(jnp.bfloat16)
    windows = start.reshape(CH, N_TM, 2, WIN, GRID, GRID)
    first = jnp.transpose(windows[:, :, 0], (1, 0, 2, 3, 4))
    second = jnp.transpose(windows[:, :, 1], (1, 0, 2, 3, 4))
    kernels = conv_weights.reshape(LAYERS, CH, CH, 3, 3, 3)
    zeros = jnp.zeros((N_TM, CH, 1, GRID, GRID), jnp.bfloat16)
    first = run_window(first, zeros, zeros, kernels, conv_bias)
    after = jnp.concatenate([first[1:, :, :1], zeros[:1]], 0)
    second = run_window(second, first[:, :, -1:], after, kernels, conv_bias)
    stacked = jnp.stack([first, second], 1)
    logits = jnp.einsum('c,nscwyx->nswyx', readout_weight, stacked.astype(jnp.float32))
    return logits.reshape(ROUNDS, GRID, GRID)
```

```python
import functools

import jax
import jax.numpy as jnp
from jax import lax
from jax.experimental import pallas as pl
from jax.experimental.pallas import tpu as pltpu
from jax.sharding import PartitionSpec as P

HALO = 8
SUB = 16
EDGE = 4
CHUNK = 8
BF = jnp.bfloat16
F32 = jnp.float32


def prep_kernel(layers, ch, w_ref, embed_ref, gain_ref, bias_ref, read_ref, wout_ref, ws_ref, bout_ref, rw_ref, wt_ref):
    lanes = 4 * ch
    taps = 27
    zero_half = jnp.zeros((ch, ch), F32)
    zero_block = jnp.zeros((2 * ch, 2 * ch), BF)
    for layer in range(layers):
        wt_ref[...] = w_ref[layer].astype(F32).T
        for dx in range(3):
            sets = []
            for dr in range(3):
                g = [wt_ref[pl.ds(dr * 9 + dy * 3 + dx, ch, stride=taps), :] for dy in range(3)]
                outer = (g[0] + g[2]) * 0.5
                inner = g[1] * 0.5
                sets.append((g[0], outer + inner, outer - inner, g[2]))
            for i in range(4):
                own = jnp.concatenate(
                    [
                        jnp.concatenate([sets[1][i], sets[0][i]], 1),
                        jnp.concatenate([sets[2][i], sets[1][i]], 1),
                    ],
                    0,
                ).astype(BF)
                side = jnp.concatenate(
                    [
                        jnp.concatenate([zero_half, sets[2][i]], 1),
                        jnp.concatenate([sets[0][i], zero_half], 1),
                    ],
                    0,
                ).astype(BF)
                for b in range(2):
                    a = dx + b
                    wout_ref[layer, i, pl.ds(a * 2 * ch, 2 * ch), pl.ds(b * 2 * ch, 2 * ch)] = own
                    wout_ref[layer, i, pl.ds(lanes * 2 + a * 2 * ch, 2 * ch), pl.ds(b * 2 * ch, 2 * ch)] = side
        for i in range(4):
            for base in (0, lanes * 2):
                wout_ref[layer, i, pl.ds(base + 6 * ch, 2 * ch), pl.ds(0, 2 * ch)] = zero_block
                wout_ref[layer, i, pl.ds(base, 2 * ch), pl.ds(2 * ch, 2 * ch)] = zero_block
        bout_ref[pl.ds(layer, 1), :] = jnp.concatenate([bias_ref[pl.ds(layer, 1), :]] * 4, 1)
    table = jnp.concatenate([embed_ref[...], gain_ref[...], jnp.zeros((3, ch), F32)], 0)
    table = jnp.concatenate([table] * 4, 1)
    table = jnp.concatenate([table] * 4, 0)
    group = lax.broadcasted_iota(jnp.int32, table.shape, 0) // 8
    table = jnp.where(group == lax.broadcasted_iota(jnp.int32, table.shape, 1) // ch, table, 0.0)
    high = table.astype(BF).astype(F32)
    ws_ref[...] = jnp.concatenate([high, table - high], 0).astype(BF)
    read = jnp.concatenate([read_ref[...]] * 4, 1)
    high = read.astype(BF).astype(F32)
    row = lax.broadcasted_iota(jnp.int32, (8, lanes), 0)
    read = jnp.where(row < 4, jnp.broadcast_to(high, (8, lanes)), jnp.broadcast_to(read - high, (8, lanes)))
    rw_ref[...] = jnp.where(row % 4 == lax.broadcasted_iota(jnp.int32, (8, lanes), 1) // ch, read, 0.0).astype(BF)


def prepare(conv_weights, embed, soft_gain, conv_bias, readout_weight):
    layers, ch, depth = conv_weights.shape
    vmem = pl.BlockSpec(memory_space=pltpu.VMEM)
    return pl.pallas_call(
        functools.partial(prep_kernel, layers, ch),
        out_shape=(
            jax.ShapeDtypeStruct((layers, 4, 16 * ch, 4 * ch), BF),
            jax.ShapeDtypeStruct((64, 4 * ch), BF),
            jax.ShapeDtypeStruct((8, 4 * ch), F32),
            jax.ShapeDtypeStruct((8, 4 * ch), BF),
        ),
        in_specs=[vmem] * 5,
        out_specs=(vmem,) * 4,
        scratch_shapes=[pltpu.VMEM((depth, ch), F32)],
        compiler_params=pltpu.CompilerParams(vmem_limit_bytes=20 << 20),
        cost_estimate=pl.CostEstimate(flops=0, bytes_accessed=20_000_000, transcendentals=0),
        name="prepare",
    )(conv_weights, embed, soft_gain[None], conv_bias, readout_weight[None])


def main_kernel(
    cfg,
    ev_ref, soft_ref, up_ref, down_ref, next_ref, nup_ref, ndown_ref,
    w_ref, ws_ref, b_ref, rw_ref,
    out_ref,
    c_ref, e_ref, o_ref, d_ref, f_ref, t_ref, m_ref,
):
    layers, tile, strip, cols, n_space, n_tm, n_chan = cfg
    pairs = strip // 2
    rows = strip + 2 * HALO
    slabs = cols // SUB
    half = slabs // 2
    block = half * SUB
    chan = lax.axis_index("chan")
    first_pair = (lax.axis_index("space") * n_chan + chan) * pairs
    all_pairs = n_space * tile // 2
    has_next = jnp.where(lax.axis_index("tm") < n_tm - 1, 1.0, 0.0).astype(F32)

    def lay(slot, up, body, down):
        d_ref[slot, pl.ds(0, HALO), :] = up.astype(F32)
        d_ref[slot, pl.ds(HALO, tile), :] = body.astype(F32)
        d_ref[slot, pl.ds(HALO + tile, HALO), :] = down.astype(F32)

    for window, source in ((0, 0), (2, 2), (1, None)):
        for r in range(2):
            slot = (window * 2 + r) * 2
            if source is None:
                for kind in range(2):
                    lay(slot + kind, nup_ref[kind, r], next_ref[kind, r], ndown_ref[kind, r])
            else:
                lay(slot, up_ref[0, source + r], ev_ref[source + r], down_ref[0, source + r])
                lay(slot + 1, up_ref[1, source + r], soft_ref[source + r], down_ref[1, source + r])

    start = chan * strip
    if strip % 8 == 0:
        start = pl.multiple_of(start, 8)
    gathered = jnp.concatenate([d_ref[k, pl.ds(start, rows), :] for k in range(12)], 0).astype(BF)

    def column(lane):
        q = lane // SUB
        return (lane % SUB) * slabs + 2 * (q % half) + q // half

    perm = (
        lax.broadcasted_iota(jnp.int32, (cols, cols), 0)
        == column(lax.broadcasted_iota(jnp.int32, (cols, cols), 1))
    ).astype(F32).astype(BF)
    gathered = jnp.dot(gathered, perm, preferred_element_type=F32)

    row_id = lax.broadcasted_iota(jnp.int32, (rows, cols), 0) - HALO + first_pair * 2
    inside = (row_id >= 0) & (row_id < 2 * all_pairs)
    odd = (row_id + lax.broadcasted_iota(jnp.int32, (rows, cols), 1) // block) % 2
    for window in range(3):
        for r in range(2):
            slot = (window * 2 + r) * 2
            code = 2.0 * odd.astype(F32) + gathered[slot * rows : (slot + 1) * rows]
            signal = gathered[(slot + 1) * rows : (slot + 2) * rows]
            feats = [jnp.where(inside & (code == float(k)), 1.0, 0.0) for k in range(4)]
            feats.append(jnp.where(inside, signal, 0.0))
            feats += [jnp.zeros((rows, cols), F32)] * 3
            for k, feat in enumerate(feats):
                f_ref[window, pl.ds((r * 8 + k) * rows, rows), :] = feat

    sub_row = lax.broadcasted_iota(jnp.int32, (SUB, 2 * 64), 0)

    def keep(ref, window, pair, value):
        lanes = value.shape[1]
        mid = lanes // 2
        slot = pair + EDGE
        ref[window, slot, pl.ds(1, half)] = value.reshape(half, SUB, lanes).astype(BF)
        last = pltpu.roll(value[block - SUB :, mid:], 1, 0)
        ref[window, slot, 0, :, mid:] = jnp.where(sub_row == 0, 0.0, last).astype(BF)
        head = pltpu.roll(value[:SUB, :mid], SUB - 1, 0)
        ref[window, slot, half + 1, :, :mid] = jnp.where(sub_row == SUB - 1, 0.0, head).astype(BF)

    lanes = ws_ref.shape[1]
    mid = lanes // 2
    for window, reach in ((0, 3), (1, 3), (2, 2)):
        for p in range(-reach, pairs + reach):
            at = 2 * p + HALO
            feats = jnp.concatenate(
                [f_ref[window, pl.ds(at + k, 16, stride=rows), :] for k in range(2)], 0
            )
            feats = jnp.concatenate([feats, feats], 0).astype(BF)
            value = lax.dot_general(
                feats, ws_ref[...], (((0,), (0,)), ((), ())), preferred_element_type=F32
            )
            for k, ref in enumerate((e_ref, o_ref)):
                part = value[:, k * mid : (k + 1) * mid]
                keep(ref, window, p, jnp.concatenate([part[:block], part[block:]], 1))
        if window < 2:
            for ref, p in ((o_ref, -reach - 1), (e_ref, pairs + reach)):
                ref[window, p + EDGE] = jnp.zeros((half + 2, SUB, lanes), BF)

    pieces = (
        (slice(1, half + 1), slice(0, lanes)),
        (slice(0, 1), slice(mid, lanes)),
        (slice(half + 1, half + 2), slice(0, mid)),
    )

    def transform(window, reach):
        low, n = EDGE - reach, pairs + 2 * reach
        for slab, lane in pieces:
            even = e_ref[window, pl.ds(low, n), slab, :, lane]
            after = e_ref[window, pl.ds(low + 1, n), slab, :, lane]
            odd_ = o_ref[window, pl.ds(low, n), slab, :, lane]
            before = o_ref[window, pl.ds(low - 1, n), slab, :, lane]
            c_ref[0, window, pl.ds(low, n), slab, :, lane] = before - odd_
            c_ref[1, window, pl.ds(low, n), slab, :, lane] = even + odd_
            c_ref[2, window, pl.ds(low, n), slab, :, lane] = odd_ - even
            c_ref[3, window, pl.ds(low, n), slab, :, lane] = even - after

    def taps(i, window, low, n):
        view = lambda slab, lane: c_ref[i, window, pl.ds(low, n), slab, :, lane].reshape(n * block, -1)
        return [
            view(slice(0, half), slice(mid, lanes)),
            view(slice(1, half + 1), slice(0, lanes)),
            view(slice(2, half + 2), slice(0, mid)),
        ]

    def layer_step(layer, windows, reach, side, chunk):
        depth = lanes * 4 if side else lanes * 2
        bias = b_ref[pl.ds(layer, 1), :]
        total = pairs + 2 * reach
        for begin in range(0, total, chunk):
            n = min(chunk, total - begin)
            low = EDGE - reach + begin
            spare = begin // chunk % 2
            for i in range(4):
                lhs = []
                for window in windows:
                    parts = taps(i, window, low, n)
                    if side:
                        parts += taps(i, 1, low, n)
                    lhs.append(jnp.concatenate(parts, 1))
                lhs = jnp.concatenate(lhs, 0) if len(lhs) > 1 else lhs[0]
                size = lhs.shape[0]
                m_ref[spare, i, pl.ds(0, size)] = jnp.dot(
                    lhs, w_ref[layer, i, pl.ds(0, depth), :], preferred_element_type=F32
                )
            m = [m_ref[spare, i, pl.ds(0, size)] for i in range(4)]
            base = m[1] + bias
            even = jnp.maximum(base + (m[0] + m[2]), 0.0)
            odd_ = jnp.maximum(base - (m[2] + m[3]), 0.0)
            for k, window in enumerate(windows):
                for q in range(n):
                    p = begin + q - reach
                    at = (k * n + q) * block
                    ev, od = even[at : at + block], odd_[at : at + block]
                    if p < 0 or p >= pairs:
                        spot = first_pair + p
                        ok = jnp.where((spot >= 0) & (spot < all_pairs), 1.0, 0.0).astype(F32)
                        ev, od = ev * ok, od * ok
                    keep(e_ref, window, p, ev)
                    keep(o_ref, window, p, od)

    reach_of = lambda extent: (extent + 1) // 2
    for layer in range(layers):
        reach = reach_of(2 * layers - 1 - layer)
        for window in range(2):
            transform(window, reach)
        layer_step(layer, (0, 1), reach, False, CHUNK // 2)

    def logits(window, at):
        for k, ref in enumerate((e_ref, o_ref)):
            final = ref[window, pl.ds(EDGE, pairs), pl.ds(1, half)].reshape(pairs * block, lanes)
            value = lax.dot_general(
                rw_ref[...], final, (((1,), (1,)), ((), ())), preferred_element_type=F32
            )
            value = value[:4] + value[4:]
            value = jnp.concatenate([value, jnp.zeros_like(value)], 0)
            value = jnp.concatenate([value[:, p * block : (p + 1) * block] for p in range(pairs)], 0)
            high = value.astype(BF)
            rest = value - high.astype(F32)
            mid_part = rest.astype(BF)
            stacked = jnp.concatenate([high, mid_part, (rest - mid_part.astype(F32)).astype(BF)], 0)
            lane = lax.broadcasted_iota(jnp.int32, (block, 2 * cols), 1)
            spot = column(lax.broadcasted_iota(jnp.int32, (block, 2 * cols), 0) + (lane // cols) * block)
            back = (spot == lane % cols).astype(F32).astype(BF)
            value = jnp.dot(stacked, back, preferred_element_type=F32)
            n = pairs * 8
            value = value[:n] + value[n : 2 * n] + value[2 * n :]
            t_ref[0] = value[:, :cols]
            t_ref[1] = value[:, cols:]
            for r in range(2):
                line = t_ref[0, pl.ds(r, pairs, stride=8), :] + t_ref[1, pl.ds(2 + r, pairs, stride=8), :]
                out_ref[at + r, pl.ds(k, pairs, stride=2), :] = line

    logits(0, 0)

    reach = reach_of(layers)
    lane_id = lax.broadcasted_iota(jnp.int32, (SUB, lanes), 1)
    is_next = (lane_id % mid) < mid // 2
    for ref in (e_ref, o_ref):
        for slot in range(EDGE - reach, EDGE + pairs + reach):
            own = ref[0, slot].astype(F32)
            after = ref[1, slot].astype(F32) * has_next
            ref[1, slot] = jnp.where(is_next[None], after, own).astype(BF)
    reach = reach_of(layers - 1)
    transform(1, reach)
    for layer in range(layers):
        reach = reach_of(layers - 1 - layer)
        transform(2, reach)
        layer_step(layer, (2,), reach, True, CHUNK // 2)
    logits(2, 2)


def decode(cfg, arrays, weights):
    layers, tile, strip, cols = cfg[:4]
    rows = strip + 2 * HALO
    pairs = strip // 2
    lanes = weights[1].shape[1]
    slabs = cols // SUB // 2 + 2
    rounds = arrays[0].shape[0]
    vmem = pl.BlockSpec(memory_space=pltpu.VMEM)
    return pl.pallas_call(
        functools.partial(main_kernel, cfg),
        out_shape=jax.ShapeDtypeStruct((rounds, strip, cols), F32),
        in_specs=[vmem] * 11,
        out_specs=vmem,
        scratch_shapes=[
            pltpu.VMEM((4, 3, pairs + 2 * EDGE, slabs, SUB, lanes), BF),
            pltpu.VMEM((3, pairs + 2 * EDGE, slabs, SUB, lanes), BF),
            pltpu.VMEM((3, pairs + 2 * EDGE, slabs, SUB, lanes), BF),
            pltpu.VMEM((12, tile + 2 * HALO, cols), F32),
            pltpu.VMEM((3, 16 * rows, cols), F32),
            pltpu.VMEM((2, pairs * 8, cols), F32),
            pltpu.VMEM((2, 4, CHUNK * (slabs - 2) * SUB, lanes), F32),
        ],
        compiler_params=pltpu.CompilerParams(vmem_limit_bytes=40 << 20),
        name="decode",
    )(*arrays, *weights)


def per_device(sizes, events, soft_info, embed, soft_gain, conv_weights, conv_bias, readout_weight):
    n_space, n_tm, n_chan = sizes
    rounds, tile, cols = events.shape
    layers = conv_weights.shape[0]
    strip = tile // n_chan
    first = rounds // 2
    both = jnp.stack([events.astype(BF), soft_info])
    ahead = both[:, :first]
    shift_tm = [(t, t - 1) for t in range(1, n_tm)]
    if n_chan == 2 and strip >= HALO:
        chan = lax.axis_index("chan")
        edge = jnp.where(chan == 0, both[:, :, tile - HALO :], both[:, :, :HALO])
        own, diag = [], []
        for s in range(n_space):
            for c in range(n_chan):
                to = s + (1 if c == 0 else -1)
                if not 0 <= to < n_space:
                    continue
                own.append((s * n_chan + c, to * n_chan + c))
                for t in range(1, n_tm):
                    diag.append(((s * n_tm + t) * n_chan + c, (to * n_tm + t - 1) * n_chan + c))
        up = down = lax.ppermute(edge, ("space", "chan"), own)
        nup = ndown = lax.ppermute(edge[:, :first], ("space", "tm", "chan"), diag)
    else:
        low, high = both[:, :, :HALO], both[:, :, tile - HALO :]

        def pairs_of(step):
            return [(s, s + step) for s in range(n_space) if 0 <= s + step < n_space]

        def cross(step):
            return [(s * n_tm + t, to * n_tm + t - 1) for s, to in pairs_of(step) for t in range(1, n_tm)]

        up = lax.ppermute(high, "space", pairs_of(1))
        down = lax.ppermute(low, "space", pairs_of(-1))
        nup = lax.ppermute(high[:, :first], ("space", "tm"), cross(1))
        ndown = lax.ppermute(low[:, :first], ("space", "tm"), cross(-1))
    following = lax.ppermute(ahead, "tm", shift_tm)
    weights = prepare(conv_weights, embed, soft_gain, conv_bias, readout_weight)
    cfg = (layers, tile, strip, cols, n_space, n_tm, n_chan)
    mine = decode(cfg, (events, soft_info, up, down, following, nup, ndown), weights)
    parts = [mine]
    for step in range(1, n_chan):
        parts.append(lax.ppermute(mine, "chan", [(c, (c - step) % n_chan) for c in range(n_chan)]))
    chan = lax.axis_index("chan")
    ordered = [lax.select_n((c - chan) % n_chan, *parts) for c in range(n_chan)]
    return jnp.concatenate(ordered, 1)


def solution(mesh):
    split = P(("parts", "tm"), "space", None)
    sizes = tuple(mesh.shape[axis] for axis in ("space", "tm", "chan"))
    return jax.shard_map(
        functools.partial(per_device, sizes),
        mesh=mesh,
        in_specs=(split, split, P(), P(), P(), P(), P()),
        out_specs=split,
        check_vma=False,
    )
```

```python
import functools

import jax
import jax.numpy as jnp
from jax import lax
from jax.experimental import pallas as pl
from jax.experimental.pallas import tpu as pltpu
from jax.sharding import PartitionSpec as P

HALO = 8
SUB = 16
EDGE = 4
CHUNK = 8
BF = jnp.bfloat16
F32 = jnp.float32


def pack_kernel(n_chan, *refs):
    ev_hbm, soft_hbm = refs[:2]
    small_in, small_out = refs[2:7], refs[11:16]
    both_ref, ahead_ref, edge_ref, first_ref = refs[7:11]
    ev_ref, soft_ref, sems = refs[16:]
    copies = [
        pltpu.make_async_copy(source, target, sems.at[k])
        for k, (source, target) in enumerate(
            zip((ev_hbm, soft_hbm) + small_in, (ev_ref, soft_ref) + small_out)
        )
    ]
    for copy in copies:
        copy.start()
    copies[0].wait()
    copies[1].wait()
    rounds, tile, _ = ev_ref.shape
    lower = lax.axis_index("chan") < n_chan - 1
    for r in range(rounds):
        for kind, value in enumerate((ev_ref[r].astype(F32), soft_ref[r].astype(F32))):
            narrow = value.astype(BF)
            both_ref[kind, r] = narrow
            edge = jnp.where(lower, value[tile - HALO :], value[:HALO]).astype(BF)
            edge_ref[kind, r] = edge
            if r < rounds // 2:
                ahead_ref[kind, r] = narrow
                first_ref[kind, r] = edge
    for copy in copies[2:]:
        copy.wait()


def pack(n_chan, events, soft_info, small):
    rounds, tile, cols = events.shape
    vmem = pl.BlockSpec(memory_space=pltpu.VMEM)
    outs = [
        jax.ShapeDtypeStruct((2, rounds, tile, cols), BF),
        jax.ShapeDtypeStruct((2, rounds // 2, tile, cols), BF),
        jax.ShapeDtypeStruct((2, rounds, HALO, cols), BF),
        jax.ShapeDtypeStruct((2, rounds // 2, HALO, cols), BF),
    ] + [jax.ShapeDtypeStruct(x.shape, x.dtype) for x in small]
    return pl.pallas_call(
        functools.partial(pack_kernel, n_chan),
        out_shape=outs,
        in_specs=[pl.BlockSpec(memory_space=pltpu.HBM)] * 7,
        out_specs=[vmem] * len(outs),
        scratch_shapes=[
            pltpu.VMEM(events.shape, jnp.int32),
            pltpu.VMEM(soft_info.shape, BF),
            pltpu.SemaphoreType.DMA((7,)),
        ],
        compiler_params=pltpu.CompilerParams(vmem_limit_bytes=8 << 20),
        name="pack",
    )(*[pltpu.with_memory_space_constraint(x, pltpu.HBM) for x in (events, soft_info, *small)])


def prep_kernel(layers, ch, w_ref, embed_ref, gain_ref, bias_ref, read_ref, wout_ref, ws_ref, bout_ref, rw_ref, wt_ref):
    lanes = 4 * ch
    taps = 27
    zero_half = jnp.zeros((ch, ch), F32)
    zero_block = jnp.zeros((2 * ch, 2 * ch), BF)
    for layer in range(layers):
        wt_ref[...] = w_ref[layer].astype(F32).T
        for dx in range(3):
            sets = []
            for dr in range(3):
                g = [wt_ref[pl.ds(dr * 9 + dy * 3 + dx, ch, stride=taps), :] for dy in range(3)]
                outer = (g[0] + g[2]) * 0.5
                inner = g[1] * 0.5
                sets.append((g[0], outer + inner, outer - inner, g[2]))
            for i in range(4):
                own = jnp.concatenate(
                    [
                        jnp.concatenate([sets[1][i], sets[0][i]], 1),
                        jnp.concatenate([sets[2][i], sets[1][i]], 1),
                    ],
                    0,
                ).astype(BF)
                side = jnp.concatenate(
                    [
                        jnp.concatenate([zero_half, sets[2][i]], 1),
                        jnp.concatenate([sets[0][i], zero_half], 1),
                    ],
                    0,
                ).astype(BF)
                for b in range(2):
                    a = dx + b
                    wout_ref[layer, i, pl.ds(a * 2 * ch, 2 * ch), pl.ds(b * 2 * ch, 2 * ch)] = own
                    wout_ref[layer, i, pl.ds(lanes * 2 + a * 2 * ch, 2 * ch), pl.ds(b * 2 * ch, 2 * ch)] = side
        for i in range(4):
            for base in (0, lanes * 2):
                wout_ref[layer, i, pl.ds(base + 6 * ch, 2 * ch), pl.ds(0, 2 * ch)] = zero_block
                wout_ref[layer, i, pl.ds(base, 2 * ch), pl.ds(2 * ch, 2 * ch)] = zero_block
        bout_ref[pl.ds(layer, 1), :] = jnp.concatenate([bias_ref[pl.ds(layer, 1), :]] * 4, 1)
    table = jnp.concatenate([embed_ref[...], gain_ref[...], jnp.zeros((3, ch), F32)], 0)
    table = jnp.concatenate([table] * 4, 1)
    table = jnp.concatenate([table] * 4, 0)
    group = lax.broadcasted_iota(jnp.int32, table.shape, 0) // 8
    table = jnp.where(group == lax.broadcasted_iota(jnp.int32, table.shape, 1) // ch, table, 0.0)
    high = table.astype(BF).astype(F32)
    ws_ref[...] = jnp.concatenate([high, table - high], 0).astype(BF)
    read = jnp.concatenate([read_ref[...]] * 4, 1)
    high = read.astype(BF).astype(F32)
    row = lax.broadcasted_iota(jnp.int32, (8, lanes), 0)
    read = jnp.where(row < 4, jnp.broadcast_to(high, (8, lanes)), jnp.broadcast_to(read - high, (8, lanes)))
    rw_ref[...] = jnp.where(row % 4 == lax.broadcasted_iota(jnp.int32, (8, lanes), 1) // ch, read, 0.0).astype(BF)


def prepare(conv_weights, embed, soft_gain, conv_bias, readout_weight):
    layers, ch, depth = conv_weights.shape
    vmem = pl.BlockSpec(memory_space=pltpu.VMEM)
    return pl.pallas_call(
        functools.partial(prep_kernel, layers, ch),
        out_shape=(
            jax.ShapeDtypeStruct((layers, 4, 16 * ch, 4 * ch), BF),
            jax.ShapeDtypeStruct((64, 4 * ch), BF),
            jax.ShapeDtypeStruct((8, 4 * ch), F32),
            jax.ShapeDtypeStruct((8, 4 * ch), BF),
        ),
        in_specs=[vmem] * 5,
        out_specs=(vmem,) * 4,
        scratch_shapes=[pltpu.VMEM((depth, ch), F32)],
        compiler_params=pltpu.CompilerParams(vmem_limit_bytes=20 << 20),
        cost_estimate=pl.CostEstimate(flops=0, bytes_accessed=20_000_000, transcendentals=0),
        name="prepare",
    )(conv_weights, embed, soft_gain, conv_bias, readout_weight)


def main_kernel(
    cfg,
    both_ref, up_ref, down_ref, next_ref, nup_ref, ndown_ref,
    w_ref, ws_ref, b_ref, rw_ref,
    out_ref,
    c_ref, e_ref, o_ref, d_ref, f_ref, t_ref, m_ref,
):
    layers, tile, strip, cols, n_space, n_tm, n_chan = cfg
    pairs = strip // 2
    rows = strip + 2 * HALO
    slabs = cols // SUB
    half = slabs // 2
    block = half * SUB
    chan = lax.axis_index("chan")
    first_pair = (lax.axis_index("space") * n_chan + chan) * pairs
    all_pairs = n_space * tile // 2
    has_next = lax.axis_index("tm") < n_tm - 1

    def lay(slot, up, body, down):
        d_ref[slot, pl.ds(0, HALO), :] = up.astype(F32)
        d_ref[slot, pl.ds(HALO, tile), :] = body.astype(F32)
        d_ref[slot, pl.ds(HALO + tile, HALO), :] = down.astype(F32)

    for window, source in ((0, 0), (2, 2), (1, None)):
        for r in range(2):
            slot = (window * 2 + r) * 2
            if source is None:
                for kind in range(2):
                    lay(slot + kind, nup_ref[kind, r], next_ref[kind, r], ndown_ref[kind, r])
            else:
                for kind in range(2):
                    at = (kind, source + r)
                    lay(slot + kind, up_ref[at], both_ref[at], down_ref[at])

    start = chan * strip
    if strip % 8 == 0:
        start = pl.multiple_of(start, 8)
    gathered = jnp.concatenate([d_ref[k, pl.ds(start, rows), :] for k in range(12)], 0).astype(BF)

    def column(lane):
        q = lane // SUB
        return (lane % SUB) * slabs + 2 * (q % half) + q // half

    perm = (
        lax.broadcasted_iota(jnp.int32, (cols, cols), 0)
        == column(lax.broadcasted_iota(jnp.int32, (cols, cols), 1))
    ).astype(F32).astype(BF)
    gathered = jnp.dot(gathered, perm, preferred_element_type=F32)

    row_id = lax.broadcasted_iota(jnp.int32, (rows, cols), 0) - HALO + first_pair * 2
    inside = (row_id >= 0) & (row_id < 2 * all_pairs)
    odd = (row_id + lax.broadcasted_iota(jnp.int32, (rows, cols), 1) // block) % 2
    for window in range(3):
        for r in range(2):
            slot = (window * 2 + r) * 2
            code = 2.0 * odd.astype(F32) + gathered[slot * rows : (slot + 1) * rows]
            signal = gathered[(slot + 1) * rows : (slot + 2) * rows]
            feats = [jnp.where(inside & (code == float(k)), 1.0, 0.0) for k in range(4)]
            feats.append(jnp.where(inside, signal, 0.0))
            feats += [jnp.zeros((rows, cols), F32)] * 3
            for k, feat in enumerate(feats):
                f_ref[window, pl.ds((r * 8 + k) * rows, rows), :] = feat

    sub_row = lax.broadcasted_iota(jnp.int32, (SUB, 2 * 64), 0)

    def keep(ref, window, pair, value):
        lanes = value.shape[1]
        mid = lanes // 2
        slot = pair + EDGE
        ref[window, slot, pl.ds(1, half)] = value.reshape(half, SUB, lanes).astype(BF)
        last = pltpu.roll(value[block - SUB :, mid:], 1, 0)
        ref[window, slot, 0, :, mid:] = jnp.where(sub_row == 0, 0.0, last).astype(BF)
        head = pltpu.roll(value[:SUB, :mid], SUB - 1, 0)
        ref[window, slot, half + 1, :, :mid] = jnp.where(sub_row == SUB - 1, 0.0, head).astype(BF)

    lanes = ws_ref.shape[1]
    mid = lanes // 2
    for window, reach in ((0, 3), (1, 3), (2, 2)):
        for p in range(-reach, pairs + reach):
            at = 2 * p + HALO
            feats = jnp.concatenate(
                [f_ref[window, pl.ds(at + k, 16, stride=rows), :] for k in range(2)], 0
            )
            feats = jnp.concatenate([feats, feats], 0).astype(BF)
            value = lax.dot_general(
                feats, ws_ref[...], (((0,), (0,)), ((), ())), preferred_element_type=F32
            )
            for k, ref in enumerate((e_ref, o_ref)):
                part = value[:, k * mid : (k + 1) * mid]
                keep(ref, window, p, jnp.concatenate([part[:block], part[block:]], 1))
        if window < 2:
            for ref, p in ((o_ref, -reach - 1), (e_ref, pairs + reach)):
                ref[window, p + EDGE] = jnp.zeros((half + 2, SUB, lanes), BF)

    pieces = (
        (slice(1, half + 1), slice(0, lanes)),
        (slice(0, 1), slice(mid, lanes)),
        (slice(half + 1, half + 2), slice(0, mid)),
    )

    def transform(window, reach):
        low, n = EDGE - reach, pairs + 2 * reach
        for slab, lane in pieces:
            even = e_ref[window, pl.ds(low, n), slab, :, lane]
            after = e_ref[window, pl.ds(low + 1, n), slab, :, lane]
            odd_ = o_ref[window, pl.ds(low, n), slab, :, lane]
            before = o_ref[window, pl.ds(low - 1, n), slab, :, lane]
            c_ref[0, window, pl.ds(low, n), slab, :, lane] = before - odd_
            c_ref[1, window, pl.ds(low, n), slab, :, lane] = even + odd_
            c_ref[2, window, pl.ds(low, n), slab, :, lane] = odd_ - even
            c_ref[3, window, pl.ds(low, n), slab, :, lane] = even - after

    def taps(i, window, low, n):
        view = lambda slab, lane: c_ref[i, window, pl.ds(low, n), slab, :, lane].reshape(n * block, -1)
        return [
            view(slice(0, half), slice(mid, lanes)),
            view(slice(1, half + 1), slice(0, lanes)),
            view(slice(2, half + 2), slice(0, mid)),
        ]

    def layer_step(layer, windows, reach, side, chunk):
        depth = lanes * 4 if side else lanes * 2
        bias = b_ref[pl.ds(layer, 1), :]
        total = pairs + 2 * reach
        for begin in range(0, total, chunk):
            n = min(chunk, total - begin)
            low = EDGE - reach + begin
            spare = begin // chunk % 2
            for i in range(4):
                lhs = []
                for window in windows:
                    parts = taps(i, window, low, n)
                    if side:
                        parts += taps(i, 1, low, n)
                    lhs.append(jnp.concatenate(parts, 1))
                lhs = jnp.concatenate(lhs, 0) if len(lhs) > 1 else lhs[0]
                size = lhs.shape[0]
                m_ref[spare, i, pl.ds(0, size)] = jnp.dot(
                    lhs, w_ref[layer, i, pl.ds(0, depth), :], preferred_element_type=F32
                )
            m = [m_ref[spare, i, pl.ds(0, size)] for i in range(4)]
            base = m[1] + bias
            even = jnp.maximum(base + (m[0] + m[2]), 0.0)
            odd_ = jnp.maximum(base - (m[2] + m[3]), 0.0)
            for k, window in enumerate(windows):
                for q in range(n):
                    p = begin + q - reach
                    at = (k * n + q) * block
                    ev, od = even[at : at + block], odd_[at : at + block]
                    if p < 0 or p >= pairs:
                        spot = first_pair + p
                        ok = jnp.where((spot >= 0) & (spot < all_pairs), 1.0, 0.0).astype(F32)
                        ev, od = ev * ok, od * ok
                    keep(e_ref, window, p, ev)
                    keep(o_ref, window, p, od)

    reach_of = lambda extent: (extent + 1) // 2
    for layer in range(layers):
        reach = reach_of(2 * layers - 1 - layer)
        for window in range(2):
            transform(window, reach)
        layer_step(layer, (0, 1), reach, False, CHUNK // 2)

    def logits(window, at):
        for k, ref in enumerate((e_ref, o_ref)):
            final = ref[window, pl.ds(EDGE, pairs), pl.ds(1, half)].reshape(pairs * block, lanes)
            value = lax.dot_general(
                rw_ref[...], final, (((1,), (1,)), ((), ())), preferred_element_type=F32
            )
            value = value[:4] + value[4:]
            value = jnp.concatenate([value, jnp.zeros_like(value)], 0)
            value = jnp.concatenate([value[:, p * block : (p + 1) * block] for p in range(pairs)], 0)
            high = value.astype(BF)
            rest = value - high.astype(F32)
            mid_part = rest.astype(BF)
            stacked = jnp.concatenate([high, mid_part, (rest - mid_part.astype(F32)).astype(BF)], 0)
            lane = lax.broadcasted_iota(jnp.int32, (block, 2 * cols), 1)
            spot = column(lax.broadcasted_iota(jnp.int32, (block, 2 * cols), 0) + (lane // cols) * block)
            back = (spot == lane % cols).astype(F32).astype(BF)
            value = jnp.dot(stacked, back, preferred_element_type=F32)
            n = pairs * 8
            value = value[:n] + value[n : 2 * n] + value[2 * n :]
            t_ref[0] = value[:, :cols]
            t_ref[1] = value[:, cols:]
            for r in range(2):
                line = t_ref[0, pl.ds(r, pairs, stride=8), :] + t_ref[1, pl.ds(2 + r, pairs, stride=8), :]
                out_ref[at + r, pl.ds(k, pairs, stride=2), :] = line

    logits(0, 0)

    reach = reach_of(layers)
    lane_id = lax.broadcasted_iota(jnp.int32, (SUB, lanes), 1)
    is_next = (lane_id % mid) < mid // 2
    for ref in (e_ref, o_ref):
        for slot in range(EDGE - reach, EDGE + pairs + reach):
            own = ref[0, slot].astype(F32)
            after = jnp.where(has_next, ref[1, slot].astype(F32), 0.0)
            ref[1, slot] = jnp.where(is_next[None], after, own).astype(BF)
    reach = reach_of(layers - 1)
    transform(1, reach)
    for layer in range(layers):
        reach = reach_of(layers - 1 - layer)
        transform(2, reach)
        layer_step(layer, (2,), reach, True, CHUNK // 2)
    logits(2, 2)


def decode(cfg, arrays, weights):
    layers, tile, strip, cols = cfg[:4]
    rows = strip + 2 * HALO
    pairs = strip // 2
    lanes = weights[1].shape[1]
    slabs = cols // SUB // 2 + 2
    rounds = arrays[0].shape[1]
    vmem = pl.BlockSpec(memory_space=pltpu.VMEM)
    return pl.pallas_call(
        functools.partial(main_kernel, cfg),
        out_shape=jax.ShapeDtypeStruct((rounds, strip, cols), F32),
        in_specs=[vmem] * 10,
        out_specs=vmem,
        scratch_shapes=[
            pltpu.VMEM((4, 3, pairs + 2 * EDGE, slabs, SUB, lanes), BF),
            pltpu.VMEM((3, pairs + 2 * EDGE, slabs, SUB, lanes), BF),
            pltpu.VMEM((3, pairs + 2 * EDGE, slabs, SUB, lanes), BF),
            pltpu.VMEM((12, tile + 2 * HALO, cols), F32),
            pltpu.VMEM((3, 16 * rows, cols), F32),
            pltpu.VMEM((2, pairs * 8, cols), F32),
            pltpu.VMEM((2, 4, CHUNK * (slabs - 2) * SUB, lanes), F32),
        ],
        compiler_params=pltpu.CompilerParams(vmem_limit_bytes=40 << 20),
        name="decode",
    )(*arrays, *weights)


def per_device(sizes, events, soft_info, embed, soft_gain, conv_weights, conv_bias, readout_weight):
    n_space, n_tm, n_chan = sizes
    rounds, tile, cols = events.shape
    layers = conv_weights.shape[0]
    strip = tile // n_chan
    packed = pack(
        n_chan,
        events,
        soft_info,
        (conv_weights, embed, soft_gain[None], conv_bias, readout_weight[None]),
    )
    both, ahead, edge, edge_first = packed[:4]
    back = [(t, (t - 1) % n_tm) for t in range(n_tm)]
    following = lax.ppermute(ahead, "tm", back)
    if n_chan == 2 and strip >= HALO:
        own, diag = [], []
        for s in range(n_space):
            for c in range(2):
                to = s + 1 - 2 * c
                spot = (to, c) if 0 <= to < n_space else (s, 1 - c)
                own.append((s * 2 + c, spot[0] * 2 + spot[1]))
                for t, u in back:
                    diag.append(((s * n_tm + t) * 2 + c, (spot[0] * n_tm + u) * 2 + spot[1]))
        up = down = lax.ppermute(edge, ("space", "chan"), own)
        nup = ndown = lax.ppermute(edge_first, ("space", "tm", "chan"), diag)
    else:
        low, high = both[:, :, :HALO], both[:, :, tile - HALO :]
        first = rounds // 2

        def ring(step):
            return [(s, (s + step) % n_space) for s in range(n_space)]

        def cross(step):
            return [(s * n_tm + t, to * n_tm + u) for s, to in ring(step) for t, u in back]

        up = lax.ppermute(high, "space", ring(1))
        down = lax.ppermute(low, "space", ring(-1))
        nup = lax.ppermute(high[:, :first], ("space", "tm"), cross(1))
        ndown = lax.ppermute(low[:, :first], ("space", "tm"), cross(-1))
    weights = prepare(*packed[4:])
    cfg = (layers, tile, strip, cols, n_space, n_tm, n_chan)
    mine = decode(cfg, (both, up, down, following, nup, ndown), weights)
    parts = [mine]
    for step in range(1, n_chan):
        parts.append(lax.ppermute(mine, "chan", [(c, (c - step) % n_chan) for c in range(n_chan)]))
    chan = lax.axis_index("chan")
    ordered = [lax.select_n((c - chan) % n_chan, *parts) for c in range(n_chan)]
    return jnp.concatenate(ordered, 1)


def solution(mesh):
    split = P(("parts", "tm"), "space", None)
    sizes = tuple(mesh.shape[axis] for axis in ("space", "tm", "chan"))
    return jax.shard_map(
        functools.partial(per_device, sizes),
        mesh=mesh,
        in_specs=(split, split, P(), P(), P(), P(), P()),
        out_specs=split,
        check_vma=False,
    )
```

```python
import functools

import jax
import jax.numpy as jnp
from jax import lax
from jax.experimental import pallas as pl
from jax.experimental.pallas import tpu as pltpu
from jax.sharding import PartitionSpec as P

HALO = 8
SUB = 16
EDGE = 4
CHUNK = 13
BF = jnp.bfloat16
F32 = jnp.float32


def pack_kernel(n_chan, *refs):
    ev_hbm, soft_hbm = refs[:2]
    small_in, small_out = refs[2:7], refs[9:14]
    both_ref, edge_ref = refs[7:9]
    ev_ref, soft_ref, sems = refs[14:]
    copies = [
        pltpu.make_async_copy(source, target, sems.at[k])
        for k, (source, target) in enumerate(
            zip((ev_hbm, soft_hbm) + small_in, (ev_ref, soft_ref) + small_out)
        )
    ]
    for copy in copies:
        copy.start()
    copies[0].wait()
    copies[1].wait()
    rounds, tile, _ = ev_ref.shape
    lower = lax.axis_index("chan") < n_chan - 1
    for r in range(rounds):
        for kind, value in enumerate((ev_ref[r].astype(F32), soft_ref[r].astype(F32))):
            both_ref[kind, r] = value.astype(BF)
            edge_ref[kind, r] = jnp.where(lower, value[tile - HALO :], value[:HALO]).astype(BF)
    for copy in copies[2:]:
        copy.wait()


def pack(n_chan, events, soft_info, small):
    rounds, tile, cols = events.shape
    vmem = pl.BlockSpec(memory_space=pltpu.VMEM)
    outs = [
        jax.ShapeDtypeStruct((2, rounds, tile, cols), BF),
        jax.ShapeDtypeStruct((2, rounds, HALO, cols), BF),
    ] + [jax.ShapeDtypeStruct(x.shape, x.dtype) for x in small]
    return pl.pallas_call(
        functools.partial(pack_kernel, n_chan),
        out_shape=outs,
        in_specs=[pl.BlockSpec(memory_space=pltpu.HBM)] * 7,
        out_specs=[vmem] * len(outs),
        scratch_shapes=[
            pltpu.VMEM(events.shape, jnp.int32),
            pltpu.VMEM(soft_info.shape, BF),
            pltpu.SemaphoreType.DMA((7,)),
        ],
        compiler_params=pltpu.CompilerParams(vmem_limit_bytes=8 << 20),
        name="pack",
    )(*[pltpu.with_memory_space_constraint(x, pltpu.HBM) for x in (events, soft_info, *small)])


def prep_kernel(layers, ch, w_ref, embed_ref, gain_ref, bias_ref, read_ref, wout_ref, ws_ref, bout_ref, rw_ref, wt_ref):
    lanes = 4 * ch
    taps = 27
    zero_half = jnp.zeros((ch, ch), F32)
    zero_block = jnp.zeros((2 * ch, 2 * ch), BF)
    for layer in range(layers):
        wt_ref[...] = w_ref[layer].astype(F32).T
        for dx in range(3):
            sets = []
            for dr in range(3):
                g = [wt_ref[pl.ds(dr * 9 + dy * 3 + dx, ch, stride=taps), :] for dy in range(3)]
                outer = (g[0] + g[2]) * 0.5
                inner = g[1] * 0.5
                sets.append((g[0], outer + inner, outer - inner, g[2]))
            for i in range(4):
                own = jnp.concatenate(
                    [
                        jnp.concatenate([sets[1][i], sets[0][i]], 1),
                        jnp.concatenate([sets[2][i], sets[1][i]], 1),
                    ],
                    0,
                ).astype(BF)
                side = jnp.concatenate(
                    [
                        jnp.concatenate([zero_half, sets[2][i]], 1),
                        jnp.concatenate([sets[0][i], zero_half], 1),
                    ],
                    0,
                ).astype(BF)
                for b in range(2):
                    a = dx + b
                    wout_ref[layer, i, pl.ds(a * 2 * ch, 2 * ch), pl.ds(b * 2 * ch, 2 * ch)] = own
                    wout_ref[layer, i, pl.ds(lanes * 2 + a * 2 * ch, 2 * ch), pl.ds(b * 2 * ch, 2 * ch)] = side
        for i in range(4):
            for base in (0, lanes * 2):
                wout_ref[layer, i, pl.ds(base + 6 * ch, 2 * ch), pl.ds(0, 2 * ch)] = zero_block
                wout_ref[layer, i, pl.ds(base, 2 * ch), pl.ds(2 * ch, 2 * ch)] = zero_block
        bout_ref[pl.ds(layer, 1), :] = jnp.concatenate([bias_ref[pl.ds(layer, 1), :]] * 4, 1)
    table = jnp.concatenate([embed_ref[...], gain_ref[...], jnp.zeros((3, ch), F32)], 0)
    table = jnp.concatenate([table] * 4, 1)
    table = jnp.concatenate([table] * 4, 0)
    group = lax.broadcasted_iota(jnp.int32, table.shape, 0) // 8
    table = jnp.where(group == lax.broadcasted_iota(jnp.int32, table.shape, 1) // ch, table, 0.0)
    high = table.astype(BF).astype(F32)
    ws_ref[...] = jnp.concatenate([high, table - high], 0).astype(BF)
    read = jnp.concatenate([read_ref[...]] * 4, 1)
    high = read.astype(BF).astype(F32)
    row = lax.broadcasted_iota(jnp.int32, (8, lanes), 0)
    read = jnp.where(row < 4, jnp.broadcast_to(high, (8, lanes)), jnp.broadcast_to(read - high, (8, lanes)))
    rw_ref[...] = jnp.where(row % 4 == lax.broadcasted_iota(jnp.int32, (8, lanes), 1) // ch, read, 0.0).astype(BF)


def prepare(conv_weights, embed, soft_gain, conv_bias, readout_weight):
    layers, ch, depth = conv_weights.shape
    vmem = pl.BlockSpec(memory_space=pltpu.VMEM)
    return pl.pallas_call(
        functools.partial(prep_kernel, layers, ch),
        out_shape=(
            jax.ShapeDtypeStruct((layers, 4, 16 * ch, 4 * ch), BF),
            jax.ShapeDtypeStruct((64, 4 * ch), BF),
            jax.ShapeDtypeStruct((8, 4 * ch), F32),
            jax.ShapeDtypeStruct((8, 4 * ch), BF),
        ),
        in_specs=[vmem] * 5,
        out_specs=(vmem,) * 4,
        scratch_shapes=[pltpu.VMEM((depth, ch), F32)],
        compiler_params=pltpu.CompilerParams(vmem_limit_bytes=20 << 20),
        cost_estimate=pl.CostEstimate(flops=0, bytes_accessed=20_000_000, transcendentals=0),
        name="prepare",
    )(conv_weights, embed, soft_gain, conv_bias, readout_weight)


def window_kernel(n_chan, both_ref, up_ref, down_ref, own_ref, send_ref, d_ref):
    _, rounds, tile, _ = both_ref.shape
    strip = tile // n_chan
    start = lax.axis_index("chan") * strip
    if strip % 8 == 0:
        start = pl.multiple_of(start, 8)
    for r in range(rounds):
        for kind in range(2):
            slot = r * 2 + kind
            d_ref[slot, pl.ds(0, HALO), :] = up_ref[kind, r].astype(F32)
            d_ref[slot, pl.ds(HALO, tile), :] = both_ref[kind, r].astype(F32)
            d_ref[slot, pl.ds(HALO + tile, HALO), :] = down_ref[kind, r].astype(F32)
            value = d_ref[slot, pl.ds(start, strip + 2 * HALO), :].astype(BF)
            own_ref[kind, r] = value
            if r < rounds // 2:
                send_ref[kind, r] = value


def cut_window(n_chan, both, up, down):
    kinds, rounds, tile, cols = both.shape
    rows = tile // n_chan + 2 * HALO
    vmem = pl.BlockSpec(memory_space=pltpu.VMEM)
    return pl.pallas_call(
        functools.partial(window_kernel, n_chan),
        out_shape=(
            jax.ShapeDtypeStruct((kinds, rounds, rows, cols), BF),
            jax.ShapeDtypeStruct((kinds, rounds // 2, rows, cols), BF),
        ),
        in_specs=[vmem] * 3,
        out_specs=(vmem,) * 2,
        scratch_shapes=[pltpu.VMEM((kinds * rounds, tile + 2 * HALO, cols), F32)],
        compiler_params=pltpu.CompilerParams(vmem_limit_bytes=8 << 20),
        name="window",
    )(both, up, down)


class Strip:
    def __init__(self, cfg, lanes):
        self.layers, tile, strip, self.cols, n_space, n_tm, n_chan = cfg
        self.strip, self.pairs = strip, strip // 2
        self.rows = strip + 2 * HALO
        self.slabs = self.cols // SUB
        self.half = self.slabs // 2
        self.block = self.half * SUB
        self.lanes, self.mid = lanes, lanes // 2
        self.first_row = (lax.axis_index("space") * n_chan + lax.axis_index("chan")) * strip
        self.all_rows = n_space * tile
        self.has_next = lax.axis_index("tm") < n_tm - 1
        self.sub_row = lax.broadcasted_iota(jnp.int32, (SUB, self.mid), 0)

    def column(self, lane):
        q = lane // SUB
        return (lane % SUB) * self.slabs + 2 * (q % self.half) + q // self.half

    def features(self, arrays, f_ref):
        cols, rows = self.cols, self.rows
        perm = (
            lax.broadcasted_iota(jnp.int32, (cols, cols), 0)
            == self.column(lax.broadcasted_iota(jnp.int32, (cols, cols), 1))
        ).astype(F32).astype(BF)
        gathered = jnp.dot(jnp.concatenate(arrays, 0), perm, preferred_element_type=F32)
        row_id = lax.broadcasted_iota(jnp.int32, (rows, cols), 0) - HALO + self.first_row
        inside = (row_id >= 0) & (row_id < self.all_rows)
        odd = (row_id + lax.broadcasted_iota(jnp.int32, (rows, cols), 1) // self.block) % 2
        base = 2.0 * odd.astype(F32)
        for slot in range(0, len(arrays), 2):
            code = base + gathered[slot * rows : (slot + 1) * rows]
            signal = gathered[(slot + 1) * rows : (slot + 2) * rows]
            feats = [jnp.where(inside & (code == float(k)), 1.0, 0.0) for k in range(4)]
            feats.append(jnp.where(inside, signal, 0.0))
            feats += [jnp.zeros((rows, cols), F32)] * 3
            for k, feat in enumerate(feats):
                f_ref[slot // 4, pl.ds((slot // 2 % 2 * 8 + k) * rows, rows), :] = feat

    def keep(self, ref, pair, value):
        half, block, mid = self.half, self.block, self.mid
        slot = pair + EDGE
        ref[slot, pl.ds(1, half)] = value.reshape(half, SUB, self.lanes).astype(BF)
        last = pltpu.roll(value[block - SUB :, mid:], 1, 0)
        ref[slot, 0, :, mid:] = jnp.where(self.sub_row == 0, 0.0, last).astype(BF)
        head = pltpu.roll(value[:SUB, :mid], SUB - 1, 0)
        ref[slot, half + 1, :, :mid] = jnp.where(self.sub_row == SUB - 1, 0.0, head).astype(BF)

    def begin(self, f_ref, ws_ref, e_ref, o_ref, reach):
        block, mid = self.block, self.mid
        for p in range(-reach, self.pairs + reach):
            at = 2 * p + HALO
            feats = jnp.concatenate(
                [f_ref[pl.ds(at + k, 16, stride=self.rows), :] for k in range(2)], 0
            )
            feats = jnp.concatenate([feats, feats], 0).astype(BF)
            value = lax.dot_general(
                feats, ws_ref[...], (((0,), (0,)), ((), ())), preferred_element_type=F32
            )
            for k, ref in enumerate((e_ref, o_ref)):
                part = value[:, k * mid : (k + 1) * mid]
                self.keep(ref, p, jnp.concatenate([part[:block], part[block:]], 1))

    def reach(self, extent):
        return EDGE - (extent + 1) // 2, self.pairs + extent, extent % 2

    def transform(self, e_ref, o_ref, c_ref, extent):
        half, lanes, mid = self.half, self.lanes, self.mid
        low, n, shift = self.reach(extent)
        for slab, lane in (
            (slice(1, half + 1), slice(0, lanes)),
            (slice(0, 1), slice(mid, lanes)),
            (slice(half + 1, half + 2), slice(0, mid)),
        ):
            view = lambda ref, step: ref[pl.ds(low + step, n), slab, :, lane]
            if shift:
                d = (view(e_ref, 0), view(o_ref, 0), view(e_ref, 1), view(o_ref, 1))
            else:
                d = (view(o_ref, -1), view(e_ref, 0), view(o_ref, 0), view(e_ref, 1))
            for i, value in enumerate((d[0] - d[2], d[1] + d[2], d[2] - d[1], d[1] - d[3])):
                c_ref[i, pl.ds(low, n), slab, :, lane] = value

    def taps(self, c_ref, i, low, n):
        half, lanes, mid = self.half, self.lanes, self.mid
        view = lambda slab, lane: c_ref[i, pl.ds(low, n), slab, :, lane].reshape(n * self.block, -1)
        return [
            view(slice(0, half), slice(mid, lanes)),
            view(slice(1, half + 1), slice(0, lanes)),
            view(slice(2, half + 2), slice(0, mid)),
        ]

    def layer(self, index, sources, e_ref, o_ref, m_ref, w_ref, b_ref, extent):
        depth = self.lanes * 2 * len(sources)
        bias = b_ref[pl.ds(index, 1), :]
        low, n_all, shift = self.reach(extent)
        count = -(-n_all // CHUNK)
        edges = [n_all * k // count for k in range(count + 1)]
        for spare, (begin, end) in enumerate(zip(edges, edges[1:])):
            n = end - begin
            spare %= 2
            size = n * self.block
            for i in range(4):
                lhs = sum([self.taps(c_ref, i, low + begin, n) for c_ref in sources], [])
                m_ref[spare, i, pl.ds(0, size)] = jnp.dot(
                    jnp.concatenate(lhs, 1),
                    w_ref[index, i, pl.ds(0, depth), :],
                    preferred_element_type=F32,
                )
            m = [m_ref[spare, i, pl.ds(0, size)] for i in range(4)]
            base = m[1] + bias
            upper = jnp.maximum(base + (m[0] + m[2]), 0.0)
            lower = jnp.maximum(base - (m[2] + m[3]), 0.0)
            for q in range(n):
                p = low - EDGE + begin + q
                for k, value in enumerate((upper, lower)):
                    y = 2 * p + shift + k
                    row = value[q * self.block : (q + 1) * self.block]
                    if y < 0 or y >= self.strip:
                        spot = self.first_row + y
                        row = row * jnp.where((spot >= 0) & (spot < self.all_rows), 1.0, 0.0).astype(F32)
                    self.keep(o_ref if y % 2 else e_ref, y // 2, row)

    def logits(self, e_ref, o_ref, rw_ref, t_ref, out_ref, at):
        pairs, block, cols = self.pairs, self.block, self.cols
        lane = lax.broadcasted_iota(jnp.int32, (block, 2 * cols), 1)
        spot = self.column(lax.broadcasted_iota(jnp.int32, (block, 2 * cols), 0) + (lane // cols) * block)
        back = (spot == lane % cols).astype(F32).astype(BF)
        for k, ref in enumerate((e_ref, o_ref)):
            final = ref[pl.ds(EDGE, pairs), pl.ds(1, self.half)].reshape(pairs * block, self.lanes)
            value = lax.dot_general(
                rw_ref[...], final, (((1,), (1,)), ((), ())), preferred_element_type=F32
            )
            value = value[:4] + value[4:]
            value = jnp.concatenate([value, jnp.zeros_like(value)], 0)
            value = jnp.concatenate([value[:, p * block : (p + 1) * block] for p in range(pairs)], 0)
            high = value.astype(BF)
            rest = value - high.astype(F32)
            next_part = rest.astype(BF)
            stacked = jnp.concatenate([high, next_part, (rest - next_part.astype(F32)).astype(BF)], 0)
            value = jnp.dot(stacked, back, preferred_element_type=F32)
            n = pairs * 8
            value = value[:n] + value[n : 2 * n] + value[2 * n :]
            t_ref[0] = value[:, :cols]
            t_ref[1] = value[:, cols:]
            for r in range(2):
                line = t_ref[0, pl.ds(r, pairs, stride=8), :] + t_ref[1, pl.ds(2 + r, pairs, stride=8), :]
                out_ref[at + r, pl.ds(k, pairs, stride=2), :] = line


def first_kernel(cfg, own_ref, w_ref, ws_ref, b_ref, e0_ref, o0_ref, e2_ref, o2_ref, c_ref, f_ref, m_ref):
    s = Strip(cfg, ws_ref.shape[1])
    s.features([own_ref[kind, r] for r in range(4) for kind in range(2)], f_ref)
    s.begin(f_ref.at[0], ws_ref, e0_ref, o0_ref, s.layers)
    for layer in range(s.layers):
        extent = 2 * s.layers - 1 - layer
        s.transform(e0_ref, o0_ref, c_ref, extent)
        s.layer(layer, (c_ref,), e0_ref, o0_ref, m_ref, w_ref, b_ref, extent)
    s.begin(f_ref.at[1], ws_ref, e2_ref, o2_ref, (s.layers + 1) // 2)


def second_kernel(
    cfg, next_ref, e0_ref, o0_ref, e2_ref, o2_ref, w_ref, ws_ref, b_ref, rw_ref, out_ref,
    e_ref, o_ref, eb_ref, ob_ref, c_ref, side_ref, f_ref, m_ref, t_ref,
):
    s = Strip(cfg, ws_ref.shape[1])
    s.features([next_ref[kind, r] for r in range(2) for kind in range(2)], f_ref)
    s.begin(f_ref.at[0], ws_ref, e_ref, o_ref, s.layers)
    for layer in range(s.layers):
        extent = 2 * s.layers - 1 - layer
        s.transform(e_ref, o_ref, c_ref, extent)
        s.layer(layer, (c_ref,), e_ref, o_ref, m_ref, w_ref, b_ref, extent)
    s.logits(e0_ref, o0_ref, rw_ref, t_ref, out_ref, 0)
    lane_id = lax.broadcasted_iota(jnp.int32, (SUB, s.lanes), 1)
    is_next = (lane_id % s.mid) < s.mid // 2
    reach = (s.layers + 1) // 2
    for source, ref in ((e0_ref, e_ref), (o0_ref, o_ref)):
        for slot in range(EDGE - reach, EDGE + s.pairs + reach):
            after = jnp.where(s.has_next, ref[slot].astype(F32), 0.0)
            ref[slot] = jnp.where(is_next[None], after, source[slot].astype(F32)).astype(BF)
    sources = (e2_ref, o2_ref)
    side = (e_ref, o_ref)
    for layer in range(s.layers):
        extent = s.layers - 1 - layer
        s.transform(*sources, c_ref, extent)
        s.transform(*side, side_ref, extent)
        sources = (eb_ref, ob_ref)
        s.layer(layer, (c_ref, side_ref), *sources, m_ref, w_ref, b_ref, extent)
    s.logits(*sources, rw_ref, t_ref, out_ref, 2)


def row_buffer(cfg, lanes):
    return (cfg[2] // 2 + 2 * EDGE, cfg[3] // SUB // 2 + 2, SUB, lanes)


def scratch(cfg, lanes, windows):
    rows = cfg[2] + 2 * HALO
    block = cfg[3] // 2
    return (
        pltpu.VMEM((windows, 16 * rows, cfg[3]), F32),
        pltpu.VMEM((2, 4, CHUNK * block, lanes), F32),
    )


def first_half(cfg, own, weights):
    lanes = weights[1].shape[1]
    buffer = row_buffer(cfg, lanes)
    vmem = pl.BlockSpec(memory_space=pltpu.VMEM)
    return pl.pallas_call(
        functools.partial(first_kernel, cfg),
        out_shape=(jax.ShapeDtypeStruct(buffer, BF),) * 4,
        in_specs=[vmem] * 4,
        out_specs=(vmem,) * 4,
        scratch_shapes=[pltpu.VMEM((4,) + buffer, BF), *scratch(cfg, lanes, 2)],
        compiler_params=pltpu.CompilerParams(vmem_limit_bytes=30 << 20),
        cost_estimate=pl.CostEstimate(flops=2_500_000_000, bytes_accessed=20_000_000, transcendentals=0),
        name="first",
    )(own, *weights[:3])


def second_half(cfg, following, held, weights):
    lanes = weights[1].shape[1]
    buffer = row_buffer(cfg, lanes)
    vmem = pl.BlockSpec(memory_space=pltpu.VMEM)
    return pl.pallas_call(
        functools.partial(second_kernel, cfg),
        out_shape=jax.ShapeDtypeStruct((4, cfg[2], cfg[3]), F32),
        in_specs=[vmem] * 9,
        out_specs=vmem,
        scratch_shapes=[pltpu.VMEM(buffer, BF)] * 4
        + [pltpu.VMEM((4,) + buffer, BF)] * 2
        + [*scratch(cfg, lanes, 1), pltpu.VMEM((2, cfg[2] // 2 * 8, cfg[3]), F32)],
        compiler_params=pltpu.CompilerParams(vmem_limit_bytes=40 << 20),
        name="second",
    )(following, *held, *weights)


def per_device(sizes, events, soft_info, embed, soft_gain, conv_weights, conv_bias, readout_weight):
    n_space, n_tm, n_chan = sizes
    rounds, tile, cols = events.shape
    layers = conv_weights.shape[0]
    strip = tile // n_chan
    packed = pack(
        n_chan,
        events,
        soft_info,
        (conv_weights, embed, soft_gain[None], conv_bias, readout_weight[None]),
    )
    both, edge = packed[:2]
    if n_chan == 2 and strip >= HALO:
        chain = []
        for s in range(n_space):
            for c in range(2):
                to = s + 1 - 2 * c
                spot = (to, c) if 0 <= to < n_space else (s, 1 - c)
                chain.append((s * 2 + c, spot[0] * 2 + spot[1]))
        up = down = lax.ppermute(edge, ("space", "chan"), chain)
    else:
        ring = lambda step: [(s, (s + step) % n_space) for s in range(n_space)]
        up = lax.ppermute(both[:, :, tile - HALO :], "space", ring(1))
        down = lax.ppermute(both[:, :, :HALO], "space", ring(-1))
    weights = prepare(*packed[2:])
    own, send = cut_window(n_chan, both, up, down)
    following = lax.ppermute(send, "tm", [(t, (t - 1) % n_tm) for t in range(n_tm)])
    cfg = (layers, tile, strip, cols, n_space, n_tm, n_chan)
    held = first_half(cfg, own, weights)
    mine = second_half(cfg, following, held, weights)
    parts = [mine]
    for step in range(1, n_chan):
        parts.append(lax.ppermute(mine, "chan", [(c, (c - step) % n_chan) for c in range(n_chan)]))
    chan = lax.axis_index("chan")
    ordered = [lax.select_n((c - chan) % n_chan, *parts) for c in range(n_chan)]
    return jnp.concatenate(ordered, 1)


def solution(mesh):
    split = P(("parts", "tm"), "space", None)
    sizes = tuple(mesh.shape[axis] for axis in ("space", "tm", "chan"))
    return jax.shard_map(
        functools.partial(per_device, sizes),
        mesh=mesh,
        in_specs=(split, split, P(), P(), P(), P(), P()),
        out_specs=split,
        check_vma=False,
    )
```

```python
import functools

import jax
import jax.numpy as jnp
from jax import lax
from jax.experimental import pallas as pl
from jax.experimental.pallas import tpu as pltpu
from jax.sharding import PartitionSpec as P

HALO = 8
SUB = 16
EDGE = 4
CHUNK = 13
BF = jnp.bfloat16
F32 = jnp.float32


def pack_kernel(n_chan, *refs):
    ev_hbm, soft_hbm = refs[:2]
    small_in, small_out = refs[2:7], refs[9:14]
    both_ref, edge_ref = refs[7:9]
    ev_ref, soft_ref, sems = refs[14:]
    copies = [
        pltpu.make_async_copy(source, target, sems.at[k])
        for k, (source, target) in enumerate(
            zip((ev_hbm, soft_hbm) + small_in, (ev_ref, soft_ref) + small_out)
        )
    ]
    for copy in copies:
        copy.start()
    copies[0].wait()
    copies[1].wait()
    rounds, tile, _ = ev_ref.shape
    lower = lax.axis_index("chan") < n_chan - 1
    for r in range(rounds):
        for kind, value in enumerate((ev_ref[r].astype(F32), soft_ref[r].astype(F32))):
            both_ref[kind, r] = value.astype(BF)
            edge_ref[kind, r] = jnp.where(lower, value[tile - HALO :], value[:HALO]).astype(BF)
    for copy in copies[2:]:
        copy.wait()


def pack(n_chan, events, soft_info, small):
    rounds, tile, cols = events.shape
    vmem = pl.BlockSpec(memory_space=pltpu.VMEM)
    outs = [
        jax.ShapeDtypeStruct((2, rounds, tile, cols), BF),
        jax.ShapeDtypeStruct((2, rounds, HALO, cols), BF),
    ] + [jax.ShapeDtypeStruct(x.shape, x.dtype) for x in small]
    return pl.pallas_call(
        functools.partial(pack_kernel, n_chan),
        out_shape=outs,
        in_specs=[pl.BlockSpec(memory_space=pltpu.HBM)] * 7,
        out_specs=[vmem] * len(outs),
        scratch_shapes=[
            pltpu.VMEM(events.shape, jnp.int32),
            pltpu.VMEM(soft_info.shape, BF),
            pltpu.SemaphoreType.DMA((7,)),
        ],
        compiler_params=pltpu.CompilerParams(vmem_limit_bytes=8 << 20),
        name="pack",
    )(*[pltpu.with_memory_space_constraint(x, pltpu.HBM) for x in (events, soft_info, *small)])


def open_weights(ch, embed_ref, gain_ref, wc_ref, wt_ref):
    table = jnp.concatenate([embed_ref[...], gain_ref[...], jnp.zeros((3, ch), F32)], 0)
    high = table.astype(BF)
    table = jnp.concatenate([high.astype(F32), table - high.astype(F32)], 0).astype(BF)
    zero = jnp.zeros((8, 2 * ch), F32)
    pieces = {}
    for dy in range(3):
        for dx in range(3):
            made = []
            for dr in range(3):
                tap = wt_ref[pl.ds(dr * 9 + dy * 3 + dx, ch, stride=27), :].astype(BF)
                value = jnp.dot(table, tap, preferred_element_type=F32)
                made.append(value[:8] + value[8:])
            for r in range(2):
                pieces[dy, dx, r] = jnp.concatenate([made[r + 1], made[r]], 1)
    for a in range(4):
        for j in range(4):
            rows = [
                jnp.concatenate([pieces.get((j - yp, a - xp, r), zero) for yp in range(2) for xp in range(2)], 1)
                for r in range(2)
            ]
            wc_ref[pl.ds((a * 4 + j) * 16, 16), :] = jnp.concatenate(rows, 0).astype(BF)


def prep_kernel(layers, ch, w_ref, embed_ref, gain_ref, bias_ref, read_ref, wout_ref, wc_ref, bout_ref, rw_ref, wt_ref):
    lanes = 4 * ch
    taps = 27
    zero_half = jnp.zeros((ch, ch), F32)
    zero_block = jnp.zeros((2 * ch, 2 * ch), BF)
    for layer in range(layers):
        wt_ref[...] = w_ref[layer].astype(F32).T
        if layer == 0:
            open_weights(ch, embed_ref, gain_ref, wc_ref, wt_ref)
        for dx in range(3):
            sets = []
            for dr in range(3):
                g = [wt_ref[pl.ds(dr * 9 + dy * 3 + dx, ch, stride=taps), :] for dy in range(3)]
                outer = (g[0] + g[2]) * 0.5
                inner = g[1] * 0.5
                sets.append((g[0], outer + inner, outer - inner, g[2]))
            for i in range(4):
                own = jnp.concatenate(
                    [
                        jnp.concatenate([sets[1][i], sets[0][i]], 1),
                        jnp.concatenate([sets[2][i], sets[1][i]], 1),
                    ],
                    0,
                ).astype(BF)
                side = jnp.concatenate(
                    [
                        jnp.concatenate([zero_half, sets[2][i]], 1),
                        jnp.concatenate([sets[0][i], zero_half], 1),
                    ],
                    0,
                ).astype(BF)
                for b in range(2):
                    a = dx + b
                    if layer > 0:
                        wout_ref[layer, i, pl.ds(a * 2 * ch, 2 * ch), pl.ds(b * 2 * ch, 2 * ch)] = own
                    wout_ref[layer, i, pl.ds(lanes * 2 + a * 2 * ch, 2 * ch), pl.ds(b * 2 * ch, 2 * ch)] = side
        for i in range(4):
            for base in (0, lanes * 2)[layer == 0 :]:
                wout_ref[layer, i, pl.ds(base + 6 * ch, 2 * ch), pl.ds(0, 2 * ch)] = zero_block
                wout_ref[layer, i, pl.ds(base, 2 * ch), pl.ds(2 * ch, 2 * ch)] = zero_block
        bout_ref[pl.ds(layer, 1), :] = jnp.concatenate([bias_ref[pl.ds(layer, 1), :]] * 4, 1)
    read = jnp.concatenate([read_ref[...]] * 4, 1)
    high = read.astype(BF).astype(F32)
    row = lax.broadcasted_iota(jnp.int32, (8, lanes), 0)
    read = jnp.where(row < 4, jnp.broadcast_to(high, (8, lanes)), jnp.broadcast_to(read - high, (8, lanes)))
    rw_ref[...] = jnp.where(row % 4 == lax.broadcasted_iota(jnp.int32, (8, lanes), 1) // ch, read, 0.0).astype(BF)


def prepare(conv_weights, embed, soft_gain, conv_bias, readout_weight):
    layers, ch, depth = conv_weights.shape
    vmem = pl.BlockSpec(memory_space=pltpu.VMEM)
    return pl.pallas_call(
        functools.partial(prep_kernel, layers, ch),
        out_shape=(
            jax.ShapeDtypeStruct((layers, 4, 16 * ch, 4 * ch), BF),
            jax.ShapeDtypeStruct((256, 8 * ch), BF),
            jax.ShapeDtypeStruct((8, 4 * ch), F32),
            jax.ShapeDtypeStruct((8, 4 * ch), BF),
        ),
        in_specs=[vmem] * 5,
        out_specs=(vmem,) * 4,
        scratch_shapes=[pltpu.VMEM((depth, ch), F32)],
        compiler_params=pltpu.CompilerParams(vmem_limit_bytes=20 << 20),
        cost_estimate=pl.CostEstimate(flops=0, bytes_accessed=20_000_000, transcendentals=0),
        name="prepare",
    )(conv_weights, embed, soft_gain, conv_bias, readout_weight)


def window_kernel(n_chan, both_ref, up_ref, down_ref, own_ref, send_ref, d_ref):
    _, rounds, tile, _ = both_ref.shape
    strip = tile // n_chan
    start = lax.axis_index("chan") * strip
    if strip % 8 == 0:
        start = pl.multiple_of(start, 8)
    for r in range(rounds):
        for kind in range(2):
            slot = r * 2 + kind
            d_ref[slot, pl.ds(0, HALO), :] = up_ref[kind, r].astype(F32)
            d_ref[slot, pl.ds(HALO, tile), :] = both_ref[kind, r].astype(F32)
            d_ref[slot, pl.ds(HALO + tile, HALO), :] = down_ref[kind, r].astype(F32)
            value = d_ref[slot, pl.ds(start, strip + 2 * HALO), :].astype(BF)
            own_ref[kind, r] = value
            if r < rounds // 2:
                send_ref[kind, r] = value


def cut_window(n_chan, both, up, down):
    kinds, rounds, tile, cols = both.shape
    rows = tile // n_chan + 2 * HALO
    vmem = pl.BlockSpec(memory_space=pltpu.VMEM)
    return pl.pallas_call(
        functools.partial(window_kernel, n_chan),
        out_shape=(
            jax.ShapeDtypeStruct((kinds, rounds, rows, cols), BF),
            jax.ShapeDtypeStruct((kinds, rounds // 2, rows, cols), BF),
        ),
        in_specs=[vmem] * 3,
        out_specs=(vmem,) * 2,
        scratch_shapes=[pltpu.VMEM((kinds * rounds, tile + 2 * HALO, cols), F32)],
        compiler_params=pltpu.CompilerParams(vmem_limit_bytes=8 << 20),
        name="window",
    )(both, up, down)


class Strip:
    def __init__(self, cfg, lanes):
        self.layers, tile, strip, self.cols, n_space, n_tm, n_chan = cfg
        self.strip, self.pairs = strip, strip // 2
        self.rows = strip + 2 * HALO
        self.slabs = self.cols // SUB
        self.half = self.slabs // 2
        self.block = self.half * SUB
        self.lanes, self.mid = lanes, lanes // 2
        self.first_row = (lax.axis_index("space") * n_chan + lax.axis_index("chan")) * strip
        self.all_rows = n_space * tile
        self.has_next = lax.axis_index("tm") < n_tm - 1
        self.sub_row = lax.broadcasted_iota(jnp.int32, (SUB, self.mid), 0)

    def column(self, lane):
        q = lane // SUB
        return (lane % SUB) * self.slabs + 2 * (q % self.half) + q // self.half

    def features(self, arrays, f_ref):
        cols, rows, block = self.cols, self.rows, self.block
        shape = (2 * cols, 4 * cols)
        source = lax.broadcasted_iota(jnp.int32, shape, 0)
        lane = lax.broadcasted_iota(jnp.int32, shape, 1)
        inner = lane % block
        wanted = (inner % SUB) * self.slabs + 2 * (inner // SUB) + lane // cols - 1
        select = (source % cols == wanted) & (source // cols == lane // block % 2)
        stacked = jnp.concatenate(arrays, 0)
        wide = jnp.concatenate(arrays, 0).astype(F32)
        later = pltpu.roll(wide, wide.shape[0] - 2, 0).astype(BF)
        gathered = jnp.dot(
            jnp.concatenate([stacked, later], 1), select.astype(F32).astype(BF), preferred_element_type=F32
        )
        lane = lax.broadcasted_iota(jnp.int32, (rows, cols), 1)
        row_id = lax.broadcasted_iota(jnp.int32, (rows, cols), 0) - HALO + self.first_row + 2 * (lane // block)
        inner = lane % block
        column = (inner % SUB) * self.slabs + 2 * (inner // SUB)
        blank = jnp.zeros((rows, cols), F32)
        for a in range(4):
            x = column + (a - 1)
            inside = (row_id >= 0) & (row_id < self.all_rows) & (x >= 0) & (x < cols)
            base = jnp.where(inside, 2.0 * ((row_id + a + 1) % 2).astype(F32), -8.0)
            for slot in range(0, len(arrays), 2):
                code = base + gathered[slot * rows : (slot + 1) * rows, a * cols : (a + 1) * cols]
                signal = gathered[(slot + 1) * rows : (slot + 2) * rows, a * cols : (a + 1) * cols]
                feats = [jnp.where(code == float(k), 1.0, 0.0) for k in range(4)]
                feats += [jnp.where(inside, signal, 0.0), blank, blank, blank]
                for k, feat in enumerate(feats):
                    f_ref[slot // 4, a, pl.ds((slot // 2 % 2 * 8 + k) * rows, rows), :] = feat

    def opening(self, f_ref, wc_ref, open_ref, extent):
        low, n_all, shift = self.reach(extent)
        for q in range(0, n_all, 2):
            at = 2 * (low - EDGE + q) + shift - 1 + HALO
            feats = [f_ref[a, pl.ds(at + j, 16, stride=self.rows), :] for a in range(4) for j in range(4)]
            value = lax.dot_general(
                jnp.concatenate(feats, 0).astype(BF),
                wc_ref[...],
                (((0,), (0,)), ((), ())),
                preferred_element_type=F32,
            )
            for k in range(2):
                open_ref[k, pl.ds(q * self.block, 2 * self.block), :] = value[:, k * self.lanes : (k + 1) * self.lanes]

    def keep(self, ref, pair, value):
        half, block, mid = self.half, self.block, self.mid
        slot = pair + EDGE
        ref[slot, pl.ds(1, half)] = value.reshape(half, SUB, self.lanes).astype(BF)
        last = pltpu.roll(value[block - SUB :, mid:], 1, 0)
        ref[slot, 0, :, mid:] = jnp.where(self.sub_row == 0, 0.0, last).astype(BF)
        head = pltpu.roll(value[:SUB, :mid], SUB - 1, 0)
        ref[slot, half + 1, :, :mid] = jnp.where(self.sub_row == SUB - 1, 0.0, head).astype(BF)

    def reach(self, extent):
        return EDGE - (extent + 1) // 2, self.pairs + extent, extent % 2

    def transform(self, e_ref, o_ref, c_ref, extent):
        half, lanes, mid = self.half, self.lanes, self.mid
        low, n, shift = self.reach(extent)
        for slab, lane in (
            (slice(1, half + 1), slice(0, lanes)),
            (slice(0, 1), slice(mid, lanes)),
            (slice(half + 1, half + 2), slice(0, mid)),
        ):
            view = lambda ref, step: ref[pl.ds(low + step, n), slab, :, lane]
            if shift:
                d = (view(e_ref, 0), view(o_ref, 0), view(e_ref, 1), view(o_ref, 1))
            else:
                d = (view(o_ref, -1), view(e_ref, 0), view(o_ref, 0), view(e_ref, 1))
            for i, value in enumerate((d[0] - d[2], d[1] + d[2], d[2] - d[1], d[1] - d[3])):
                c_ref[i, pl.ds(low, n), slab, :, lane] = value

    def taps(self, c_ref, i, low, n):
        half, lanes, mid = self.half, self.lanes, self.mid
        view = lambda slab, lane: c_ref[i, pl.ds(low, n), slab, :, lane].reshape(n * self.block, -1)
        return [
            view(slice(0, half), slice(mid, lanes)),
            view(slice(1, half + 1), slice(0, lanes)),
            view(slice(2, half + 2), slice(0, mid)),
        ]

    def layer(self, index, sources, e_ref, o_ref, m_ref, w_ref, b_ref, extent, open_ref=None):
        bias = b_ref[pl.ds(index, 1), :]
        low, n_all, shift = self.reach(extent)
        count = -(-n_all // CHUNK)
        edges = [n_all * k // count for k in range(count + 1)]
        for spare, (begin, end) in enumerate(zip(edges, edges[1:])):
            n = end - begin
            spare %= 2
            size = n * self.block
            upper = lower = bias
            if open_ref is not None:
                at = pl.ds(begin * self.block, size)
                upper, lower = open_ref[0, at, :] + bias, open_ref[1, at, :] + bias
            if sources:
                first = sources[0][1]
                depth = self.lanes * 2 * len(sources)
                for i in range(4):
                    lhs = sum([self.taps(c_ref, i, low + begin, n) for c_ref, _ in sources], [])
                    m_ref[spare, i, pl.ds(0, size)] = jnp.dot(
                        jnp.concatenate(lhs, 1),
                        w_ref[index, i, pl.ds(first, depth), :],
                        preferred_element_type=F32,
                    )
                m = [m_ref[spare, i, pl.ds(0, size)] for i in range(4)]
                upper = upper + m[1] + (m[0] + m[2])
                lower = lower + m[1] - (m[2] + m[3])
            upper, lower = jnp.maximum(upper, 0.0), jnp.maximum(lower, 0.0)
            for q in range(n):
                p = low - EDGE + begin + q
                for k, value in enumerate((upper, lower)):
                    y = 2 * p + shift + k
                    row = value[q * self.block : (q + 1) * self.block]
                    if y < 0 or y >= self.strip:
                        spot = self.first_row + y
                        row = row * jnp.where((spot >= 0) & (spot < self.all_rows), 1.0, 0.0).astype(F32)
                    self.keep(o_ref if y % 2 else e_ref, y // 2, row)

    def logits(self, e_ref, o_ref, rw_ref, t_ref, out_ref, at):
        pairs, block, cols = self.pairs, self.block, self.cols
        lane = lax.broadcasted_iota(jnp.int32, (block, 2 * cols), 1)
        spot = self.column(lax.broadcasted_iota(jnp.int32, (block, 2 * cols), 0) + (lane // cols) * block)
        back = (spot == lane % cols).astype(F32).astype(BF)
        for k, ref in enumerate((e_ref, o_ref)):
            final = ref[pl.ds(EDGE, pairs), pl.ds(1, self.half)].reshape(pairs * block, self.lanes)
            value = lax.dot_general(
                rw_ref[...], final, (((1,), (1,)), ((), ())), preferred_element_type=F32
            )
            value = value[:4] + value[4:]
            value = jnp.concatenate([value, jnp.zeros_like(value)], 0)
            value = jnp.concatenate([value[:, p * block : (p + 1) * block] for p in range(pairs)], 0)
            high = value.astype(BF)
            rest = value - high.astype(F32)
            next_part = rest.astype(BF)
            stacked = jnp.concatenate([high, next_part, (rest - next_part.astype(F32)).astype(BF)], 0)
            value = jnp.dot(stacked, back, preferred_element_type=F32)
            n = pairs * 8
            value = value[:n] + value[n : 2 * n] + value[2 * n :]
            t_ref[0] = value[:, :cols]
            t_ref[1] = value[:, cols:]
            for r in range(2):
                line = t_ref[0, pl.ds(r, pairs, stride=8), :] + t_ref[1, pl.ds(2 + r, pairs, stride=8), :]
                out_ref[at + r, pl.ds(k, pairs, stride=2), :] = line


def run_first_window(s, f_ref, wc_ref, e_ref, o_ref, c_ref, m_ref, open_ref, w_ref, b_ref):
    extent = 2 * s.layers - 1
    s.opening(f_ref, wc_ref, open_ref, extent)
    s.layer(0, (), e_ref, o_ref, m_ref, w_ref, b_ref, extent, open_ref)
    for layer in range(1, s.layers):
        extent -= 1
        s.transform(e_ref, o_ref, c_ref, extent)
        s.layer(layer, ((c_ref, 0),), e_ref, o_ref, m_ref, w_ref, b_ref, extent)


def first_kernel(cfg, own_ref, w_ref, wc_ref, b_ref, e0_ref, o0_ref, start_ref, c_ref, f_ref, m_ref, open_ref):
    s = Strip(cfg, b_ref.shape[1])
    s.features([own_ref[kind, r] for r in range(4) for kind in range(2)], f_ref)
    run_first_window(s, f_ref.at[0], wc_ref, e0_ref, o0_ref, c_ref, m_ref, open_ref, w_ref, b_ref)
    s.opening(f_ref.at[1], wc_ref, start_ref, s.layers - 1)


def second_kernel(
    cfg, next_ref, e0_ref, o0_ref, start_ref, w_ref, wc_ref, b_ref, rw_ref, out_ref,
    e_ref, o_ref, eb_ref, ob_ref, c_ref, side_ref, f_ref, m_ref, open_ref, t_ref,
):
    s = Strip(cfg, b_ref.shape[1])
    s.features([next_ref[kind, r] for r in range(2) for kind in range(2)], f_ref)
    run_first_window(s, f_ref.at[0], wc_ref, e_ref, o_ref, c_ref, m_ref, open_ref, w_ref, b_ref)
    s.logits(e0_ref, o0_ref, rw_ref, t_ref, out_ref, 0)
    lane_id = lax.broadcasted_iota(jnp.int32, (SUB, s.lanes), 1)
    is_next = (lane_id % s.mid) < s.mid // 2
    reach = (s.layers + 1) // 2
    for source, ref in ((e0_ref, e_ref), (o0_ref, o_ref)):
        for slot in range(EDGE - reach, EDGE + s.pairs + reach):
            after = jnp.where(s.has_next, ref[slot].astype(F32), 0.0)
            ref[slot] = jnp.where(is_next[None], after, source[slot].astype(F32)).astype(BF)
    final = (eb_ref, ob_ref)
    for layer in range(s.layers):
        extent = s.layers - 1 - layer
        s.transform(e_ref, o_ref, side_ref, extent)
        if layer == 0:
            sources = ((side_ref, 2 * s.lanes),)
        else:
            s.transform(*final, c_ref, extent)
            sources = ((c_ref, 0), (side_ref, 2 * s.lanes))
        s.layer(layer, sources, *final, m_ref, w_ref, b_ref, extent, None if layer else start_ref)
    s.logits(*final, rw_ref, t_ref, out_ref, 2)


def row_buffer(cfg, lanes):
    return (cfg[2] // 2 + 2 * EDGE, cfg[3] // SUB // 2 + 2, SUB, lanes)


def open_buffer(cfg, lanes, extent):
    pairs = cfg[2] // 2 + extent
    return (2, (pairs + pairs % 2) * cfg[3] // 2, lanes)


def scratch(cfg, lanes, windows):
    rows = cfg[2] + 2 * HALO
    block = cfg[3] // 2
    return (
        pltpu.VMEM((windows, 4, 16 * rows, cfg[3]), F32),
        pltpu.VMEM((2, 4, CHUNK * block, lanes), F32),
        pltpu.VMEM(open_buffer(cfg, lanes, 2 * cfg[0] - 1), F32),
    )


def first_half(cfg, own, weights):
    lanes = weights[2].shape[1]
    buffer = row_buffer(cfg, lanes)
    vmem = pl.BlockSpec(memory_space=pltpu.VMEM)
    return pl.pallas_call(
        functools.partial(first_kernel, cfg),
        out_shape=(
            jax.ShapeDtypeStruct(buffer, BF),
            jax.ShapeDtypeStruct(buffer, BF),
            jax.ShapeDtypeStruct(open_buffer(cfg, lanes, cfg[0] - 1), F32),
        ),
        in_specs=[vmem] * 4,
        out_specs=(vmem,) * 3,
        scratch_shapes=[pltpu.VMEM((4,) + buffer, BF), *scratch(cfg, lanes, 2)],
        compiler_params=pltpu.CompilerParams(vmem_limit_bytes=30 << 20),
        cost_estimate=pl.CostEstimate(flops=2_500_000_000, bytes_accessed=20_000_000, transcendentals=0),
        name="first",
    )(own, *weights[:3])


def second_half(cfg, following, held, weights):
    lanes = weights[2].shape[1]
    buffer = row_buffer(cfg, lanes)
    vmem = pl.BlockSpec(memory_space=pltpu.VMEM)
    return pl.pallas_call(
        functools.partial(second_kernel, cfg),
        out_shape=jax.ShapeDtypeStruct((4, cfg[2], cfg[3]), F32),
        in_specs=[vmem] * 8,
        out_specs=vmem,
        scratch_shapes=[pltpu.VMEM(buffer, BF)] * 4
        + [pltpu.VMEM((4,) + buffer, BF)] * 2
        + [*scratch(cfg, lanes, 1), pltpu.VMEM((2, cfg[2] // 2 * 8, cfg[3]), F32)],
        compiler_params=pltpu.CompilerParams(vmem_limit_bytes=40 << 20),
        name="second",
    )(following, *held, *weights)


def per_device(sizes, events, soft_info, embed, soft_gain, conv_weights, conv_bias, readout_weight):
    n_space, n_tm, n_chan = sizes
    rounds, tile, cols = events.shape
    layers = conv_weights.shape[0]
    strip = tile // n_chan
    packed = pack(
        n_chan,
        events,
        soft_info,
        (conv_weights, embed, soft_gain[None], conv_bias, readout_weight[None]),
    )
    both, edge = packed[:2]
    if n_chan == 2 and strip >= HALO:
        chain = []
        for s in range(n_space):
            for c in range(2):
                to = s + 1 - 2 * c
                spot = (to, c) if 0 <= to < n_space else (s, 1 - c)
                chain.append((s * 2 + c, spot[0] * 2 + spot[1]))
        up = down = lax.ppermute(edge, ("space", "chan"), chain)
    else:
        ring = lambda step: [(s, (s + step) % n_space) for s in range(n_space)]
        up = lax.ppermute(both[:, :, tile - HALO :], "space", ring(1))
        down = lax.ppermute(both[:, :, :HALO], "space", ring(-1))
    weights = prepare(*packed[2:])
    own, send = cut_window(n_chan, both, up, down)
    following = lax.ppermute(send, "tm", [(t, (t - 1) % n_tm) for t in range(n_tm)])
    cfg = (layers, tile, strip, cols, n_space, n_tm, n_chan)
    held = first_half(cfg, own, weights)
    mine = second_half(cfg, following, held, weights)
    parts = [mine]
    for step in range(1, n_chan):
        parts.append(lax.ppermute(mine, "chan", [(c, (c - step) % n_chan) for c in range(n_chan)]))
    chan = lax.axis_index("chan")
    ordered = [lax.select_n((c - chan) % n_chan, *parts) for c in range(n_chan)]
    return jnp.concatenate(ordered, 1)


def solution(mesh):
    split = P(("parts", "tm"), "space", None)
    sizes = tuple(mesh.shape[axis] for axis in ("space", "tm", "chan"))
    return jax.shard_map(
        functools.partial(per_device, sizes),
        mesh=mesh,
        in_specs=(split, split, P(), P(), P(), P(), P()),
        out_specs=split,
        check_vma=False,
    )
```

```python
import functools

import jax
import jax.numpy as jnp
from jax import lax
from jax.experimental import pallas as pl
from jax.experimental.pallas import tpu as pltpu
from jax.sharding import PartitionSpec as P

HALO = 8
SUB = 16
EDGE = 4
CHUNK = 13
BF = jnp.bfloat16
F32 = jnp.float32


def quotient(value, by):
    return lax.shift_right_logical(value, by.bit_length() - 1) if by & (by - 1) == 0 else value // by


def remainder(value, by):
    return value & (by - 1) if by & (by - 1) == 0 else value % by


def pack_kernel(n_chan, *refs):
    ev_hbm, soft_hbm = refs[:2]
    small_in, small_out = refs[2:7], refs[9:14]
    both_ref, edge_ref = refs[7:9]
    ev_ref, soft_ref, sems = refs[14:]
    copies = [
        pltpu.make_async_copy(source, target, sems.at[k])
        for k, (source, target) in enumerate(
            zip((ev_hbm, soft_hbm) + small_in, (ev_ref, soft_ref) + small_out)
        )
    ]
    for copy in copies:
        copy.start()
    copies[0].wait()
    copies[1].wait()
    rounds, tile, _ = ev_ref.shape
    lower = lax.axis_index("chan") < n_chan - 1
    for r in range(rounds):
        for kind, value in enumerate((ev_ref[r].astype(F32), soft_ref[r].astype(F32))):
            both_ref[kind, r] = value.astype(BF)
            edge_ref[kind, r] = jnp.where(lower, value[tile - HALO :], value[:HALO]).astype(BF)
    for copy in copies[2:]:
        copy.wait()


def pack(n_chan, events, soft_info, small):
    rounds, tile, cols = events.shape
    vmem = pl.BlockSpec(memory_space=pltpu.VMEM)
    outs = [
        jax.ShapeDtypeStruct((2, rounds, tile, cols), BF),
        jax.ShapeDtypeStruct((2, rounds, HALO, cols), BF),
    ] + [jax.ShapeDtypeStruct(x.shape, x.dtype) for x in small]
    return pl.pallas_call(
        functools.partial(pack_kernel, n_chan),
        out_shape=outs,
        in_specs=[pl.BlockSpec(memory_space=pltpu.HBM)] * 7,
        out_specs=[vmem] * len(outs),
        scratch_shapes=[
            pltpu.VMEM(events.shape, jnp.int32),
            pltpu.VMEM(soft_info.shape, BF),
            pltpu.SemaphoreType.DMA((7,)),
        ],
        compiler_params=pltpu.CompilerParams(vmem_limit_bytes=8 << 20),
        name="pack",
    )(*[pltpu.with_memory_space_constraint(x, pltpu.HBM) for x in (events, soft_info, *small)])


def open_weights(ch, embed_ref, gain_ref, wc_ref, wt_ref):
    table = jnp.concatenate([embed_ref[...], gain_ref[...], jnp.zeros((3, ch), F32)], 0)
    high = table.astype(BF)
    table = jnp.concatenate([high.astype(F32), table - high.astype(F32)], 0).astype(BF)
    zero = jnp.zeros((8, 2 * ch), F32)
    pieces = {}
    for dy in range(3):
        for dx in range(3):
            made = []
            for dr in range(3):
                tap = wt_ref[pl.ds(dr * 9 + dy * 3 + dx, ch, stride=27), :].astype(BF)
                value = jnp.dot(table, tap, preferred_element_type=F32)
                made.append(value[:8] + value[8:])
            for r in range(2):
                pieces[dy, dx, r] = jnp.concatenate([made[r + 1], made[r]], 1)
    blocks = []
    for a in range(4):
        for j in range(4):
            rows = [
                jnp.concatenate([pieces.get((j - yp, a - xp, r), zero) for yp in range(2) for xp in range(2)], 1)
                for r in range(2)
            ]
            blocks.append(jnp.concatenate(rows, 0))
    shape = (wc_ref.shape[0], 256)
    row = lax.broadcasted_iota(jnp.int32, shape, 0)
    inner = remainder(row, 8)
    group = quotient(row, 8)
    a = (group >= 5).astype(jnp.int32) + (group >= 10).astype(jnp.int32) + (group >= 15).astype(jnp.int32)
    old = (a * 8 + inner) * 8 + group - 5 * a
    order = (old == lax.broadcasted_iota(jnp.int32, shape, 1)).astype(F32).astype(BF)
    wide = jnp.concatenate(blocks, 0).astype(BF)
    wc_ref[...] = jnp.dot(order, wide, preferred_element_type=F32).astype(BF)


def prep_kernel(layers, ch, w_ref, embed_ref, gain_ref, bias_ref, read_ref, wout_ref, wc_ref, bout_ref, rw_ref, wt_ref):
    lanes = 4 * ch
    taps = 27
    zero_half = jnp.zeros((ch, ch), F32)
    zero_block = jnp.zeros((2 * ch, 2 * ch), BF)
    for layer in range(layers):
        wt_ref[...] = w_ref[layer].astype(F32).T
        if layer == 0:
            open_weights(ch, embed_ref, gain_ref, wc_ref, wt_ref)
        for dx in range(3):
            sets = []
            for dr in range(3):
                g = [wt_ref[pl.ds(dr * 9 + dy * 3 + dx, ch, stride=taps), :] for dy in range(3)]
                outer = (g[0] + g[2]) * 0.5
                inner = g[1] * 0.5
                sets.append((g[0], outer + inner, outer - inner, g[2]))
            for i in range(4):
                own = jnp.concatenate(
                    [
                        jnp.concatenate([sets[1][i], sets[0][i]], 1),
                        jnp.concatenate([sets[2][i], sets[1][i]], 1),
                    ],
                    0,
                ).astype(BF)
                side = jnp.concatenate(
                    [
                        jnp.concatenate([zero_half, sets[2][i]], 1),
                        jnp.concatenate([sets[0][i], zero_half], 1),
                    ],
                    0,
                ).astype(BF)
                for b in range(2):
                    a = dx + b
                    if layer > 0:
                        wout_ref[layer, i, pl.ds(a * 2 * ch, 2 * ch), pl.ds(b * 2 * ch, 2 * ch)] = own
                    wout_ref[layer, i, pl.ds(lanes * 2 + a * 2 * ch, 2 * ch), pl.ds(b * 2 * ch, 2 * ch)] = side
        for i in range(4):
            for base in (0, lanes * 2)[layer == 0 :]:
                wout_ref[layer, i, pl.ds(base + 6 * ch, 2 * ch), pl.ds(0, 2 * ch)] = zero_block
                wout_ref[layer, i, pl.ds(base, 2 * ch), pl.ds(2 * ch, 2 * ch)] = zero_block
        bout_ref[pl.ds(layer, 1), :] = jnp.concatenate([bias_ref[pl.ds(layer, 1), :]] * 4, 1)
    read = jnp.concatenate([read_ref[...]] * 4, 1)
    high = read.astype(BF).astype(F32)
    row = lax.broadcasted_iota(jnp.int32, (8, lanes), 0)
    read = jnp.where(row < 4, jnp.broadcast_to(high, (8, lanes)), jnp.broadcast_to(read - high, (8, lanes)))
    rw_ref[...] = jnp.where(remainder(row, 4) == quotient(lax.broadcasted_iota(jnp.int32, (8, lanes), 1), ch), read, 0.0).astype(BF)


def prepare(conv_weights, embed, soft_gain, conv_bias, readout_weight):
    layers, ch, depth = conv_weights.shape
    vmem = pl.BlockSpec(memory_space=pltpu.VMEM)
    return pl.pallas_call(
        functools.partial(prep_kernel, layers, ch),
        out_shape=(
            jax.ShapeDtypeStruct((layers, 4, 16 * ch, 4 * ch), BF),
            jax.ShapeDtypeStruct((160, 8 * ch), BF),
            jax.ShapeDtypeStruct((8, 4 * ch), F32),
            jax.ShapeDtypeStruct((8, 4 * ch), BF),
        ),
        in_specs=[vmem] * 5,
        out_specs=(vmem,) * 4,
        scratch_shapes=[pltpu.VMEM((depth, ch), F32)],
        compiler_params=pltpu.CompilerParams(vmem_limit_bytes=20 << 20),
        cost_estimate=pl.CostEstimate(flops=0, bytes_accessed=20_000_000, transcendentals=0),
        name="prepare",
    )(conv_weights, embed, soft_gain, conv_bias, readout_weight)


def window_kernel(n_chan, both_ref, up_ref, down_ref, own_ref, send_ref, d_ref):
    _, rounds, tile, _ = both_ref.shape
    strip = tile // n_chan
    start = lax.axis_index("chan") * strip
    if strip % 8 == 0:
        start = pl.multiple_of(start, 8)
    for r in range(rounds):
        for kind in range(2):
            slot = r * 2 + kind
            d_ref[slot, pl.ds(0, HALO), :] = up_ref[kind, r].astype(F32)
            d_ref[slot, pl.ds(HALO, tile), :] = both_ref[kind, r].astype(F32)
            d_ref[slot, pl.ds(HALO + tile, HALO), :] = down_ref[kind, r].astype(F32)
            value = d_ref[slot, pl.ds(start, strip + 2 * HALO), :].astype(BF)
            own_ref[kind, r] = value
            if r < rounds // 2:
                send_ref[kind, r] = value


def cut_window(n_chan, both, up, down):
    kinds, rounds, tile, cols = both.shape
    rows = tile // n_chan + 2 * HALO
    vmem = pl.BlockSpec(memory_space=pltpu.VMEM)
    return pl.pallas_call(
        functools.partial(window_kernel, n_chan),
        out_shape=(
            jax.ShapeDtypeStruct((kinds, rounds, rows, cols), BF),
            jax.ShapeDtypeStruct((kinds, rounds // 2, rows, cols), BF),
        ),
        in_specs=[vmem] * 3,
        out_specs=(vmem,) * 2,
        scratch_shapes=[pltpu.VMEM((kinds * rounds, tile + 2 * HALO, cols), F32)],
        compiler_params=pltpu.CompilerParams(vmem_limit_bytes=8 << 20),
        name="window",
    )(both, up, down)


class Strip:
    def __init__(self, cfg, lanes):
        self.layers, tile, strip, self.cols, n_space, n_tm, n_chan = cfg
        self.strip, self.pairs = strip, strip // 2
        self.rows = strip + 2 * HALO
        self.slabs = self.cols // SUB
        self.half = self.slabs // 2
        self.block = self.half * SUB
        self.lanes, self.mid = lanes, lanes // 2
        self.first_row = (lax.axis_index("space") * n_chan + lax.axis_index("chan")) * strip
        self.all_rows = n_space * tile
        self.has_next = lax.axis_index("tm") < n_tm - 1
        self.sub_row = lax.broadcasted_iota(jnp.int32, (SUB, self.mid), 0)

    def column(self, lane):
        q = quotient(lane, SUB)
        return remainder(lane, SUB) * self.slabs + 2 * remainder(q, self.half) + quotient(q, self.half)

    def features(self, arrays, f_ref):
        cols, rows, block = self.cols, self.rows, self.block
        shape = (2 * cols, 4 * cols)
        source = lax.broadcasted_iota(jnp.int32, shape, 0)
        lane = lax.broadcasted_iota(jnp.int32, (1, 4 * cols), 1)
        inner = remainder(lane, block)
        wanted = remainder(inner, SUB) * self.slabs + 2 * quotient(inner, SUB) + quotient(lane, cols) - 1
        wanted = jnp.where((wanted >= 0) & (wanted < cols), wanted, -2 * cols)
        wanted = wanted + cols * remainder(quotient(lane, block), 2)
        select = (source == wanted).astype(F32).astype(BF)
        stacked = jnp.concatenate(arrays, 0)
        wide = stacked.astype(F32)
        later = pltpu.roll(wide, wide.shape[0] - 2, 0).astype(BF)
        gathered = jnp.dot(jnp.concatenate([stacked, later], 1), select, preferred_element_type=F32)
        lane = lax.broadcasted_iota(jnp.int32, (rows, cols), 1)
        row_id = lax.broadcasted_iota(jnp.int32, (rows, cols), 0) - HALO + self.first_row + 2 * quotient(lane, block)
        inside_rows = (row_id >= 0) & (row_id < self.all_rows)
        inner = remainder(lane, block)
        column = remainder(inner, SUB) * self.slabs + 2 * quotient(inner, SUB)
        for a in range(4):
            x = column + (a - 1)
            inside = inside_rows & (x >= 0) & (x < cols)
            base = jnp.where(inside, 2.0 * ((row_id + a + 1) & 1).astype(F32), -8.0)
            keep = jnp.where(inside, 1.0, 0.0)
            for slot in range(0, len(arrays), 2):
                code = base + gathered[slot * rows : (slot + 1) * rows, a * cols : (a + 1) * cols]
                signal = gathered[(slot + 1) * rows : (slot + 2) * rows, a * cols : (a + 1) * cols]
                feats = [jnp.where(code == float(k), 1.0, 0.0) for k in range(4)] + [signal * keep]
                for k, feat in enumerate(feats):
                    f_ref[slot // 4, a, k, pl.ds(slot // 2 % 2, rows, stride=2), :] = feat

    def opening(self, f_ref, wc_ref, open_ref, extent):
        low, n_all, shift = self.reach(extent)
        for q in range(0, n_all, 2):
            at = 2 * (low - EDGE + q) + shift - 1 + HALO
            feats = [f_ref[a, k, pl.ds(2 * at, 8), :] for a in range(4) for k in range(5)]
            value = lax.dot_general(
                jnp.concatenate(feats, 0).astype(BF),
                wc_ref[...],
                (((0,), (0,)), ((), ())),
                preferred_element_type=F32,
            )
            for k in range(2):
                open_ref[k, pl.ds(q * self.block, 2 * self.block), :] = value[:, k * self.lanes : (k + 1) * self.lanes]

    def keep(self, ref, pair, value):
        half, block, mid = self.half, self.block, self.mid
        slot = pair + EDGE
        ref[slot, pl.ds(1, half)] = value.reshape(half, SUB, self.lanes).astype(BF)
        last = pltpu.roll(value[block - SUB :, mid:], 1, 0)
        ref[slot, 0, :, mid:] = jnp.where(self.sub_row == 0, 0.0, last).astype(BF)
        head = pltpu.roll(value[:SUB, :mid], SUB - 1, 0)
        ref[slot, half + 1, :, :mid] = jnp.where(self.sub_row == SUB - 1, 0.0, head).astype(BF)

    def reach(self, extent):
        return EDGE - (extent + 1) // 2, self.pairs + extent, extent % 2

    def transform(self, e_ref, o_ref, c_ref, extent):
        half, lanes, mid = self.half, self.lanes, self.mid
        low, n, shift = self.reach(extent)
        for slab, lane in (
            (slice(1, half + 1), slice(0, lanes)),
            (slice(0, 1), slice(mid, lanes)),
            (slice(half + 1, half + 2), slice(0, mid)),
        ):
            view = lambda ref, step: ref[pl.ds(low + step, n), slab, :, lane]
            if shift:
                d = (view(e_ref, 0), view(o_ref, 0), view(e_ref, 1), view(o_ref, 1))
            else:
                d = (view(o_ref, -1), view(e_ref, 0), view(o_ref, 0), view(e_ref, 1))
            for i, value in enumerate((d[0] - d[2], d[1] + d[2], d[2] - d[1], d[1] - d[3])):
                c_ref[i, pl.ds(low, n), slab, :, lane] = value

    def taps(self, c_ref, i, low, n):
        half, lanes, mid = self.half, self.lanes, self.mid
        view = lambda slab, lane: c_ref[i, pl.ds(low, n), slab, :, lane].reshape(n * self.block, -1)
        return [
            view(slice(0, half), slice(mid, lanes)),
            view(slice(1, half + 1), slice(0, lanes)),
            view(slice(2, half + 2), slice(0, mid)),
        ]

    def layer(self, index, sources, e_ref, o_ref, m_ref, w_ref, b_ref, extent, open_ref=None):
        bias = b_ref[pl.ds(index, 1), :]
        low, n_all, shift = self.reach(extent)
        count = -(-n_all // CHUNK)
        edges = [n_all * k // count for k in range(count + 1)]
        for spare, (begin, end) in enumerate(zip(edges, edges[1:])):
            n = end - begin
            spare %= 2
            size = n * self.block
            upper = lower = bias
            if open_ref is not None:
                at = pl.ds(begin * self.block, size)
                upper, lower = open_ref[0, at, :] + bias, open_ref[1, at, :] + bias
            if sources:
                first = sources[0][1]
                depth = self.lanes * 2 * len(sources)
                for i in range(4):
                    lhs = sum([self.taps(c_ref, i, low + begin, n) for c_ref, _ in sources], [])
                    m_ref[spare, i, pl.ds(0, size)] = jnp.dot(
                        jnp.concatenate(lhs, 1),
                        w_ref[index, i, pl.ds(first, depth), :],
                        preferred_element_type=F32,
                    )
                m = [m_ref[spare, i, pl.ds(0, size)] for i in range(4)]
                upper = upper + m[1] + (m[0] + m[2])
                lower = lower + m[1] - (m[2] + m[3])
            upper, lower = jnp.maximum(upper, 0.0), jnp.maximum(lower, 0.0)
            for q in range(n):
                p = low - EDGE + begin + q
                for k, value in enumerate((upper, lower)):
                    y = 2 * p + shift + k
                    row = value[q * self.block : (q + 1) * self.block]
                    if y < 0 or y >= self.strip:
                        spot = self.first_row + y
                        row = row * jnp.where((spot >= 0) & (spot < self.all_rows), 1.0, 0.0).astype(F32)
                    self.keep(o_ref if y % 2 else e_ref, y // 2, row)

    def logits(self, e_ref, o_ref, rw_ref, t_ref, out_ref, at):
        pairs, block, cols = self.pairs, self.block, self.cols
        lane = lax.broadcasted_iota(jnp.int32, (block, 2 * cols), 1)
        spot = self.column(lax.broadcasted_iota(jnp.int32, (block, 2 * cols), 0) + quotient(lane, cols) * block)
        back = (spot == remainder(lane, cols)).astype(F32).astype(BF)
        for k, ref in enumerate((e_ref, o_ref)):
            final = ref[pl.ds(EDGE, pairs), pl.ds(1, self.half)].reshape(pairs * block, self.lanes)
            value = lax.dot_general(
                rw_ref[...], final, (((1,), (1,)), ((), ())), preferred_element_type=F32
            )
            value = value[:4] + value[4:]
            value = jnp.concatenate([value, jnp.zeros_like(value)], 0)
            value = jnp.concatenate([value[:, p * block : (p + 1) * block] for p in range(pairs)], 0)
            high = value.astype(BF)
            stacked = jnp.concatenate([high, (value - high.astype(F32)).astype(BF)], 0)
            value = jnp.dot(stacked, back, preferred_element_type=F32)
            n = pairs * 8
            value = value[:n] + value[n:]
            t_ref[0] = value[:, :cols]
            t_ref[1] = value[:, cols:]
            for r in range(2):
                line = t_ref[0, pl.ds(r, pairs, stride=8), :] + t_ref[1, pl.ds(2 + r, pairs, stride=8), :]
                out_ref[at + r, pl.ds(k, pairs, stride=2), :] = line


def run_first_window(s, f_ref, wc_ref, e_ref, o_ref, c_ref, m_ref, open_ref, w_ref, b_ref):
    extent = 2 * s.layers - 1
    s.opening(f_ref, wc_ref, open_ref, extent)
    s.layer(0, (), e_ref, o_ref, m_ref, w_ref, b_ref, extent, open_ref)
    for layer in range(1, s.layers):
        extent -= 1
        s.transform(e_ref, o_ref, c_ref, extent)
        s.layer(layer, ((c_ref, 0),), e_ref, o_ref, m_ref, w_ref, b_ref, extent)


def first_kernel(cfg, own_ref, w_ref, wc_ref, b_ref, e0_ref, o0_ref, start_ref, c_ref, f_ref, m_ref, open_ref):
    s = Strip(cfg, b_ref.shape[1])
    s.features([own_ref[kind, r] for r in range(4) for kind in range(2)], f_ref)
    run_first_window(s, f_ref.at[0], wc_ref, e0_ref, o0_ref, c_ref, m_ref, open_ref, w_ref, b_ref)
    s.opening(f_ref.at[1], wc_ref, start_ref, s.layers - 1)


def second_kernel(
    cfg, next_ref, e0_ref, o0_ref, start_ref, w_ref, wc_ref, b_ref, rw_ref, out_ref,
    e_ref, o_ref, eb_ref, ob_ref, c_ref, side_ref, f_ref, m_ref, open_ref, t_ref,
):
    s = Strip(cfg, b_ref.shape[1])
    s.features([next_ref[kind, r] for r in range(2) for kind in range(2)], f_ref)
    run_first_window(s, f_ref.at[0], wc_ref, e_ref, o_ref, c_ref, m_ref, open_ref, w_ref, b_ref)
    s.logits(e0_ref, o0_ref, rw_ref, t_ref, out_ref, 0)
    lane_id = lax.broadcasted_iota(jnp.int32, (SUB, s.lanes), 1)
    is_next = remainder(lane_id, s.mid) < s.mid // 2
    own_part = jnp.where(is_next, 0.0, 1.0).astype(BF)[None]
    next_part = jnp.where(is_next & s.has_next, 1.0, 0.0).astype(BF)[None]
    reach = (s.layers + 1) // 2
    for source, ref in ((e0_ref, e_ref), (o0_ref, o_ref)):
        for slot in range(EDGE - reach, EDGE + s.pairs + reach):
            ref[slot] = ref[slot] * next_part + source[slot] * own_part
    final = (eb_ref, ob_ref)
    for layer in range(s.layers):
        extent = s.layers - 1 - layer
        s.transform(e_ref, o_ref, side_ref, extent)
        if layer == 0:
            sources = ((side_ref, 2 * s.lanes),)
        else:
            s.transform(*final, c_ref, extent)
            sources = ((c_ref, 0), (side_ref, 2 * s.lanes))
        s.layer(layer, sources, *final, m_ref, w_ref, b_ref, extent, None if layer else start_ref)
    s.logits(*final, rw_ref, t_ref, out_ref, 2)


def row_buffer(cfg, lanes):
    return (cfg[2] // 2 + 2 * EDGE, cfg[3] // SUB // 2 + 2, SUB, lanes)


def open_buffer(cfg, lanes, extent):
    pairs = cfg[2] // 2 + extent
    return (2, (pairs + pairs % 2) * cfg[3] // 2, lanes)


def scratch(cfg, lanes, windows):
    rows = cfg[2] + 2 * HALO
    block = cfg[3] // 2
    return (
        pltpu.VMEM((windows, 4, 5, 2 * rows, cfg[3]), F32),
        pltpu.VMEM((2, 4, CHUNK * block, lanes), F32),
        pltpu.VMEM(open_buffer(cfg, lanes, 2 * cfg[0] - 1), F32),
    )


def first_half(cfg, own, weights):
    lanes = weights[2].shape[1]
    buffer = row_buffer(cfg, lanes)
    vmem = pl.BlockSpec(memory_space=pltpu.VMEM)
    return pl.pallas_call(
        functools.partial(first_kernel, cfg),
        out_shape=(
            jax.ShapeDtypeStruct(buffer, BF),
            jax.ShapeDtypeStruct(buffer, BF),
            jax.ShapeDtypeStruct(open_buffer(cfg, lanes, cfg[0] - 1), F32),
        ),
        in_specs=[vmem] * 4,
        out_specs=(vmem,) * 3,
        scratch_shapes=[pltpu.VMEM((4,) + buffer, BF), *scratch(cfg, lanes, 2)],
        compiler_params=pltpu.CompilerParams(vmem_limit_bytes=30 << 20),
        cost_estimate=pl.CostEstimate(flops=2_500_000_000, bytes_accessed=20_000_000, transcendentals=0),
        name="first",
    )(own, *weights[:3])


def second_half(cfg, following, held, weights):
    lanes = weights[2].shape[1]
    buffer = row_buffer(cfg, lanes)
    vmem = pl.BlockSpec(memory_space=pltpu.VMEM)
    return pl.pallas_call(
        functools.partial(second_kernel, cfg),
        out_shape=jax.ShapeDtypeStruct((4, cfg[2], cfg[3]), F32),
        in_specs=[vmem] * 8,
        out_specs=vmem,
        scratch_shapes=[pltpu.VMEM(buffer, BF)] * 4
        + [pltpu.VMEM((4,) + buffer, BF)] * 2
        + [*scratch(cfg, lanes, 1), pltpu.VMEM((2, cfg[2] // 2 * 8, cfg[3]), F32)],
        compiler_params=pltpu.CompilerParams(vmem_limit_bytes=40 << 20),
        name="second",
    )(following, *held, *weights)


def per_device(sizes, events, soft_info, embed, soft_gain, conv_weights, conv_bias, readout_weight):
    n_space, n_tm, n_chan = sizes
    rounds, tile, cols = events.shape
    layers = conv_weights.shape[0]
    strip = tile // n_chan
    packed = pack(
        n_chan,
        events,
        soft_info,
        (conv_weights, embed, soft_gain[None], conv_bias, readout_weight[None]),
    )
    both, edge = packed[:2]
    if n_chan == 2 and strip >= HALO:
        chain = []
        for s in range(n_space):
            for c in range(2):
                to = s + 1 - 2 * c
                spot = (to, c) if 0 <= to < n_space else (s, 1 - c)
                chain.append((s * 2 + c, spot[0] * 2 + spot[1]))
        up = down = lax.ppermute(edge, ("space", "chan"), chain)
    else:
        ring = lambda step: [(s, (s + step) % n_space) for s in range(n_space)]
        up = lax.ppermute(both[:, :, tile - HALO :], "space", ring(1))
        down = lax.ppermute(both[:, :, :HALO], "space", ring(-1))
    weights = prepare(*packed[2:])
    own, send = cut_window(n_chan, both, up, down)
    following = lax.ppermute(send, "tm", [(t, (t - 1) % n_tm) for t in range(n_tm)])
    cfg = (layers, tile, strip, cols, n_space, n_tm, n_chan)
    held = first_half(cfg, own, weights)
    mine = second_half(cfg, following, held, weights)
    parts = [mine]
    for step in range(1, n_chan):
        parts.append(lax.ppermute(mine, "chan", [(c, (c - step) % n_chan) for c in range(n_chan)]))
    chan = lax.axis_index("chan")
    ordered = [lax.select_n((c - chan) % n_chan, *parts) for c in range(n_chan)]
    return jnp.concatenate(ordered, 1)


def solution(mesh):
    split = P(("parts", "tm"), "space", None)
    sizes = tuple(mesh.shape[axis] for axis in ("space", "tm", "chan"))
    return jax.shard_map(
        functools.partial(per_device, sizes),
        mesh=mesh,
        in_specs=(split, split, P(), P(), P(), P(), P()),
        out_specs=split,
        check_vma=False,
    )
```

```python
import functools

import jax
import jax.numpy as jnp
from jax import lax
from jax.experimental import pallas as pl
from jax.experimental.pallas import tpu as pltpu
from jax.sharding import PartitionSpec as P

HALO = 8
SUB = 16
EDGE = 4
CHUNK = 13
BF = jnp.bfloat16
F32 = jnp.float32


def quotient(value, by):
    return lax.shift_right_logical(value, by.bit_length() - 1) if by & (by - 1) == 0 else value // by


def remainder(value, by):
    return value & (by - 1) if by & (by - 1) == 0 else value % by


def pack_kernel(n_chan, *refs):
    ev_hbm, soft_hbm = refs[:2]
    small_in, small_out = refs[2:7], refs[9:14]
    both_ref, edge_ref = refs[7:9]
    ev_ref, soft_ref, sems = refs[14:]
    copies = [
        pltpu.make_async_copy(source, target, sems.at[k])
        for k, (source, target) in enumerate(
            zip((ev_hbm, soft_hbm) + small_in, (ev_ref, soft_ref) + small_out)
        )
    ]
    for copy in copies:
        copy.start()
    copies[0].wait()
    copies[1].wait()
    rounds, tile, _ = ev_ref.shape
    lower = lax.axis_index("chan") < n_chan - 1
    for r in range(rounds):
        for kind, value in enumerate((ev_ref[r].astype(F32), soft_ref[r].astype(F32))):
            both_ref[kind, r] = value.astype(BF)
            edge_ref[kind, r] = jnp.where(lower, value[tile - HALO :], value[:HALO]).astype(BF)
    for copy in copies[2:]:
        copy.wait()


def pack(n_chan, events, soft_info, small):
    rounds, tile, cols = events.shape
    vmem = pl.BlockSpec(memory_space=pltpu.VMEM)
    outs = [
        jax.ShapeDtypeStruct((2, rounds, tile, cols), BF),
        jax.ShapeDtypeStruct((2, rounds, HALO, cols), BF),
    ] + [jax.ShapeDtypeStruct(x.shape, x.dtype) for x in small]
    return pl.pallas_call(
        functools.partial(pack_kernel, n_chan),
        out_shape=outs,
        in_specs=[pl.BlockSpec(memory_space=pltpu.HBM)] * 7,
        out_specs=[vmem] * len(outs),
        scratch_shapes=[
            pltpu.VMEM(events.shape, jnp.int32),
            pltpu.VMEM(soft_info.shape, BF),
            pltpu.SemaphoreType.DMA((7,)),
        ],
        compiler_params=pltpu.CompilerParams(vmem_limit_bytes=8 << 20),
        name="pack",
    )(*[pltpu.with_memory_space_constraint(x, pltpu.HBM) for x in (events, soft_info, *small)])


def open_weights(ch, embed_ref, gain_ref, wc_ref, wt_ref):
    table = jnp.concatenate([embed_ref[...], gain_ref[...], jnp.zeros((3, ch), F32)], 0)
    high = table.astype(BF)
    table = jnp.concatenate([high.astype(F32), table - high.astype(F32)], 0).astype(BF)
    zero = jnp.zeros((8, 2 * ch), F32)
    pieces = {}
    for dy in range(3):
        for dx in range(3):
            made = []
            for dr in range(3):
                tap = wt_ref[pl.ds(dr * 9 + dy * 3 + dx, ch, stride=27), :].astype(BF)
                value = jnp.dot(table, tap, preferred_element_type=F32)
                made.append(value[:8] + value[8:])
            for r in range(2):
                pieces[dy, dx, r] = jnp.concatenate([made[r + 1], made[r]], 1)
    blocks = []
    for a in range(4):
        for j in range(4):
            rows = [
                jnp.concatenate([pieces.get((j - yp, a - xp, r), zero) for yp in range(2) for xp in range(2)], 1)
                for r in range(2)
            ]
            blocks.append(jnp.concatenate(rows, 0))
    shape = (wc_ref.shape[0], 256)
    row = lax.broadcasted_iota(jnp.int32, shape, 0)
    inner = remainder(row, 8)
    group = quotient(row, 8)
    a = (group >= 5).astype(jnp.int32) + (group >= 10).astype(jnp.int32) + (group >= 15).astype(jnp.int32)
    old = (a * 8 + inner) * 8 + group - 5 * a
    order = (old == lax.broadcasted_iota(jnp.int32, shape, 1)).astype(F32).astype(BF)
    wide = jnp.concatenate(blocks, 0).astype(BF)
    wc_ref[...] = jnp.dot(order, wide, preferred_element_type=F32).astype(BF)


def prep_kernel(layers, ch, w_ref, embed_ref, gain_ref, bias_ref, read_ref, wout_ref, wc_ref, bout_ref, rw_ref, wt_ref):
    lanes = 4 * ch
    taps = 27
    zero_half = jnp.zeros((ch, ch), F32)
    zero_block = jnp.zeros((2 * ch, 2 * ch), BF)
    for layer in range(layers):
        wt_ref[...] = w_ref[layer].astype(F32).T
        if layer == 0:
            open_weights(ch, embed_ref, gain_ref, wc_ref, wt_ref)
        for dx in range(3):
            sets = []
            for dr in range(3):
                g = [wt_ref[pl.ds(dr * 9 + dy * 3 + dx, ch, stride=taps), :] for dy in range(3)]
                outer = (g[0] + g[2]) * 0.5
                inner = g[1] * 0.5
                sets.append((g[0], outer + inner, outer - inner, g[2]))
            for i in range(4):
                own = jnp.concatenate(
                    [
                        jnp.concatenate([sets[1][i], sets[0][i]], 1),
                        jnp.concatenate([sets[2][i], sets[1][i]], 1),
                    ],
                    0,
                ).astype(BF)
                side = jnp.concatenate(
                    [
                        jnp.concatenate([zero_half, sets[2][i]], 1),
                        jnp.concatenate([sets[0][i], zero_half], 1),
                    ],
                    0,
                ).astype(BF)
                for b in range(2):
                    a = dx + b
                    if layer > 0:
                        wout_ref[layer, i, pl.ds(a * 2 * ch, 2 * ch), pl.ds(b * 2 * ch, 2 * ch)] = own
                    wout_ref[layer, i, pl.ds(lanes * 2 + a * 2 * ch, 2 * ch), pl.ds(b * 2 * ch, 2 * ch)] = side
        for i in range(4):
            for base in (0, lanes * 2)[layer == 0 :]:
                wout_ref[layer, i, pl.ds(base + 6 * ch, 2 * ch), pl.ds(0, 2 * ch)] = zero_block
                wout_ref[layer, i, pl.ds(base, 2 * ch), pl.ds(2 * ch, 2 * ch)] = zero_block
        bout_ref[pl.ds(layer, 1), :] = jnp.concatenate([bias_ref[pl.ds(layer, 1), :]] * 4, 1)
    read = jnp.concatenate([read_ref[...]] * 4, 1)
    high = read.astype(BF).astype(F32)
    row = lax.broadcasted_iota(jnp.int32, (8, lanes), 0)
    read = jnp.where(row < 4, jnp.broadcast_to(high, (8, lanes)), jnp.broadcast_to(read - high, (8, lanes)))
    rw_ref[...] = jnp.where(remainder(row, 4) == quotient(lax.broadcasted_iota(jnp.int32, (8, lanes), 1), ch), read, 0.0).astype(BF)


def prepare(conv_weights, embed, soft_gain, conv_bias, readout_weight):
    layers, ch, depth = conv_weights.shape
    vmem = pl.BlockSpec(memory_space=pltpu.VMEM)
    return pl.pallas_call(
        functools.partial(prep_kernel, layers, ch),
        out_shape=(
            jax.ShapeDtypeStruct((layers, 4, 16 * ch, 4 * ch), BF),
            jax.ShapeDtypeStruct((160, 8 * ch), BF),
            jax.ShapeDtypeStruct((8, 4 * ch), F32),
            jax.ShapeDtypeStruct((8, 4 * ch), BF),
        ),
        in_specs=[vmem] * 5,
        out_specs=(vmem,) * 4,
        scratch_shapes=[pltpu.VMEM((depth, ch), F32)],
        compiler_params=pltpu.CompilerParams(vmem_limit_bytes=20 << 20),
        cost_estimate=pl.CostEstimate(flops=0, bytes_accessed=20_000_000, transcendentals=0),
        name="prepare",
    )(conv_weights, embed, soft_gain, conv_bias, readout_weight)


def window_kernel(n_chan, both_ref, up_ref, down_ref, own_ref, send_ref, d_ref):
    _, rounds, tile, _ = both_ref.shape
    strip = tile // n_chan
    start = lax.axis_index("chan") * strip
    if strip % 8 == 0:
        start = pl.multiple_of(start, 8)
    for r in range(rounds):
        for kind in range(2):
            slot = r * 2 + kind
            d_ref[slot, pl.ds(0, HALO), :] = up_ref[kind, r].astype(F32)
            d_ref[slot, pl.ds(HALO, tile), :] = both_ref[kind, r].astype(F32)
            d_ref[slot, pl.ds(HALO + tile, HALO), :] = down_ref[kind, r].astype(F32)
            value = d_ref[slot, pl.ds(start, strip + 2 * HALO), :].astype(BF)
            own_ref[kind, r] = value
            if r < rounds // 2:
                send_ref[kind, r] = value


def cut_window(n_chan, both, up, down):
    kinds, rounds, tile, cols = both.shape
    rows = tile // n_chan + 2 * HALO
    vmem = pl.BlockSpec(memory_space=pltpu.VMEM)
    return pl.pallas_call(
        functools.partial(window_kernel, n_chan),
        out_shape=(
            jax.ShapeDtypeStruct((kinds, rounds, rows, cols), BF),
            jax.ShapeDtypeStruct((kinds, rounds // 2, rows, cols), BF),
        ),
        in_specs=[vmem] * 3,
        out_specs=(vmem,) * 2,
        scratch_shapes=[pltpu.VMEM((kinds * rounds, tile + 2 * HALO, cols), F32)],
        compiler_params=pltpu.CompilerParams(vmem_limit_bytes=8 << 20),
        name="window",
    )(both, up, down)


class Strip:
    def __init__(self, cfg, lanes):
        self.layers, tile, strip, self.cols, n_space, n_tm, n_chan = cfg
        self.strip, self.pairs = strip, strip // 2
        self.rows = strip + 2 * HALO
        self.slabs = self.cols // SUB
        self.half = self.slabs // 2
        self.block = self.half * SUB
        self.lanes, self.mid = lanes, lanes // 2
        self.first_row = (lax.axis_index("space") * n_chan + lax.axis_index("chan")) * strip
        self.all_rows = n_space * tile
        self.has_next = lax.axis_index("tm") < n_tm - 1
        self.sub_row = lax.broadcasted_iota(jnp.int32, (SUB, self.mid), 0)

    def column(self, lane):
        q = quotient(lane, SUB)
        return remainder(lane, SUB) * self.slabs + 2 * remainder(q, self.half) + quotient(q, self.half)

    def features(self, arrays, f_ref):
        cols, rows, block = self.cols, self.rows, self.block
        shape = (2 * cols, 4 * cols)
        source = lax.broadcasted_iota(jnp.int32, shape, 0)
        lane = lax.broadcasted_iota(jnp.int32, (1, 4 * cols), 1)
        inner = remainder(lane, block)
        wanted = remainder(inner, SUB) * self.slabs + 2 * quotient(inner, SUB) + quotient(lane, cols) - 1
        wanted = jnp.where((wanted >= 0) & (wanted < cols), wanted, -2 * cols)
        wanted = wanted + cols * remainder(quotient(lane, block), 2)
        select = (source == wanted).astype(F32).astype(BF)
        stacked = jnp.concatenate(arrays, 0)
        wide = stacked.astype(F32)
        later = pltpu.roll(wide, wide.shape[0] - 2, 0).astype(BF)
        gathered = jnp.dot(jnp.concatenate([stacked, later], 1), select, preferred_element_type=F32)
        lane = lax.broadcasted_iota(jnp.int32, (rows, cols), 1)
        row_id = lax.broadcasted_iota(jnp.int32, (rows, cols), 0) - HALO + self.first_row + 2 * quotient(lane, block)
        inside_rows = (row_id >= 0) & (row_id < self.all_rows)
        inner = remainder(lane, block)
        column = remainder(inner, SUB) * self.slabs + 2 * quotient(inner, SUB)
        for a in range(4):
            x = column + (a - 1)
            inside = inside_rows & (x >= 0) & (x < cols)
            base = jnp.where(inside, 2.0 * ((row_id + a + 1) & 1).astype(F32), -8.0)
            keep = jnp.where(inside, 1.0, 0.0)
            for slot in range(0, len(arrays), 2):
                code = base + gathered[slot * rows : (slot + 1) * rows, a * cols : (a + 1) * cols]
                signal = gathered[(slot + 1) * rows : (slot + 2) * rows, a * cols : (a + 1) * cols]
                feats = [jnp.where(code == float(k), 1.0, 0.0) for k in range(4)] + [signal * keep]
                for k, feat in enumerate(feats):
                    f_ref[slot // 4, a, k, pl.ds(slot // 2 % 2, rows, stride=2), :] = feat

    def opening(self, f_ref, wc_ref, open_ref, extent):
        low, n_all, shift = self.reach(extent)
        for q in range(0, n_all, 2):
            at = 2 * (low - EDGE + q) + shift - 1 + HALO
            feats = [f_ref[a, k, pl.ds(2 * at, 8), :] for a in range(4) for k in range(5)]
            value = lax.dot_general(
                jnp.concatenate(feats, 0).astype(BF),
                wc_ref[...],
                (((0,), (0,)), ((), ())),
                preferred_element_type=F32,
            )
            for k in range(2):
                open_ref[k, pl.ds(q * self.block, 2 * self.block), :] = value[:, k * self.lanes : (k + 1) * self.lanes]

    def keep(self, ref, pair, value, blend=None):
        half, block, mid = self.half, self.block, self.mid
        slot = pair + EDGE

        def put(slab, lane, part):
            part = part.astype(BF)
            if blend is not None:
                other, mine, theirs = blend
                part = part * mine[..., lane] + other[slot, slab, :, lane] * theirs[..., lane]
            ref[slot, slab, :, lane] = part

        put(slice(1, half + 1), slice(0, self.lanes), value.reshape(half, SUB, self.lanes))
        last = pltpu.roll(value[block - SUB :, mid:], 1, 0)
        put(slice(0, 1), slice(mid, 2 * mid), jnp.where(self.sub_row == 0, 0.0, last)[None])
        head = pltpu.roll(value[:SUB, :mid], SUB - 1, 0)
        put(slice(half + 1, half + 2), slice(0, mid), jnp.where(self.sub_row == SUB - 1, 0.0, head)[None])

    def reach(self, extent):
        return EDGE - (extent + 1) // 2, self.pairs + extent, extent % 2

    def transform(self, e_ref, o_ref, c_ref, extent):
        half, lanes, mid = self.half, self.lanes, self.mid
        low, n, shift = self.reach(extent)
        for slab, lane in (
            (slice(1, half + 1), slice(0, lanes)),
            (slice(0, 1), slice(mid, lanes)),
            (slice(half + 1, half + 2), slice(0, mid)),
        ):
            view = lambda ref, step: ref[pl.ds(low + step, n), slab, :, lane]
            if shift:
                d = (view(e_ref, 0), view(o_ref, 0), view(e_ref, 1), view(o_ref, 1))
            else:
                d = (view(o_ref, -1), view(e_ref, 0), view(o_ref, 0), view(e_ref, 1))
            for i, value in enumerate((d[0] - d[2], d[1] + d[2], d[2] - d[1], d[1] - d[3])):
                c_ref[i, pl.ds(low, n), slab, :, lane] = value

    def taps(self, c_ref, i, low, n):
        half, lanes, mid = self.half, self.lanes, self.mid
        view = lambda slab, lane: c_ref[i, pl.ds(low, n), slab, :, lane].reshape(n * self.block, -1)
        return [
            view(slice(0, half), slice(mid, lanes)),
            view(slice(1, half + 1), slice(0, lanes)),
            view(slice(2, half + 2), slice(0, mid)),
        ]

    def layer(self, index, sources, e_ref, o_ref, m_ref, w_ref, b_ref, extent, open_ref=None, blend=(None, None)):
        bias = b_ref[pl.ds(index, 1), :]
        low, n_all, shift = self.reach(extent)
        count = -(-n_all // CHUNK)
        edges = [n_all * k // count for k in range(count + 1)]
        for spare, (begin, end) in enumerate(zip(edges, edges[1:])):
            n = end - begin
            spare %= 2
            size = n * self.block
            upper = lower = bias
            if open_ref is not None:
                at = pl.ds(begin * self.block, size)
                upper, lower = open_ref[0, at, :] + bias, open_ref[1, at, :] + bias
            if sources:
                first = sources[0][1]
                depth = self.lanes * 2 * len(sources)
                for i in range(4):
                    lhs = sum([self.taps(c_ref, i, low + begin, n) for c_ref, _ in sources], [])
                    m_ref[spare, i, pl.ds(0, size)] = jnp.dot(
                        jnp.concatenate(lhs, 1),
                        w_ref[index, i, pl.ds(first, depth), :],
                        preferred_element_type=F32,
                    )
                m = [m_ref[spare, i, pl.ds(0, size)] for i in range(4)]
                upper = upper + m[1] + (m[0] + m[2])
                lower = lower + m[1] - (m[2] + m[3])
            upper, lower = jnp.maximum(upper, 0.0), jnp.maximum(lower, 0.0)
            for q in range(n):
                p = low - EDGE + begin + q
                for k, value in enumerate((upper, lower)):
                    y = 2 * p + shift + k
                    row = value[q * self.block : (q + 1) * self.block]
                    if y < 0 or y >= self.strip:
                        spot = self.first_row + y
                        row = row * jnp.where((spot >= 0) & (spot < self.all_rows), 1.0, 0.0).astype(F32)
                    self.keep(o_ref if y % 2 else e_ref, y // 2, row, blend[y % 2])

    def logits(self, e_ref, o_ref, rw_ref, t_ref, out_ref, at):
        pairs, block, cols = self.pairs, self.block, self.cols
        lane = lax.broadcasted_iota(jnp.int32, (block, 2 * cols), 1)
        spot = self.column(lax.broadcasted_iota(jnp.int32, (block, 2 * cols), 0) + quotient(lane, cols) * block)
        back = (spot == remainder(lane, cols)).astype(F32).astype(BF)
        for k, ref in enumerate((e_ref, o_ref)):
            final = ref[pl.ds(EDGE, pairs), pl.ds(1, self.half)].reshape(pairs * block, self.lanes)
            value = lax.dot_general(
                rw_ref[...], final, (((1,), (1,)), ((), ())), preferred_element_type=F32
            )
            value = value[:4] + value[4:]
            value = jnp.concatenate([value, jnp.zeros_like(value)], 0)
            value = jnp.concatenate([value[:, p * block : (p + 1) * block] for p in range(pairs)], 0)
            high = value.astype(BF)
            stacked = jnp.concatenate([high, (value - high.astype(F32)).astype(BF)], 0)
            value = jnp.dot(stacked, back, preferred_element_type=F32)
            n = pairs * 8
            value = value[:n] + value[n:]
            t_ref[0] = value[:, :cols]
            t_ref[1] = value[:, cols:]
            for r in range(2):
                line = t_ref[0, pl.ds(r, pairs, stride=8), :] + t_ref[1, pl.ds(2 + r, pairs, stride=8), :]
                out_ref[at + r, pl.ds(k, pairs, stride=2), :] = line


def run_first_window(s, f_ref, wc_ref, e_ref, o_ref, c_ref, m_ref, open_ref, w_ref, b_ref, blend=(None, None)):
    extent = 2 * s.layers - 1
    s.opening(f_ref, wc_ref, open_ref, extent)
    s.layer(0, (), e_ref, o_ref, m_ref, w_ref, b_ref, extent, open_ref)
    for layer in range(1, s.layers):
        extent -= 1
        s.transform(e_ref, o_ref, c_ref, extent)
        last = blend if layer == s.layers - 1 else (None, None)
        s.layer(layer, ((c_ref, 0),), e_ref, o_ref, m_ref, w_ref, b_ref, extent, None, last)


def first_kernel(cfg, own_ref, w_ref, wc_ref, b_ref, e0_ref, o0_ref, start_ref, c_ref, f_ref, m_ref, open_ref):
    s = Strip(cfg, b_ref.shape[1])
    s.features([own_ref[kind, r] for r in range(4) for kind in range(2)], f_ref)
    run_first_window(s, f_ref.at[0], wc_ref, e0_ref, o0_ref, c_ref, m_ref, open_ref, w_ref, b_ref)
    s.opening(f_ref.at[1], wc_ref, start_ref, s.layers - 1)


def second_kernel(
    cfg, next_ref, e0_ref, o0_ref, start_ref, w_ref, wc_ref, b_ref, rw_ref, out_ref,
    e_ref, o_ref, eb_ref, ob_ref, c_ref, side_ref, f_ref, m_ref, open_ref, t_ref,
):
    s = Strip(cfg, b_ref.shape[1])
    s.features([next_ref[kind, r] for r in range(2) for kind in range(2)], f_ref)
    lane_id = lax.broadcasted_iota(jnp.int32, (SUB, s.lanes), 1)
    is_next = remainder(lane_id, s.mid) < s.mid // 2
    theirs = jnp.where(is_next, 0.0, 1.0).astype(BF)[None]
    mine = jnp.where(is_next & s.has_next, 1.0, 0.0).astype(BF)[None]
    run_first_window(
        s, f_ref.at[0], wc_ref, e_ref, o_ref, c_ref, m_ref, open_ref, w_ref, b_ref,
        ((e0_ref, mine, theirs), (o0_ref, mine, theirs)),
    )
    s.logits(e0_ref, o0_ref, rw_ref, t_ref, out_ref, 0)
    final = (eb_ref, ob_ref)
    for layer in range(s.layers):
        extent = s.layers - 1 - layer
        shift = extent % 2
        if s.layers - 1 - extent < 2:
            s.transform(e_ref, o_ref, side_ref.at[shift], extent)
        sources = ((side_ref.at[shift], 2 * s.lanes),)
        if layer > 0:
            s.transform(*final, c_ref, extent)
            sources = ((c_ref, 0),) + sources
        s.layer(layer, sources, *final, m_ref, w_ref, b_ref, extent, None if layer else start_ref)
    s.logits(*final, rw_ref, t_ref, out_ref, 2)


def row_buffer(cfg, lanes):
    return (cfg[2] // 2 + 2 * EDGE, cfg[3] // SUB // 2 + 2, SUB, lanes)


def open_buffer(cfg, lanes, extent):
    pairs = cfg[2] // 2 + extent
    return (2, (pairs + pairs % 2) * cfg[3] // 2, lanes)


def scratch(cfg, lanes, windows):
    rows = cfg[2] + 2 * HALO
    block = cfg[3] // 2
    return (
        pltpu.VMEM((windows, 4, 5, 2 * rows, cfg[3]), F32),
        pltpu.VMEM((2, 4, CHUNK * block, lanes), F32),
        pltpu.VMEM(open_buffer(cfg, lanes, 2 * cfg[0] - 1), F32),
    )


def first_half(cfg, own, weights):
    lanes = weights[2].shape[1]
    buffer = row_buffer(cfg, lanes)
    vmem = pl.BlockSpec(memory_space=pltpu.VMEM)
    return pl.pallas_call(
        functools.partial(first_kernel, cfg),
        out_shape=(
            jax.ShapeDtypeStruct(buffer, BF),
            jax.ShapeDtypeStruct(buffer, BF),
            jax.ShapeDtypeStruct(open_buffer(cfg, lanes, cfg[0] - 1), F32),
        ),
        in_specs=[vmem] * 4,
        out_specs=(vmem,) * 3,
        scratch_shapes=[pltpu.VMEM((4,) + buffer, BF), *scratch(cfg, lanes, 2)],
        compiler_params=pltpu.CompilerParams(vmem_limit_bytes=30 << 20),
        cost_estimate=pl.CostEstimate(flops=2_500_000_000, bytes_accessed=20_000_000, transcendentals=0),
        name="first",
    )(own, *weights[:3])


def second_half(cfg, following, held, weights):
    lanes = weights[2].shape[1]
    buffer = row_buffer(cfg, lanes)
    vmem = pl.BlockSpec(memory_space=pltpu.VMEM)
    return pl.pallas_call(
        functools.partial(second_kernel, cfg),
        out_shape=jax.ShapeDtypeStruct((4, cfg[2], cfg[3]), F32),
        in_specs=[vmem] * 8,
        out_specs=vmem,
        scratch_shapes=[pltpu.VMEM(buffer, BF)] * 4
        + [pltpu.VMEM((4,) + buffer, BF), pltpu.VMEM((2, 4) + buffer, BF)]
        + [*scratch(cfg, lanes, 1), pltpu.VMEM((2, cfg[2] // 2 * 8, cfg[3]), F32)],
        compiler_params=pltpu.CompilerParams(vmem_limit_bytes=40 << 20),
        name="second",
    )(following, *held, *weights)


def per_device(sizes, events, soft_info, embed, soft_gain, conv_weights, conv_bias, readout_weight):
    n_space, n_tm, n_chan = sizes
    rounds, tile, cols = events.shape
    layers = conv_weights.shape[0]
    strip = tile // n_chan
    packed = pack(
        n_chan,
        events,
        soft_info,
        (conv_weights, embed, soft_gain[None], conv_bias, readout_weight[None]),
    )
    both, edge = packed[:2]
    if n_chan == 2 and strip >= HALO:
        chain = []
        for s in range(n_space):
            for c in range(2):
                to = s + 1 - 2 * c
                spot = (to, c) if 0 <= to < n_space else (s, 1 - c)
                chain.append((s * 2 + c, spot[0] * 2 + spot[1]))
        up = down = lax.ppermute(edge, ("space", "chan"), chain)
    else:
        ring = lambda step: [(s, (s + step) % n_space) for s in range(n_space)]
        up = lax.ppermute(both[:, :, tile - HALO :], "space", ring(1))
        down = lax.ppermute(both[:, :, :HALO], "space", ring(-1))
    weights = prepare(*packed[2:])
    own, send = cut_window(n_chan, both, up, down)
    following = lax.ppermute(send, "tm", [(t, (t - 1) % n_tm) for t in range(n_tm)])
    cfg = (layers, tile, strip, cols, n_space, n_tm, n_chan)
    held = first_half(cfg, own, weights)
    mine = second_half(cfg, following, held, weights)
    parts = [mine]
    for step in range(1, n_chan):
        parts.append(lax.ppermute(mine, "chan", [(c, (c - step) % n_chan) for c in range(n_chan)]))
    chan = lax.axis_index("chan")
    ordered = [lax.select_n((c - chan) % n_chan, *parts) for c in range(n_chan)]
    return jnp.concatenate(ordered, 1)


def solution(mesh):
    split = P(("parts", "tm"), "space", None)
    sizes = tuple(mesh.shape[axis] for axis in ("space", "tm", "chan"))
    return jax.shard_map(
        functools.partial(per_device, sizes),
        mesh=mesh,
        in_specs=(split, split, P(), P(), P(), P(), P()),
        out_specs=split,
        check_vma=False,
    )
```

```python
import functools

import jax
import jax.numpy as jnp
from jax import lax
from jax.experimental import pallas as pl
from jax.experimental.pallas import tpu as pltpu
from jax.sharding import PartitionSpec as P

HALO = 8
SUB = 16
EDGE = 4
CHUNK = 13
BF = jnp.bfloat16
F32 = jnp.float32


def quotient(value, by):
    return lax.shift_right_logical(value, by.bit_length() - 1) if by & (by - 1) == 0 else value // by


def remainder(value, by):
    return value & (by - 1) if by & (by - 1) == 0 else value % by


def pack_kernel(n_chan, *refs):
    ev_hbm, soft_hbm = refs[:2]
    small_in, small_out = refs[2:7], refs[9:14]
    both_ref, edge_ref = refs[7:9]
    ev_ref, soft_ref, sems = refs[14:]
    copies = [
        pltpu.make_async_copy(source, target, sems.at[k])
        for k, (source, target) in enumerate(
            zip((ev_hbm, soft_hbm) + small_in, (ev_ref, soft_ref) + small_out)
        )
    ]
    for copy in copies:
        copy.start()
    copies[0].wait()
    copies[1].wait()
    rounds, tile, _ = ev_ref.shape
    lower = lax.axis_index("chan") < n_chan - 1
    for r in range(rounds):
        for kind, value in enumerate((ev_ref[r].astype(F32), soft_ref[r].astype(F32))):
            both_ref[kind, r] = value.astype(BF)
            edge_ref[kind, r] = jnp.where(lower, value[tile - HALO :], value[:HALO]).astype(BF)
    for copy in copies[2:]:
        copy.wait()


def pack(n_chan, events, soft_info, small):
    rounds, tile, cols = events.shape
    vmem = pl.BlockSpec(memory_space=pltpu.VMEM)
    outs = [
        jax.ShapeDtypeStruct((2, rounds, tile, cols), BF),
        jax.ShapeDtypeStruct((2, rounds, HALO, cols), BF),
    ] + [jax.ShapeDtypeStruct(x.shape, x.dtype) for x in small]
    return pl.pallas_call(
        functools.partial(pack_kernel, n_chan),
        out_shape=outs,
        in_specs=[pl.BlockSpec(memory_space=pltpu.HBM)] * 7,
        out_specs=[vmem] * len(outs),
        scratch_shapes=[
            pltpu.VMEM(events.shape, jnp.int32),
            pltpu.VMEM(soft_info.shape, BF),
            pltpu.SemaphoreType.DMA((7,)),
        ],
        compiler_params=pltpu.CompilerParams(vmem_limit_bytes=8 << 20),
        name="pack",
    )(*[pltpu.with_memory_space_constraint(x, pltpu.HBM) for x in (events, soft_info, *small)])


def open_weights(ch, embed_ref, gain_ref, wc_ref, wt_ref):
    table = jnp.concatenate([embed_ref[...], gain_ref[...], jnp.zeros((3, ch), F32)], 0)
    high = table.astype(BF)
    table = jnp.concatenate([high.astype(F32), table - high.astype(F32)], 0).astype(BF)
    zero = jnp.zeros((8, 2 * ch), F32)
    pieces = {}
    for dy in range(3):
        for dx in range(3):
            made = []
            for dr in range(3):
                tap = wt_ref[pl.ds(dr * 9 + dy * 3 + dx, ch, stride=27), :].astype(BF)
                value = jnp.dot(table, tap, preferred_element_type=F32)
                made.append(value[:8] + value[8:])
            for r in range(2):
                pieces[dy, dx, r] = jnp.concatenate([made[r + 1], made[r]], 1)
    blocks = []
    for a in range(4):
        for j in range(4):
            rows = [
                jnp.concatenate([pieces.get((j - yp, a - xp, r), zero) for yp in range(2) for xp in range(2)], 1)
                for r in range(2)
            ]
            blocks.append(jnp.concatenate(rows, 0))
    shape = (wc_ref.shape[0], 256)
    row = lax.broadcasted_iota(jnp.int32, shape, 0)
    inner = remainder(row, 8)
    group = quotient(row, 8)
    a = (group >= 5).astype(jnp.int32) + (group >= 10).astype(jnp.int32) + (group >= 15).astype(jnp.int32)
    old = (a * 8 + inner) * 8 + group - 5 * a
    order = (old == lax.broadcasted_iota(jnp.int32, shape, 1)).astype(F32).astype(BF)
    wide = jnp.concatenate(blocks, 0).astype(BF)
    wc_ref[...] = jnp.dot(order, wide, preferred_element_type=F32).astype(BF)


def prep_kernel(layers, ch, w_ref, embed_ref, gain_ref, bias_ref, read_ref, wout_ref, wc_ref, bout_ref, rw_ref, wt_ref):
    lanes = 4 * ch
    taps = 27
    zero_half = jnp.zeros((ch, ch), F32)
    zero_block = jnp.zeros((2 * ch, 2 * ch), BF)
    for layer in range(layers):
        wt_ref[...] = w_ref[layer].astype(F32).T
        if layer == 0:
            open_weights(ch, embed_ref, gain_ref, wc_ref, wt_ref)
        for dx in range(3):
            sets = []
            for dr in range(3):
                g = [wt_ref[pl.ds(dr * 9 + dy * 3 + dx, ch, stride=taps), :] for dy in range(3)]
                outer = (g[0] + g[2]) * 0.5
                inner = g[1] * 0.5
                sets.append((g[0], outer + inner, outer - inner, g[2]))
            for i in range(4):
                own = jnp.concatenate(
                    [
                        jnp.concatenate([sets[1][i], sets[0][i]], 1),
                        jnp.concatenate([sets[2][i], sets[1][i]], 1),
                    ],
                    0,
                ).astype(BF)
                side = jnp.concatenate(
                    [
                        jnp.concatenate([zero_half, sets[2][i]], 1),
                        jnp.concatenate([sets[0][i], zero_half], 1),
                    ],
                    0,
                ).astype(BF)
                for b in range(2):
                    a = dx + b
                    if layer > 0:
                        wout_ref[layer, i, pl.ds(a * 2 * ch, 2 * ch), pl.ds(b * 2 * ch, 2 * ch)] = own
                    if layer > 1:
                        wout_ref[layer, i, pl.ds(lanes * 2 + a * 2 * ch, 2 * ch), pl.ds(b * 2 * ch, 2 * ch)] = side
                        continue
                    spot = (2, 0, 1, 3)[a] * ch
                    for k in range(2):
                        lane = b * 2 * ch + (layer ^ k) * ch
                        wout_ref[0, i, pl.ds(k * lanes + spot, ch), pl.ds(lane, ch)] = sets[2 * k][i].astype(BF)
        for i in range(4):
            for base in ((), (0,), (0, lanes * 2))[layer]:
                wout_ref[layer, i, pl.ds(base + 6 * ch, 2 * ch), pl.ds(0, 2 * ch)] = zero_block
                wout_ref[layer, i, pl.ds(base, 2 * ch), pl.ds(2 * ch, 2 * ch)] = zero_block
            if layer == 0:
                for base in (0, lanes):
                    wout_ref[0, i, pl.ds(base + 3 * ch, ch), pl.ds(0, 2 * ch)] = zero_block[:ch]
                    wout_ref[0, i, pl.ds(base + 2 * ch, ch), pl.ds(2 * ch, 2 * ch)] = zero_block[:ch]
        bout_ref[pl.ds(layer, 1), :] = jnp.concatenate([bias_ref[pl.ds(layer, 1), :]] * 4, 1)
    read = jnp.concatenate([read_ref[...]] * 4, 1)
    high = read.astype(BF).astype(F32)
    row = lax.broadcasted_iota(jnp.int32, (8, lanes), 0)
    read = jnp.where(row < 4, jnp.broadcast_to(high, (8, lanes)), jnp.broadcast_to(read - high, (8, lanes)))
    rw_ref[...] = jnp.where(remainder(row, 4) == quotient(lax.broadcasted_iota(jnp.int32, (8, lanes), 1), ch), read, 0.0).astype(BF)


def prepare(conv_weights, embed, soft_gain, conv_bias, readout_weight):
    layers, ch, depth = conv_weights.shape
    vmem = pl.BlockSpec(memory_space=pltpu.VMEM)
    return pl.pallas_call(
        functools.partial(prep_kernel, layers, ch),
        out_shape=(
            jax.ShapeDtypeStruct((layers, 4, 16 * ch, 4 * ch), BF),
            jax.ShapeDtypeStruct((160, 8 * ch), BF),
            jax.ShapeDtypeStruct((8, 4 * ch), F32),
            jax.ShapeDtypeStruct((8, 4 * ch), BF),
        ),
        in_specs=[vmem] * 5,
        out_specs=(vmem,) * 4,
        scratch_shapes=[pltpu.VMEM((depth, ch), F32)],
        compiler_params=pltpu.CompilerParams(vmem_limit_bytes=20 << 20),
        cost_estimate=pl.CostEstimate(flops=0, bytes_accessed=20_000_000, transcendentals=0),
        name="prepare",
    )(conv_weights, embed, soft_gain, conv_bias, readout_weight)


def window_kernel(n_chan, both_ref, up_ref, down_ref, own_ref, send_ref, d_ref):
    _, rounds, tile, _ = both_ref.shape
    strip = tile // n_chan
    start = lax.axis_index("chan") * strip
    if strip % 8 == 0:
        start = pl.multiple_of(start, 8)
    for r in range(rounds):
        for kind in range(2):
            slot = r * 2 + kind
            d_ref[slot, pl.ds(0, HALO), :] = up_ref[kind, r].astype(F32)
            d_ref[slot, pl.ds(HALO, tile), :] = both_ref[kind, r].astype(F32)
            d_ref[slot, pl.ds(HALO + tile, HALO), :] = down_ref[kind, r].astype(F32)
            value = d_ref[slot, pl.ds(start, strip + 2 * HALO), :].astype(BF)
            own_ref[kind, r] = value
            if r < rounds // 2:
                send_ref[kind, r] = value


def cut_window(n_chan, both, up, down):
    kinds, rounds, tile, cols = both.shape
    rows = tile // n_chan + 2 * HALO
    vmem = pl.BlockSpec(memory_space=pltpu.VMEM)
    return pl.pallas_call(
        functools.partial(window_kernel, n_chan),
        out_shape=(
            jax.ShapeDtypeStruct((kinds, rounds, rows, cols), BF),
            jax.ShapeDtypeStruct((kinds, rounds // 2, rows, cols), BF),
        ),
        in_specs=[vmem] * 3,
        out_specs=(vmem,) * 2,
        scratch_shapes=[pltpu.VMEM((kinds * rounds, tile + 2 * HALO, cols), F32)],
        compiler_params=pltpu.CompilerParams(vmem_limit_bytes=8 << 20),
        name="window",
    )(both, up, down)


class Strip:
    def __init__(self, cfg, lanes):
        self.layers, tile, strip, self.cols, n_space, n_tm, n_chan = cfg
        self.strip, self.pairs = strip, strip // 2
        self.rows = strip + 2 * HALO
        self.slabs = self.cols // SUB
        self.half = self.slabs // 2
        self.block = self.half * SUB
        self.lanes, self.mid = lanes, lanes // 2
        self.first_row = (lax.axis_index("space") * n_chan + lax.axis_index("chan")) * strip
        self.all_rows = n_space * tile
        self.has_next = lax.axis_index("tm") < n_tm - 1
        self.sub_row = lax.broadcasted_iota(jnp.int32, (SUB, self.mid), 0)

    def column(self, lane):
        q = quotient(lane, SUB)
        return remainder(lane, SUB) * self.slabs + 2 * remainder(q, self.half) + quotient(q, self.half)

    def features(self, arrays, f_ref):
        cols, rows, block = self.cols, self.rows, self.block
        shape = (2 * cols, 4 * cols)
        source = lax.broadcasted_iota(jnp.int32, shape, 0)
        lane = lax.broadcasted_iota(jnp.int32, (1, 4 * cols), 1)
        inner = remainder(lane, block)
        wanted = remainder(inner, SUB) * self.slabs + 2 * quotient(inner, SUB) + quotient(lane, cols) - 1
        wanted = jnp.where((wanted >= 0) & (wanted < cols), wanted, -2 * cols)
        wanted = wanted + cols * remainder(quotient(lane, block), 2)
        select = (source == wanted).astype(F32).astype(BF)
        stacked = jnp.concatenate(arrays, 0)
        wide = stacked.astype(F32)
        later = pltpu.roll(wide, wide.shape[0] - 2, 0).astype(BF)
        gathered = jnp.dot(jnp.concatenate([stacked, later], 1), select, preferred_element_type=F32)
        lane = lax.broadcasted_iota(jnp.int32, (rows, cols), 1)
        row_id = lax.broadcasted_iota(jnp.int32, (rows, cols), 0) - HALO + self.first_row + 2 * quotient(lane, block)
        inside_rows = (row_id >= 0) & (row_id < self.all_rows)
        inner = remainder(lane, block)
        column = remainder(inner, SUB) * self.slabs + 2 * quotient(inner, SUB)
        for a in range(4):
            x = column + (a - 1)
            inside = inside_rows & (x >= 0) & (x < cols)
            base = jnp.where(inside, 2.0 * ((row_id + a + 1) & 1).astype(F32), -8.0)
            keep = jnp.where(inside, 1.0, 0.0)
            for slot in range(0, len(arrays), 2):
                code = base + gathered[slot * rows : (slot + 1) * rows, a * cols : (a + 1) * cols]
                signal = gathered[(slot + 1) * rows : (slot + 2) * rows, a * cols : (a + 1) * cols]
                feats = [jnp.where(code == float(k), 1.0, 0.0) for k in range(4)] + [signal * keep]
                for k, feat in enumerate(feats):
                    f_ref[slot // 4, a, k, pl.ds(slot // 2 % 2, rows, stride=2), :] = feat

    def opening(self, f_ref, wc_ref, open_ref, extent):
        low, n_all, shift = self.reach(extent)
        for q in range(0, n_all, 2):
            at = 2 * (low - EDGE + q) + shift - 1 + HALO
            feats = [f_ref[a, k, pl.ds(2 * at, 8), :] for a in range(4) for k in range(5)]
            value = lax.dot_general(
                jnp.concatenate(feats, 0).astype(BF),
                wc_ref[...],
                (((0,), (0,)), ((), ())),
                preferred_element_type=F32,
            )
            for k in range(2):
                open_ref[k, pl.ds(q * self.block, 2 * self.block), :] = value[:, k * self.lanes : (k + 1) * self.lanes]

    def keep(self, ref, pair, value, blend=None):
        half, block, mid = self.half, self.block, self.mid
        slot = pair + EDGE

        def put(slab, lane, part):
            part = part.astype(BF)
            if blend is not None:
                other, mine, theirs = blend
                part = part * mine[..., lane] + other[slot, slab, :, lane] * theirs[..., lane]
            ref[slot, slab, :, lane] = part

        put(slice(1, half + 1), slice(0, self.lanes), value.reshape(half, SUB, self.lanes))
        last = pltpu.roll(value[block - SUB :, mid:], 1, 0)
        put(slice(0, 1), slice(mid, 2 * mid), jnp.where(self.sub_row == 0, 0.0, last)[None])
        head = pltpu.roll(value[:SUB, :mid], SUB - 1, 0)
        put(slice(half + 1, half + 2), slice(0, mid), jnp.where(self.sub_row == SUB - 1, 0.0, head)[None])

    def reach(self, extent):
        return EDGE - (extent + 1) // 2, self.pairs + extent, extent % 2

    def transform(self, e_ref, o_ref, c_ref, extent):
        half, lanes, mid = self.half, self.lanes, self.mid
        low, n, shift = self.reach(extent)
        for slab, lane in (
            (slice(1, half + 1), slice(0, lanes)),
            (slice(0, 1), slice(mid, lanes)),
            (slice(half + 1, half + 2), slice(0, mid)),
        ):
            view = lambda ref, step: ref[pl.ds(low + step, n), slab, :, lane]
            if shift:
                d = (view(e_ref, 0), view(o_ref, 0), view(e_ref, 1), view(o_ref, 1))
            else:
                d = (view(o_ref, -1), view(e_ref, 0), view(o_ref, 0), view(e_ref, 1))
            for i, value in enumerate((d[0] - d[2], d[1] + d[2], d[2] - d[1], d[1] - d[3])):
                c_ref[i, pl.ds(low, n), slab, :, lane] = value

    def taps(self, c_ref, i, low, n):
        half, lanes, mid = self.half, self.lanes, self.mid
        view = lambda slab, lane: c_ref[i, pl.ds(low, n), slab, :, lane].reshape(n * self.block, -1)
        return [
            view(slice(0, half), slice(mid, lanes)),
            view(slice(1, half + 1), slice(0, lanes)),
            view(slice(2, half + 2), slice(0, mid)),
        ]

    def layer(self, index, sources, e_ref, o_ref, m_ref, w_ref, b_ref, extent, adds=(), blend=(None, None)):
        bias = b_ref[pl.ds(index, 1), :]
        low, n_all, shift = self.reach(extent)
        count = -(-n_all // CHUNK)
        edges = [n_all * k // count for k in range(count + 1)]
        for spare, (begin, end) in enumerate(zip(edges, edges[1:])):
            n = end - begin
            spare %= 2
            size = n * self.block
            upper = lower = bias
            at = pl.ds(begin * self.block, size)
            for add in adds:
                upper, lower = upper + add[0, at, :], lower + add[1, at, :]
            if sources:
                first = sources[0][1]
                depth = self.lanes * 2 * len(sources)

                def product(i):
                    lhs = sum([self.taps(c_ref, i, low + begin, n) for c_ref, _ in sources], [])
                    return jnp.dot(
                        jnp.concatenate(lhs, 1),
                        w_ref[index, i, pl.ds(first, depth), :],
                        preferred_element_type=F32,
                    )

                for i in (1, 2):
                    m_ref[spare, i, pl.ds(0, size)] = product(i)
                one, two = (m_ref[spare, i, pl.ds(0, size)] for i in (1, 2))
                upper = upper + one + two + product(0)
                lower = lower + one - two - product(3)
            upper, lower = jnp.maximum(upper, 0.0), jnp.maximum(lower, 0.0)
            for q in range(n):
                p = low - EDGE + begin + q
                for k, value in enumerate((upper, lower)):
                    y = 2 * p + shift + k
                    row = value[q * self.block : (q + 1) * self.block]
                    if y < 0 or y >= self.strip:
                        spot = self.first_row + y
                        row = row * jnp.where((spot >= 0) & (spot < self.all_rows), 1.0, 0.0).astype(F32)
                    self.keep(o_ref if y % 2 else e_ref, y // 2, row, blend[y % 2])

    def shared_sides(self, side_ref, m_ref, w_ref, add_ref, extent):
        half, mid, ch = self.half, self.mid, self.mid // 2
        low, n, _ = self.reach(extent)
        rows = n * self.block
        sums = []
        for k in range(2):
            at = (1 - k) * ch

            def product(i):
                view = lambda slab, lane: side_ref[i, pl.ds(low, n), slab, :, lane].reshape(rows, mid)
                pieces = (
                    view(slice(1, half + 1), slice(0, mid)),
                    view(slice(1, half + 1), slice(mid, 2 * mid)),
                    view(slice(0, half), slice(mid, 2 * mid)),
                    view(slice(2, half + 2), slice(0, mid)),
                )
                return jnp.dot(
                    jnp.concatenate([piece[:, at : at + ch] for piece in pieces], 1),
                    w_ref[0, i, pl.ds(k * self.lanes, self.lanes), :],
                    preferred_element_type=F32,
                )

            for i in (1, 2):
                m_ref[k, i, pl.ds(0, rows)] = product(i)
            one, two = (m_ref[k, i, pl.ds(0, rows)] for i in (1, 2))
            sums.append((one + two + product(0), one - two - product(3)))
        first = remainder(lax.broadcasted_iota(jnp.int32, (1, self.lanes), 1), mid) < ch
        for row, (left, right) in enumerate(zip(*sums)):
            add_ref[0, row, pl.ds(0, rows)] = jnp.where(first, left, right)
            crossed = jnp.where(first, right, left)
            for lane in (0, mid):
                add_ref[1, row, pl.ds(0, rows), lane : lane + mid] = pltpu.roll(crossed[:, lane : lane + mid], ch, 1)

    def logits(self, e_ref, o_ref, rw_ref, t_ref, out_ref, at):
        pairs, block, cols = self.pairs, self.block, self.cols
        lane = lax.broadcasted_iota(jnp.int32, (block, 2 * cols), 1)
        spot = self.column(lax.broadcasted_iota(jnp.int32, (block, 2 * cols), 0) + quotient(lane, cols) * block)
        back = (spot == remainder(lane, cols)).astype(F32).astype(BF)
        for k, ref in enumerate((e_ref, o_ref)):
            final = ref[pl.ds(EDGE, pairs), pl.ds(1, self.half)].reshape(pairs * block, self.lanes)
            value = lax.dot_general(
                rw_ref[...], final, (((1,), (1,)), ((), ())), preferred_element_type=F32
            )
            value = value[:4] + value[4:]
            value = jnp.concatenate([value, jnp.zeros_like(value)], 0)
            value = jnp.concatenate([value[:, p * block : (p + 1) * block] for p in range(pairs)], 0)
            high = value.astype(BF)
            stacked = jnp.concatenate([high, (value - high.astype(F32)).astype(BF)], 0)
            value = jnp.dot(stacked, back, preferred_element_type=F32)
            n = pairs * 8
            value = value[:n] + value[n:]
            t_ref[0] = value[:, :cols]
            t_ref[1] = value[:, cols:]
            for r in range(2):
                line = t_ref[0, pl.ds(r, pairs, stride=8), :] + t_ref[1, pl.ds(2 + r, pairs, stride=8), :]
                out_ref[at + r, pl.ds(k, pairs, stride=2), :] = line


def run_first_window(s, f_ref, wc_ref, e_ref, o_ref, c_ref, m_ref, open_ref, w_ref, b_ref, blend=(None, None)):
    extent = 2 * s.layers - 1
    s.opening(f_ref, wc_ref, open_ref, extent)
    s.layer(0, (), e_ref, o_ref, m_ref, w_ref, b_ref, extent, (open_ref,))
    for layer in range(1, s.layers):
        extent -= 1
        s.transform(e_ref, o_ref, c_ref, extent)
        last = blend if layer == s.layers - 1 else (None, None)
        s.layer(layer, ((c_ref, 0),), e_ref, o_ref, m_ref, w_ref, b_ref, extent, (), last)


def first_kernel(cfg, own_ref, w_ref, wc_ref, b_ref, e0_ref, o0_ref, start_ref, c_ref, f_ref, m_ref, open_ref):
    s = Strip(cfg, b_ref.shape[1])
    s.features([own_ref[kind, r] for r in range(4) for kind in range(2)], f_ref)
    run_first_window(s, f_ref.at[0], wc_ref, e0_ref, o0_ref, c_ref, m_ref, open_ref, w_ref, b_ref)
    s.opening(f_ref.at[1], wc_ref, start_ref, s.layers - 1)


def second_kernel(
    cfg, next_ref, e0_ref, o0_ref, start_ref, w_ref, wc_ref, b_ref, rw_ref, out_ref,
    e_ref, o_ref, eb_ref, ob_ref, c_ref, side_ref, f_ref, m_ref, open_ref, t_ref, add_ref,
):
    s = Strip(cfg, b_ref.shape[1])
    s.features([next_ref[kind, r] for r in range(2) for kind in range(2)], f_ref)
    lane_id = lax.broadcasted_iota(jnp.int32, (SUB, s.lanes), 1)
    is_next = remainder(lane_id, s.mid) < s.mid // 2
    theirs = jnp.where(is_next, 0.0, 1.0).astype(BF)[None]
    mine = jnp.where(is_next & s.has_next, 1.0, 0.0).astype(BF)[None]
    run_first_window(
        s, f_ref.at[0], wc_ref, e_ref, o_ref, c_ref, m_ref, open_ref, w_ref, b_ref,
        ((e0_ref, mine, theirs), (o0_ref, mine, theirs)),
    )
    s.logits(e0_ref, o0_ref, rw_ref, t_ref, out_ref, 0)
    final = (eb_ref, ob_ref)
    wide = s.layers // 2 * 2
    blank = jnp.zeros(eb_ref.shape[1:], BF)
    ob_ref[EDGE - wide // 2 - 1] = blank
    eb_ref[EDGE + s.pairs + wide // 2] = blank
    s.transform(e_ref, o_ref, side_ref, wide)
    s.shared_sides(side_ref, m_ref, w_ref, add_ref, wide)
    s.layer(0, (), *final, m_ref, w_ref, b_ref, wide, (start_ref, add_ref.at[0]))
    s.transform(*final, c_ref, wide)
    s.layer(1, ((c_ref, 0),), *final, m_ref, w_ref, b_ref, wide, (add_ref.at[1],))
    s.transform(*final, c_ref, 0)
    s.layer(2, ((c_ref, 0), (side_ref, 2 * s.lanes)), *final, m_ref, w_ref, b_ref, 0)
    s.logits(*final, rw_ref, t_ref, out_ref, 2)


def row_buffer(cfg, lanes):
    return (cfg[2] // 2 + 2 * EDGE, cfg[3] // SUB // 2 + 2, SUB, lanes)


def open_buffer(cfg, lanes, extent):
    pairs = cfg[2] // 2 + extent
    return (2, (pairs + pairs % 2) * cfg[3] // 2, lanes)


def scratch(cfg, lanes, windows):
    rows = cfg[2] + 2 * HALO
    block = cfg[3] // 2
    return (
        pltpu.VMEM((windows, 4, 5, 2 * rows, cfg[3]), F32),
        pltpu.VMEM((2, 4, max(CHUNK, cfg[2] // 2 + cfg[0]) * block, lanes), F32),
        pltpu.VMEM(open_buffer(cfg, lanes, 2 * cfg[0] - 1), F32),
    )


def first_half(cfg, own, weights):
    lanes = weights[2].shape[1]
    buffer = row_buffer(cfg, lanes)
    vmem = pl.BlockSpec(memory_space=pltpu.VMEM)
    return pl.pallas_call(
        functools.partial(first_kernel, cfg),
        out_shape=(
            jax.ShapeDtypeStruct(buffer, BF),
            jax.ShapeDtypeStruct(buffer, BF),
            jax.ShapeDtypeStruct(open_buffer(cfg, lanes, cfg[0] - 1), F32),
        ),
        in_specs=[vmem] * 4,
        out_specs=(vmem,) * 3,
        scratch_shapes=[pltpu.VMEM((4,) + buffer, BF), *scratch(cfg, lanes, 2)],
        compiler_params=pltpu.CompilerParams(vmem_limit_bytes=30 << 20),
        cost_estimate=pl.CostEstimate(flops=2_500_000_000, bytes_accessed=20_000_000, transcendentals=0),
        name="first",
    )(own, *weights[:3])


def second_half(cfg, following, held, weights):
    lanes = weights[2].shape[1]
    buffer = row_buffer(cfg, lanes)
    vmem = pl.BlockSpec(memory_space=pltpu.VMEM)
    return pl.pallas_call(
        functools.partial(second_kernel, cfg),
        out_shape=jax.ShapeDtypeStruct((4, cfg[2], cfg[3]), F32),
        in_specs=[vmem] * 8,
        out_specs=vmem,
        scratch_shapes=[pltpu.VMEM(buffer, BF)] * 4
        + [pltpu.VMEM((4,) + buffer, BF)] * 2
        + [*scratch(cfg, lanes, 1), pltpu.VMEM((2, cfg[2] // 2 * 8, cfg[3]), F32)]
        + [pltpu.VMEM((2,) + open_buffer(cfg, lanes, cfg[0] // 2 * 2), F32)],
        compiler_params=pltpu.CompilerParams(vmem_limit_bytes=40 << 20),
        name="second",
    )(following, *held, *weights)


def per_device(sizes, events, soft_info, embed, soft_gain, conv_weights, conv_bias, readout_weight):
    n_space, n_tm, n_chan = sizes
    rounds, tile, cols = events.shape
    layers = conv_weights.shape[0]
    strip = tile // n_chan
    packed = pack(
        n_chan,
        events,
        soft_info,
        (conv_weights, embed, soft_gain[None], conv_bias, readout_weight[None]),
    )
    both, edge = packed[:2]
    if n_chan == 2 and strip >= HALO:
        chain = []
        for s in range(n_space):
            for c in range(2):
                to = s + 1 - 2 * c
                spot = (to, c) if 0 <= to < n_space else (s, 1 - c)
                chain.append((s * 2 + c, spot[0] * 2 + spot[1]))
        up = down = lax.ppermute(edge, ("space", "chan"), chain)
    else:
        ring = lambda step: [(s, (s + step) % n_space) for s in range(n_space)]
        up = lax.ppermute(both[:, :, tile - HALO :], "space", ring(1))
        down = lax.ppermute(both[:, :, :HALO], "space", ring(-1))
    weights = prepare(*packed[2:])
    own, send = cut_window(n_chan, both, up, down)
    following = lax.ppermute(send, "tm", [(t, (t - 1) % n_tm) for t in range(n_tm)])
    cfg = (layers, tile, strip, cols, n_space, n_tm, n_chan)
    held = first_half(cfg, own, weights)
    mine = second_half(cfg, following, held, weights)
    parts = [mine]
    for step in range(1, n_chan):
        parts.append(lax.ppermute(mine, "chan", [(c, (c - step) % n_chan) for c in range(n_chan)]))
    chan = lax.axis_index("chan")
    ordered = [lax.select_n((c - chan) % n_chan, *parts) for c in range(n_chan)]
    return jnp.concatenate(ordered, 1)


def solution(mesh):
    split = P(("parts", "tm"), "space", None)
    sizes = tuple(mesh.shape[axis] for axis in ("space", "tm", "chan"))
    return jax.shard_map(
        functools.partial(per_device, sizes),
        mesh=mesh,
        in_specs=(split, split, P(), P(), P(), P(), P()),
        out_specs=split,
        check_vma=False,
    )
```

```python
import functools

import jax
import jax.numpy as jnp
from jax import lax
from jax.experimental import pallas as pl
from jax.experimental.pallas import tpu as pltpu
from jax.sharding import PartitionSpec as P

HALO = 8
SUB = 16
EDGE = 4
CHUNK = 13
BF = jnp.bfloat16
F32 = jnp.float32


def quotient(value, by):
    return lax.shift_right_logical(value, by.bit_length() - 1) if by & (by - 1) == 0 else value // by


def remainder(value, by):
    return value & (by - 1) if by & (by - 1) == 0 else value % by


def pack_kernel(n_chan, *refs):
    ev_hbm, soft_hbm = refs[:2]
    small_in, small_out = refs[2:7], refs[9:14]
    both_ref, edge_ref = refs[7:9]
    ev_ref, soft_ref, sems = refs[14:]
    copies = [
        pltpu.make_async_copy(source, target, sems.at[k])
        for k, (source, target) in enumerate(
            zip((ev_hbm, soft_hbm) + small_in, (ev_ref, soft_ref) + small_out)
        )
    ]
    for copy in copies:
        copy.start()
    copies[0].wait()
    copies[1].wait()
    rounds, tile, _ = ev_ref.shape
    lower = lax.axis_index("chan") < n_chan - 1
    for r in range(rounds):
        for kind, value in enumerate((ev_ref[r].astype(F32), soft_ref[r].astype(F32))):
            both_ref[kind, r] = value.astype(BF)
            edge_ref[kind, r] = jnp.where(lower, value[tile - HALO :], value[:HALO]).astype(BF)
    for copy in copies[2:]:
        copy.wait()


def pack(n_chan, events, soft_info, small):
    rounds, tile, cols = events.shape
    vmem = pl.BlockSpec(memory_space=pltpu.VMEM)
    outs = [
        jax.ShapeDtypeStruct((2, rounds, tile, cols), BF),
        jax.ShapeDtypeStruct((2, rounds, HALO, cols), BF),
    ] + [jax.ShapeDtypeStruct(x.shape, x.dtype) for x in small]
    return pl.pallas_call(
        functools.partial(pack_kernel, n_chan),
        out_shape=outs,
        in_specs=[pl.BlockSpec(memory_space=pltpu.HBM)] * 7,
        out_specs=[vmem] * len(outs),
        scratch_shapes=[
            pltpu.VMEM(events.shape, jnp.int32),
            pltpu.VMEM(soft_info.shape, BF),
            pltpu.SemaphoreType.DMA((7,)),
        ],
        compiler_params=pltpu.CompilerParams(vmem_limit_bytes=8 << 20),
        name="pack",
    )(*[pltpu.with_memory_space_constraint(x, pltpu.HBM) for x in (events, soft_info, *small)])


def open_weights(ch, embed_ref, gain_ref, wc_ref, wt_ref):
    table = jnp.concatenate([embed_ref[...], gain_ref[...], jnp.zeros((3, ch), F32)], 0)
    high = table.astype(BF)
    table = jnp.concatenate([high.astype(F32), table - high.astype(F32)], 0).astype(BF)
    zero = jnp.zeros((8, 2 * ch), F32)
    pieces = {}
    for dy in range(3):
        for dx in range(3):
            made = []
            for dr in range(3):
                tap = wt_ref[pl.ds(dr * 9 + dy * 3 + dx, ch, stride=27), :].astype(BF)
                value = jnp.dot(table, tap, preferred_element_type=F32)
                made.append(value[:8] + value[8:])
            for r in range(2):
                pieces[dy, dx, r] = jnp.concatenate([made[r + 1], made[r]], 1)
    blocks = []
    for a in range(4):
        for j in range(4):
            rows = [
                jnp.concatenate([pieces.get((j - yp, a - xp, r), zero) for yp in range(2) for xp in range(2)], 1)
                for r in range(2)
            ]
            blocks.append(jnp.concatenate(rows, 0))
    shape = (wc_ref.shape[0], 256)
    row = lax.broadcasted_iota(jnp.int32, shape, 0)
    inner = remainder(row, 8)
    group = quotient(row, 8)
    a = (group >= 5).astype(jnp.int32) + (group >= 10).astype(jnp.int32) + (group >= 15).astype(jnp.int32)
    old = (a * 8 + inner) * 8 + group - 5 * a
    order = (old == lax.broadcasted_iota(jnp.int32, shape, 1)).astype(F32).astype(BF)
    wide = jnp.concatenate(blocks, 0).astype(BF)
    wc_ref[...] = jnp.dot(order, wide, preferred_element_type=F32).astype(BF)


def prep_kernel(layers, ch, w_ref, embed_ref, gain_ref, bias_ref, read_ref, wout_ref, wc_ref, bout_ref, rw_ref, wt_ref):
    lanes = 4 * ch
    taps = 27
    zero_half = jnp.zeros((ch, ch), F32)
    zero_block = jnp.zeros((2 * ch, 2 * ch), BF)
    for layer in range(layers):
        wt_ref[...] = w_ref[layer].astype(F32).T
        if layer == 0:
            open_weights(ch, embed_ref, gain_ref, wc_ref, wt_ref)
        for dx in range(3):
            sets = []
            for dr in range(3):
                g = [wt_ref[pl.ds(dr * 9 + dy * 3 + dx, ch, stride=taps), :] for dy in range(3)]
                outer = (g[0] + g[2]) * 0.5
                inner = g[1] * 0.5
                sets.append((g[0], outer + inner, outer - inner, g[2]))
            for i in range(4):
                own = jnp.concatenate(
                    [
                        jnp.concatenate([sets[1][i], sets[0][i]], 1),
                        jnp.concatenate([sets[2][i], sets[1][i]], 1),
                    ],
                    0,
                ).astype(BF)
                side = jnp.concatenate(
                    [
                        jnp.concatenate([zero_half, sets[2][i]], 1),
                        jnp.concatenate([sets[0][i], zero_half], 1),
                    ],
                    0,
                ).astype(BF)
                for b in range(2):
                    a = dx + b
                    if layer > 0:
                        wout_ref[layer, i, pl.ds(a * 2 * ch, 2 * ch), pl.ds(b * 2 * ch, 2 * ch)] = own
                    if layer > 1:
                        wout_ref[layer, i, pl.ds(lanes * 2 + a * 2 * ch, 2 * ch), pl.ds(b * 2 * ch, 2 * ch)] = side
                        continue
                    spot = (2, 0, 1, 3)[a] * ch
                    for k in range(2):
                        lane = b * 2 * ch + (layer ^ k) * ch
                        wout_ref[0, i, pl.ds(k * lanes + spot, ch), pl.ds(lane, ch)] = sets[2 * k][i].astype(BF)
        for i in range(4):
            for base in ((), (0,), (0, lanes * 2))[layer]:
                wout_ref[layer, i, pl.ds(base + 6 * ch, 2 * ch), pl.ds(0, 2 * ch)] = zero_block
                wout_ref[layer, i, pl.ds(base, 2 * ch), pl.ds(2 * ch, 2 * ch)] = zero_block
            if layer == 0:
                for base in (0, lanes):
                    wout_ref[0, i, pl.ds(base + 3 * ch, ch), pl.ds(0, 2 * ch)] = zero_block[:ch]
                    wout_ref[0, i, pl.ds(base + 2 * ch, ch), pl.ds(2 * ch, 2 * ch)] = zero_block[:ch]
        bout_ref[pl.ds(layer, 1), :] = jnp.concatenate([bias_ref[pl.ds(layer, 1), :]] * 4, 1)
    read = jnp.concatenate([read_ref[...]] * 4, 1)
    high = read.astype(BF).astype(F32)
    row = lax.broadcasted_iota(jnp.int32, (8, lanes), 0)
    read = jnp.where(row < 4, jnp.broadcast_to(high, (8, lanes)), jnp.broadcast_to(read - high, (8, lanes)))
    rw_ref[...] = jnp.where(remainder(row, 4) == quotient(lax.broadcasted_iota(jnp.int32, (8, lanes), 1), ch), read, 0.0).astype(BF)


def prepare(conv_weights, embed, soft_gain, conv_bias, readout_weight):
    layers, ch, depth = conv_weights.shape
    vmem = pl.BlockSpec(memory_space=pltpu.VMEM)
    return pl.pallas_call(
        functools.partial(prep_kernel, layers, ch),
        out_shape=(
            jax.ShapeDtypeStruct((layers, 4, 16 * ch, 4 * ch), BF),
            jax.ShapeDtypeStruct((160, 8 * ch), BF),
            jax.ShapeDtypeStruct((8, 4 * ch), F32),
            jax.ShapeDtypeStruct((8, 4 * ch), BF),
        ),
        in_specs=[vmem] * 5,
        out_specs=(vmem,) * 4,
        scratch_shapes=[pltpu.VMEM((depth, ch), F32)],
        compiler_params=pltpu.CompilerParams(vmem_limit_bytes=20 << 20),
        cost_estimate=pl.CostEstimate(flops=0, bytes_accessed=20_000_000, transcendentals=0),
        name="prepare",
    )(conv_weights, embed, soft_gain, conv_bias, readout_weight)


def window_kernel(n_chan, both_ref, up_ref, down_ref, own_ref, send_ref, d_ref):
    _, rounds, tile, _ = both_ref.shape
    strip = tile // n_chan
    start = lax.axis_index("chan") * strip
    if strip % 8 == 0:
        start = pl.multiple_of(start, 8)
    for r in range(rounds):
        for kind in range(2):
            slot = r * 2 + kind
            d_ref[slot, pl.ds(0, HALO), :] = up_ref[kind, r].astype(F32)
            d_ref[slot, pl.ds(HALO, tile), :] = both_ref[kind, r].astype(F32)
            d_ref[slot, pl.ds(HALO + tile, HALO), :] = down_ref[kind, r].astype(F32)
            value = d_ref[slot, pl.ds(start, strip + 2 * HALO), :].astype(BF)
            own_ref[kind, r] = value
            if r < rounds // 2:
                send_ref[kind, r] = value


def cut_window(n_chan, both, up, down):
    kinds, rounds, tile, cols = both.shape
    rows = tile // n_chan + 2 * HALO
    vmem = pl.BlockSpec(memory_space=pltpu.VMEM)
    return pl.pallas_call(
        functools.partial(window_kernel, n_chan),
        out_shape=(
            jax.ShapeDtypeStruct((kinds, rounds, rows, cols), BF),
            jax.ShapeDtypeStruct((kinds, rounds // 2, rows, cols), BF),
        ),
        in_specs=[vmem] * 3,
        out_specs=(vmem,) * 2,
        scratch_shapes=[pltpu.VMEM((kinds * rounds, tile + 2 * HALO, cols), F32)],
        compiler_params=pltpu.CompilerParams(vmem_limit_bytes=8 << 20),
        name="window",
    )(both, up, down)


class Strip:
    def __init__(self, cfg, lanes):
        self.layers, tile, strip, self.cols, n_space, n_tm, n_chan = cfg
        self.strip, self.pairs = strip, strip // 2
        self.rows = strip + 2 * HALO
        self.slabs = self.cols // SUB
        self.half = self.slabs // 2
        self.block = self.half * SUB
        self.lanes, self.mid = lanes, lanes // 2
        self.first_row = (lax.axis_index("space") * n_chan + lax.axis_index("chan")) * strip
        self.all_rows = n_space * tile
        self.has_next = lax.axis_index("tm") < n_tm - 1
        self.sub_row = lax.broadcasted_iota(jnp.int32, (SUB, self.mid), 0)

    def column(self, lane):
        q = quotient(lane, SUB)
        return remainder(lane, SUB) * self.slabs + 2 * remainder(q, self.half) + quotient(q, self.half)

    def features(self, arrays, f_ref):
        cols, rows, block = self.cols, self.rows, self.block
        shape = (2 * cols, 4 * cols)
        source = lax.broadcasted_iota(jnp.int32, shape, 0)
        lane = lax.broadcasted_iota(jnp.int32, (1, 4 * cols), 1)
        inner = remainder(lane, block)
        wanted = remainder(inner, SUB) * self.slabs + 2 * quotient(inner, SUB) + quotient(lane, cols) - 1
        wanted = jnp.where((wanted >= 0) & (wanted < cols), wanted, -2 * cols)
        wanted = wanted + cols * remainder(quotient(lane, block), 2)
        select = (source == wanted).astype(F32).astype(BF)
        stacked = jnp.concatenate(arrays, 0)
        wide = stacked.astype(F32)
        later = pltpu.roll(wide, wide.shape[0] - 2, 0).astype(BF)
        gathered = jnp.dot(jnp.concatenate([stacked, later], 1), select, preferred_element_type=F32)
        lane = lax.broadcasted_iota(jnp.int32, (rows, cols), 1)
        row_id = lax.broadcasted_iota(jnp.int32, (rows, cols), 0) - HALO + self.first_row + 2 * quotient(lane, block)
        inside_rows = (row_id >= 0) & (row_id < self.all_rows)
        inner = remainder(lane, block)
        column = remainder(inner, SUB) * self.slabs + 2 * quotient(inner, SUB)
        for a in range(4):
            x = column + (a - 1)
            inside = inside_rows & (x >= 0) & (x < cols)
            base = jnp.where(inside, 2.0 * ((row_id + a + 1) & 1).astype(F32), -8.0)
            keep = jnp.where(inside, 1.0, 0.0)
            for slot in range(0, len(arrays), 2):
                code = base + gathered[slot * rows : (slot + 1) * rows, a * cols : (a + 1) * cols]
                signal = gathered[(slot + 1) * rows : (slot + 2) * rows, a * cols : (a + 1) * cols]
                feats = [jnp.where(code == float(k), 1.0, 0.0) for k in range(4)] + [signal * keep]
                for k, feat in enumerate(feats):
                    f_ref[slot // 4, a, k, pl.ds(slot // 2 % 2, rows, stride=2), :] = feat

    def opening(self, f_ref, wc_ref, open_ref, extent):
        low, n_all, shift = self.reach(extent)
        for q in range(0, n_all, 2):
            at = 2 * (low - EDGE + q) + shift - 1 + HALO
            feats = [f_ref[a, k, pl.ds(2 * at, 8), :] for a in range(4) for k in range(5)]
            value = lax.dot_general(
                jnp.concatenate(feats, 0).astype(BF),
                wc_ref[...],
                (((0,), (0,)), ((), ())),
                preferred_element_type=F32,
            )
            for k in range(2):
                open_ref[k, pl.ds(q * self.block, 2 * self.block), :] = value[:, k * self.lanes : (k + 1) * self.lanes]

    def keep(self, ref, pair, value, blend=None):
        half, block, mid = self.half, self.block, self.mid
        slot = pair + EDGE

        def put(slab, lane, part):
            part = part.astype(BF)
            if blend is not None:
                other, mine, theirs = blend
                part = part * mine[..., lane] + other[slot, slab, :, lane] * theirs[..., lane]
            ref[slot, slab, :, lane] = part

        put(slice(1, half + 1), slice(0, self.lanes), value.reshape(half, SUB, self.lanes))
        last = pltpu.roll(value[block - SUB :, mid:], 1, 0)
        put(slice(0, 1), slice(mid, 2 * mid), jnp.where(self.sub_row == 0, 0.0, last)[None])
        head = pltpu.roll(value[:SUB, :mid], SUB - 1, 0)
        put(slice(half + 1, half + 2), slice(0, mid), jnp.where(self.sub_row == SUB - 1, 0.0, head)[None])

    def reach(self, extent):
        return EDGE - (extent + 1) // 2, self.pairs + extent, extent % 2

    def transform(self, e_ref, o_ref, c_ref, extent):
        half, lanes, mid = self.half, self.lanes, self.mid
        low, n, shift = self.reach(extent)
        for slab, lane in (
            (slice(1, half + 1), slice(0, lanes)),
            (slice(0, 1), slice(mid, lanes)),
            (slice(half + 1, half + 2), slice(0, mid)),
        ):
            view = lambda ref, step: ref[pl.ds(low + step, n), slab, :, lane]
            if shift:
                d = (view(e_ref, 0), view(o_ref, 0), view(e_ref, 1), view(o_ref, 1))
            else:
                d = (view(o_ref, -1), view(e_ref, 0), view(o_ref, 0), view(e_ref, 1))
            for i, value in enumerate((d[0] - d[2], d[1] + d[2], d[2] - d[1], d[1] - d[3])):
                c_ref[i, pl.ds(low, n), slab, :, lane] = value

    def taps(self, c_ref, i, low, n):
        half, lanes, mid = self.half, self.lanes, self.mid
        view = lambda slab, lane: c_ref[i, pl.ds(low, n), slab, :, lane].reshape(n * self.block, -1)
        return [
            view(slice(0, half), slice(mid, lanes)),
            view(slice(1, half + 1), slice(0, lanes)),
            view(slice(2, half + 2), slice(0, mid)),
        ]

    def layer(self, index, sources, e_ref, o_ref, m_ref, w_ref, b_ref, extent, adds=(), blend=(None, None)):
        bias = b_ref[pl.ds(index, 1), :]
        low, n_all, shift = self.reach(extent)
        count = -(-n_all // CHUNK)
        edges = [n_all * k // count for k in range(count + 1)]
        for spare, (begin, end) in enumerate(zip(edges, edges[1:])):
            n = end - begin
            spare %= 2
            size = n * self.block
            upper = lower = bias
            at = pl.ds(begin * self.block, size)
            for add in adds:
                upper, lower = upper + add[0, at, :], lower + add[1, at, :]
            if sources:
                first = sources[0][1]
                depth = self.lanes * 2 * len(sources)

                def product(i):
                    lhs = sum([self.taps(c_ref, i, low + begin, n) for c_ref, _ in sources], [])
                    return jnp.dot(
                        jnp.concatenate(lhs, 1),
                        w_ref[index, i, pl.ds(first, depth), :],
                        preferred_element_type=F32,
                    )

                for i in (1, 2):
                    m_ref[spare, i, pl.ds(0, size)] = product(i)
                one, two = (m_ref[spare, i, pl.ds(0, size)] for i in (1, 2))
                upper = upper + one + two + product(0)
                lower = lower + one - two - product(3)
            upper, lower = jnp.maximum(upper, 0.0), jnp.maximum(lower, 0.0)
            for q in range(n):
                p = low - EDGE + begin + q
                for k, value in enumerate((upper, lower)):
                    y = 2 * p + shift + k
                    row = value[q * self.block : (q + 1) * self.block]
                    if y < 0 or y >= self.strip:
                        spot = self.first_row + y
                        row = row * jnp.where((spot >= 0) & (spot < self.all_rows), 1.0, 0.0).astype(F32)
                    self.keep(o_ref if y % 2 else e_ref, y // 2, row, blend[y % 2])

    def shared_sides(self, side_ref, m_ref, w_ref, add_ref, extent):
        half, mid, ch = self.half, self.mid, self.mid // 2
        low, n, _ = self.reach(extent)
        rows = n * self.block
        sums = []
        for k in range(2):
            at = (1 - k) * ch

            def product(i):
                view = lambda slab, lane: side_ref[i, pl.ds(low, n), slab, :, lane].reshape(rows, mid)
                pieces = (
                    view(slice(1, half + 1), slice(0, mid)),
                    view(slice(1, half + 1), slice(mid, 2 * mid)),
                    view(slice(0, half), slice(mid, 2 * mid)),
                    view(slice(2, half + 2), slice(0, mid)),
                )
                return jnp.dot(
                    jnp.concatenate([piece[:, at : at + ch] for piece in pieces], 1),
                    w_ref[0, i, pl.ds(k * self.lanes, self.lanes), :],
                    preferred_element_type=F32,
                )

            for i in (1, 2):
                m_ref[k, i, pl.ds(0, rows)] = product(i)
            one, two = (m_ref[k, i, pl.ds(0, rows)] for i in (1, 2))
            sums.append((one + two + product(0), one - two - product(3)))
        first = remainder(lax.broadcasted_iota(jnp.int32, (1, self.lanes), 1), mid) < ch
        for row, (left, right) in enumerate(zip(*sums)):
            add_ref[0, row, pl.ds(0, rows)] = jnp.where(first, left, right)
            crossed = jnp.where(first, right, left)
            for lane in (0, mid):
                add_ref[1, row, pl.ds(0, rows), lane : lane + mid] = pltpu.roll(crossed[:, lane : lane + mid], ch, 1)

    def logits(self, e_ref, o_ref, rw_ref, t_ref, out_ref, at):
        pairs, block, cols = self.pairs, self.block, self.cols
        lane = lax.broadcasted_iota(jnp.int32, (block, 2 * cols), 1)
        spot = self.column(lax.broadcasted_iota(jnp.int32, (block, 2 * cols), 0) + quotient(lane, cols) * block)
        back = (spot == remainder(lane, cols)).astype(F32).astype(BF)
        for k, ref in enumerate((e_ref, o_ref)):
            final = ref[pl.ds(EDGE, pairs), pl.ds(1, self.half)].reshape(pairs * block, self.lanes)
            value = lax.dot_general(
                rw_ref[...], final, (((1,), (1,)), ((), ())), preferred_element_type=F32
            )
            value = value[:4] + value[4:]
            value = jnp.concatenate([value, jnp.zeros_like(value)], 0)
            value = jnp.concatenate([value[:, p * block : (p + 1) * block] for p in range(pairs)], 0)
            high = value.astype(BF)
            stacked = jnp.concatenate([high, (value - high.astype(F32)).astype(BF)], 0)
            value = jnp.dot(stacked, back, preferred_element_type=F32)
            n = pairs * 8
            value = value[:n] + value[n:]
            t_ref[0] = value[:, :cols]
            t_ref[1] = value[:, cols:]
            for r in range(2):
                line = t_ref[0, pl.ds(r, pairs, stride=8), :] + t_ref[1, pl.ds(2 + r, pairs, stride=8), :]
                out_ref[at + r, pl.ds(k, pairs, stride=2), :] = line


def run_first_window(s, f_ref, wc_ref, e_ref, o_ref, c_ref, m_ref, open_ref, w_ref, b_ref, blend=(None, None)):
    extent = 2 * s.layers - 1
    s.opening(f_ref, wc_ref, open_ref, extent)
    s.layer(0, (), e_ref, o_ref, m_ref, w_ref, b_ref, extent, (open_ref,))
    for layer in range(1, s.layers):
        extent -= 1
        s.transform(e_ref, o_ref, c_ref, extent)
        last = blend if layer == s.layers - 1 else (None, None)
        s.layer(layer, ((c_ref, 0),), e_ref, o_ref, m_ref, w_ref, b_ref, extent, (), last)


def first_kernel(cfg, own_ref, w_ref, wc_ref, b_ref, e0_ref, o0_ref, start_ref, c_ref, f_ref, m_ref, open_ref):
    s = Strip(cfg, b_ref.shape[1])
    s.features([own_ref[kind, r] for r in range(4) for kind in range(2)], f_ref)
    run_first_window(s, f_ref.at[0], wc_ref, e0_ref, o0_ref, c_ref, m_ref, open_ref, w_ref, b_ref)
    s.opening(f_ref.at[1], wc_ref, start_ref, s.layers - 1)


def second_kernel(
    cfg, next_ref, e0_ref, o0_ref, start_ref, w_ref, wc_ref, b_ref, rw_ref, out_ref,
    e_ref, o_ref, eb_ref, ob_ref, c_ref, side_ref, f_ref, m_ref, open_ref, t_ref, add_ref,
):
    s = Strip(cfg, b_ref.shape[1])
    s.features([next_ref[kind, r] for r in range(2) for kind in range(2)], f_ref)
    lane_id = lax.broadcasted_iota(jnp.int32, (SUB, s.lanes), 1)
    is_next = remainder(lane_id, s.mid) < s.mid // 2
    theirs = jnp.where(is_next, 0.0, 1.0).astype(BF)[None]
    mine = jnp.where(is_next & s.has_next, 1.0, 0.0).astype(BF)[None]
    run_first_window(
        s, f_ref.at[0], wc_ref, e_ref, o_ref, c_ref, m_ref, open_ref, w_ref, b_ref,
        ((e0_ref, mine, theirs), (o0_ref, mine, theirs)),
    )
    s.logits(e0_ref, o0_ref, rw_ref, t_ref, out_ref, 0)
    final = (eb_ref, ob_ref)
    wide = s.layers // 2 * 2
    blank = jnp.zeros(eb_ref.shape[1:], BF)
    ob_ref[EDGE - wide // 2 - 1] = blank
    eb_ref[EDGE + s.pairs + wide // 2] = blank
    s.transform(e_ref, o_ref, side_ref, wide)
    s.shared_sides(side_ref, m_ref, w_ref, add_ref, wide)
    s.layer(0, (), *final, m_ref, w_ref, b_ref, wide, (start_ref, add_ref.at[0]))
    s.transform(*final, c_ref, wide)
    s.layer(1, ((c_ref, 0),), *final, m_ref, w_ref, b_ref, wide, (add_ref.at[1],))
    s.transform(*final, c_ref, 0)
    s.layer(2, ((c_ref, 0), (side_ref, 2 * s.lanes)), *final, m_ref, w_ref, b_ref, 0)
    s.logits(*final, rw_ref, t_ref, out_ref, 2)


def row_buffer(cfg, lanes):
    return (cfg[2] // 2 + 2 * EDGE, cfg[3] // SUB // 2 + 2, SUB, lanes)


def open_buffer(cfg, lanes, extent):
    pairs = cfg[2] // 2 + extent
    return (2, (pairs + pairs % 2) * cfg[3] // 2, lanes)


def scratch(cfg, lanes, windows):
    rows = cfg[2] + 2 * HALO
    block = cfg[3] // 2
    return (
        pltpu.VMEM((windows, 4, 5, 2 * rows, cfg[3]), F32),
        pltpu.VMEM((2, 4, max(CHUNK, cfg[2] // 2 + cfg[0]) * block, lanes), F32),
        pltpu.VMEM(open_buffer(cfg, lanes, 2 * cfg[0] - 1), F32),
    )


def first_half(cfg, own, weights):
    lanes = weights[2].shape[1]
    buffer = row_buffer(cfg, lanes)
    vmem = pl.BlockSpec(memory_space=pltpu.VMEM)
    return pl.pallas_call(
        functools.partial(first_kernel, cfg),
        out_shape=(
            jax.ShapeDtypeStruct(buffer, BF),
            jax.ShapeDtypeStruct(buffer, BF),
            jax.ShapeDtypeStruct(open_buffer(cfg, lanes, cfg[0] - 1), F32),
        ),
        in_specs=[vmem] * 4,
        out_specs=(vmem,) * 3,
        scratch_shapes=[pltpu.VMEM((4,) + buffer, BF), *scratch(cfg, lanes, 2)],
        compiler_params=pltpu.CompilerParams(vmem_limit_bytes=30 << 20),
        cost_estimate=pl.CostEstimate(flops=2_500_000_000, bytes_accessed=20_000_000, transcendentals=0),
        name="first",
    )(own, *weights[:3])


def second_half(cfg, following, held, weights):
    lanes = weights[2].shape[1]
    buffer = row_buffer(cfg, lanes)
    vmem = pl.BlockSpec(memory_space=pltpu.VMEM)
    return pl.pallas_call(
        functools.partial(second_kernel, cfg),
        out_shape=jax.ShapeDtypeStruct((4, cfg[2], cfg[3]), F32),
        in_specs=[vmem] * 8,
        out_specs=vmem,
        scratch_shapes=[pltpu.VMEM(buffer, BF)] * 4
        + [pltpu.VMEM((4,) + buffer, BF)] * 2
        + [*scratch(cfg, lanes, 1), pltpu.VMEM((2, cfg[2] // 2 * 8, cfg[3]), F32)]
        + [pltpu.VMEM((2,) + open_buffer(cfg, lanes, cfg[0] // 2 * 2), F32)],
        compiler_params=pltpu.CompilerParams(vmem_limit_bytes=40 << 20),
        name="second",
    )(following, *held, *weights)


def join_kernel(n_chan, *refs):
    parts, out_ref, sems = refs[:n_chan], refs[n_chan], refs[n_chan + 1]
    strip = parts[0].shape[1]
    chan = lax.axis_index("chan")
    copies = []
    for k, part in enumerate(parts):
        start = lax.rem(chan + k, n_chan) * strip
        if strip % 8 == 0:
            start = pl.multiple_of(start, 8)
        copies.append(pltpu.make_async_copy(part, out_ref.at[:, pl.ds(start, strip), :], sems.at[k]))
    for copy in copies:
        copy.start()
    for copy in copies:
        copy.wait()


def join(n_chan, parts):
    rounds, strip, cols = parts[0].shape
    return pl.pallas_call(
        functools.partial(join_kernel, n_chan),
        out_shape=jax.ShapeDtypeStruct((rounds, n_chan * strip, cols), F32),
        in_specs=[pl.BlockSpec(memory_space=pltpu.VMEM)] * n_chan,
        out_specs=pl.BlockSpec(memory_space=pltpu.HBM),
        scratch_shapes=[pltpu.SemaphoreType.DMA((n_chan,))],
        compiler_params=pltpu.CompilerParams(vmem_limit_bytes=8 << 20),
        name="join",
    )(*parts)


def per_device(sizes, events, soft_info, embed, soft_gain, conv_weights, conv_bias, readout_weight):
    n_space, n_tm, n_chan = sizes
    rounds, tile, cols = events.shape
    layers = conv_weights.shape[0]
    strip = tile // n_chan
    packed = pack(
        n_chan,
        events,
        soft_info,
        (conv_weights, embed, soft_gain[None], conv_bias, readout_weight[None]),
    )
    both, edge = packed[:2]
    if n_chan == 2 and strip >= HALO:
        chain = []
        for s in range(n_space):
            for c in range(2):
                to = s + 1 - 2 * c
                spot = (to, c) if 0 <= to < n_space else (s, 1 - c)
                chain.append((s * 2 + c, spot[0] * 2 + spot[1]))
        up = down = lax.ppermute(edge, ("space", "chan"), chain)
    else:
        ring = lambda step: [(s, (s + step) % n_space) for s in range(n_space)]
        up = lax.ppermute(both[:, :, tile - HALO :], "space", ring(1))
        down = lax.ppermute(both[:, :, :HALO], "space", ring(-1))
    weights = prepare(*packed[2:])
    own, send = cut_window(n_chan, both, up, down)
    following = lax.ppermute(send, "tm", [(t, (t - 1) % n_tm) for t in range(n_tm)])
    cfg = (layers, tile, strip, cols, n_space, n_tm, n_chan)
    held = first_half(cfg, own, weights)
    mine = second_half(cfg, following, held, weights)
    parts = [mine]
    for step in range(1, n_chan):
        parts.append(lax.ppermute(mine, "chan", [(c, (c - step) % n_chan) for c in range(n_chan)]))
    return join(n_chan, parts)


def solution(mesh):
    split = P(("parts", "tm"), "space", None)
    sizes = tuple(mesh.shape[axis] for axis in ("space", "tm", "chan"))
    return jax.shard_map(
        functools.partial(per_device, sizes),
        mesh=mesh,
        in_specs=(split, split, P(), P(), P(), P(), P()),
        out_specs=split,
        check_vma=False,
    )
```
